512 devices in a mesh: slab: 32 (over y, x), band: 16 (over z, core).
Axes of the slice: x: 4, y: 8, z: 8, core: 2. Of those that a mesh axis runs over, the one named last changes fastest.
Arguments:
- basis: float32 [3, 512, 49152], P(None, 'slab', 'band')
- offsets: float32 [3, 512, 256], P(None, 'slab', 'band'), may hold values from -0.45 to 0.45
- bond_modulus: float32 [512, 256], P('slab', 'band'), may hold values from 0.5 to 2
- bulk_modulus: float32 [512, 256], P('slab', 'band'), may hold values from 0.5 to 2
- springs: float32 [512, 256], P('slab', 'band'), may hold values from 0.5 to 2
- intact: int32 [32, 32, 9], P('slab', 'band'), may hold values from 0 to 1, as said below
Outputs:
- new_modes: float32 [3, 512, 16384], P(None, 'slab', 'band')
- new_images: float32 [3, 512, 16384], P(None, 'slab', 'band')
- reduced: float32 [64, 64], replicated
The draws below stay inside these ranges and needn't reach their ends.
Inputs may be any that keep to these rules, and one draw needn't show every extreme that they name: intact[i, j, 3 (dx + 1) + (dy + 1)] is 1 where the bonds between block (i, j) and block (i + dx, j + dy) are intact, and 0 where they are broken or that block lies outside the plate; the entry for (0, 0) is always 1, and the entry for (dx, dy) of one block equals the entry for (-dx, -dy) of the other.
All inputs are finite; a program needn't handle non-finite values.
Results may differ from the reference program's by a relative error of at most 0.0003.
Values sent between devices are 32-bit elements; how exact they have to be, the bound alone decides.
No kernel may reach another device: no remote copies, remote signals or barrier semaphores. Data moves between devices by JAX's collectives and lax.ppermute only.
A program may use at most 128 MiB of HBM per device.

```python
import math
import jax
import jax.numpy as jnp
from jax import lax

BLOCK_X = 16
BLOCK_Y = 8
REACH = 3
MODES = 64
NCOL = 192
NX = 512
NY = 256
GX = 32
GY = 32


def draw_basis(key, part):
    noise_key, scale_key, column_key = jax.random.split(key, 3)
    full_shape = (3, NX, NY, NCOL)
    values = jax.random.normal(noise_key, full_shape, jnp.float32)
    point_scale = jnp.exp(jax.random.uniform(scale_key, (3, NX, NY, 1), jnp.float32, 0.0, math.log(10.0)))
    rising = jnp.exp(math.log(3.0) * jnp.arange(NX, dtype=jnp.float32) / NX).reshape(1, NX, 1, 1)
    column_scale = jnp.exp(jax.random.uniform(column_key, (NCOL,), jnp.float32, 0.0, math.log(10.0)))
    return (values * point_scale * rising * column_scale).reshape(3, NX, NY * NCOL)


def draw_intact(key, part):
    forward = (jax.random.randint(key, (4, GX, GY), 0, 4) > 0).astype(jnp.int32)
    along_x = jnp.arange(GX, dtype=jnp.int32)[:, None]
    along_y = jnp.arange(GY, dtype=jnp.int32)[None, :]
    directions = ((1, -1), (1, 0), (1, 1), (0, 1))
    entries = [jnp.ones((GX, GY), jnp.int32) for number in range(9)]
    for number in range(4):
        step_x, step_y = directions[number]
        inside = ((along_x + step_x >= 0) & (along_x + step_x < GX) & (along_y + step_y >= 0) & (along_y + step_y < GY)).astype(jnp.int32)
        bonded = forward[number] * inside
        padded = jnp.pad(bonded, 1)
        shifted = padded[1 - step_x:1 - step_x + GX, 1 - step_y:1 - step_y + GY]
        entries[3 * (step_x + 1) + step_y + 1] = bonded
        entries[3 * (1 - step_x) + 1 - step_y] = shifted
    return jnp.stack(entries, axis=-1)


def shard_levels(rng, dims, cuts, least, high):
    def one(axis_at, parts):
        heights = jax.random.uniform(jax.random.fold_in(jax.random.fold_in(rng, 6), axis_at), (parts,), jnp.float32, least / len(cuts), high / len(cuts))
        return jnp.repeat(jnp.exp(heights), dims[axis_at] // parts).reshape((-1,) + (1,) * (len(dims) - axis_at - 1))

    factor_of = one(*cuts[0])
    for cut in cuts[1:]:
        factor_of = factor_of * one(*cut)
    return factor_of


def setup_inputs(seed: int = 0) -> dict:
    streams_of = jax.random.split(jax.random.key(seed), 7)
    return {
        "basis": draw_basis(jax.random.fold_in(streams_of[6], 71), 0),
        "offsets": jnp.clip(jax.random.uniform(streams_of[1], (3, NX, NY), jnp.float32, -0.45, 0.45) * shard_levels(streams_of[1], (3, NX, NY), ((1, 32), (2, 16)), -0.4, 0.0), -0.45, 0.45),
        "bond_modulus": jnp.clip(jnp.exp(math.log(2.0) - 1.3862944 * jax.random.uniform(streams_of[2], (NX, NY), jnp.float32) ** shard_levels(streams_of[2], (NX, NY), ((0, 32), (1, 16)), -0.2, 0.2)), 0.5, 2.0),
        "bulk_modulus": jnp.clip(jnp.exp(math.log(2.0) - 1.3862944 * jax.random.uniform(streams_of[3], (NX, NY), jnp.float32) ** shard_levels(streams_of[3], (NX, NY), ((0, 32), (1, 16)), -0.2, 0.2)), 0.5, 2.0),
        "springs": jnp.clip(jnp.exp(math.log(2.0) - 1.3862944 * jax.random.uniform(streams_of[4], (NX, NY), jnp.float32) ** shard_levels(streams_of[4], (NX, NY), ((0, 32), (1, 16)), -0.2, 0.2)), 0.5, 2.0),
        "intact": draw_intact(jax.random.fold_in(streams_of[6], 71), 0),
    }


horizon_square = 9.0
bond_scale = 1.0 / 18.0
dilation_scale = 1.0 / 27.0
highest = lax.Precision.HIGHEST

def pair_geometry(home_offsets, home_x, home_y, far_offsets, far_x, far_y, intact_mask):
    bond_vector = jnp.stack([far_x[None, :] - home_x[:, None] + far_offsets[0][None, :] - home_offsets[0][:, None], far_y[None, :] - home_y[:, None] + far_offsets[1][None, :] - home_offsets[1][:, None], far_offsets[2][None, :] - home_offsets[2][:, None]], axis=1)
    distance = jnp.sum(bond_vector * bond_vector, axis=1)
    weight = jnp.maximum(1.0 - distance / horizon_square, 0.0) * intact_mask
    return (bond_vector, weight)

def stiffness_terms(bond_vector, weight, home_modulus, far_modulus, home_field, far_field):
    home_count = bond_vector.shape[0]
    far_count = bond_vector.shape[2]
    column_count = home_field.shape[2]
    weighted = weight[:, None, :] * bond_vector
    far_flat = far_field.reshape(3 * far_count, column_count)
    volume_change = jnp.dot(weighted.reshape(home_count, 3 * far_count), far_flat, precision=highest)
    volume_change = volume_change - jnp.einsum('nc,cnk->nk', jnp.sum(weighted, axis=2), home_field, precision=highest)
    coupling = weight * (home_modulus[:, None] + far_modulus[None, :]) * bond_scale
    leading = jnp.transpose(bond_vector, (1, 0, 2))
    tensor = coupling[None, :, None, :] * leading[:, :, None, :] * bond_vector[None, :, :, :]
    bond_force = jnp.einsum('cnd,dnk->cnk', jnp.sum(tensor, axis=3), home_field, precision=highest)
    bond_force = bond_force - jnp.dot(tensor.reshape(3 * home_count, 3 * far_count), far_flat, precision=highest).reshape(3, home_count, column_count)
    return (volume_change, bond_force)

def dilatation_terms(bond_vector, weight, home_value, far_value):
    home_count = bond_vector.shape[0]
    weighted = jnp.transpose(weight[:, None, :] * bond_vector, (1, 0, 2))
    remote = jnp.dot(weighted.reshape(3 * home_count, -1), far_value, precision=highest).reshape(3, home_count, far_value.shape[1])
    return -(remote + jnp.sum(weighted, axis=2)[:, :, None] * home_value[None, :, :])

def rotation(mass_gram, stiff_gram, mode_count):
    mass_factor = jnp.linalg.cholesky(mass_gram)
    left_solved = lax.linalg.triangular_solve(mass_factor, stiff_gram, left_side=True, lower=True)
    projected = lax.linalg.triangular_solve(mass_factor, left_solved.T, left_side=True, lower=True)
    projected = 0.5 * (projected + projected.T)
    stiff_factor = jnp.linalg.cholesky(projected)
    target = jnp.eye(stiff_gram.shape[0], mode_count, dtype=stiff_gram.dtype)
    forward = lax.linalg.triangular_solve(stiff_factor, target, left_side=True, lower=True)
    inverse = lax.linalg.triangular_solve(stiff_factor, forward, left_side=True, lower=True, transpose_a=True)
    normal = jnp.linalg.cholesky(jnp.dot(inverse.T, inverse, precision=highest))
    lifted = lax.linalg.triangular_solve(mass_factor, inverse, left_side=True, lower=True, transpose_a=True)
    return lax.linalg.triangular_solve(normal, lifted, left_side=False, lower=True, transpose_a=True)

def reference(basis, offsets, bond_modulus, bulk_modulus, springs, intact):
    basis = basis.reshape(3, NX, NY, NCOL)
    float_type = basis.dtype
    column_count = basis.shape[3]
    home_count = BLOCK_X * BLOCK_Y
    wide_x = BLOCK_X + 2 * REACH
    wide_y = BLOCK_Y + 2 * REACH
    zero_index = jnp.zeros((), jnp.int32)
    field_pad = jnp.pad(basis, ((0, 0), (REACH, REACH), (REACH, REACH), (0, 0)))
    offset_pad = jnp.pad(offsets, ((0, 0), (REACH, REACH), (REACH, REACH)))
    modulus_pad = jnp.pad(bond_modulus, ((REACH, REACH), (REACH, REACH)))
    home_ix = jnp.repeat(jnp.arange(BLOCK_X, dtype=jnp.int32), BLOCK_Y)
    home_iy = jnp.tile(jnp.arange(BLOCK_Y, dtype=jnp.int32), BLOCK_X)
    far_ix = jnp.repeat(jnp.arange(wide_x, dtype=jnp.int32) - REACH, wide_y)
    far_iy = jnp.tile(jnp.arange(wide_y, dtype=jnp.int32) - REACH, wide_x)
    far_code = 3 * (jnp.floor_divide(far_ix, BLOCK_X) + 1) + jnp.floor_divide(far_iy, BLOCK_Y) + 1
    home_x = home_ix.astype(float_type)
    home_y = home_iy.astype(float_type)
    far_x = far_ix.astype(float_type)
    far_y = far_iy.astype(float_type)
    block_ids = jnp.arange(GX * GY, dtype=jnp.int32)

    def geometry(block_id):
        block_row = (block_id // GY).astype(jnp.int32)
        block_col = (block_id % GY).astype(jnp.int32)
        start_x = block_row * BLOCK_X
        start_y = block_col * BLOCK_Y
        home_offsets = lax.dynamic_slice(offsets, (zero_index, start_x, start_y), (3, BLOCK_X, BLOCK_Y)).reshape(3, home_count)
        far_offsets = lax.dynamic_slice(offset_pad, (zero_index, start_x, start_y), (3, wide_x, wide_y)).reshape(3, wide_x * wide_y)
        bond_row = lax.dynamic_slice(intact, (block_row, block_col, zero_index), (1, 1, 9)).reshape(9).astype(float_type)
        intact_mask = jnp.zeros(far_code.shape, float_type)
        for offset in range(9):
            intact_mask = intact_mask + jnp.where(far_code == offset, bond_row[offset], 0.0)
        bond_vector, weight = pair_geometry(home_offsets, home_x, home_y, far_offsets, far_x, far_y, intact_mask[None, :])
        return (bond_vector, weight, start_x, start_y)

    def first_pass(block_id):
        bond_vector, weight, start_x, start_y = geometry(block_id)
        home_field = lax.dynamic_slice(basis, (zero_index, start_x, start_y, zero_index), (3, BLOCK_X, BLOCK_Y, column_count)).reshape(3, home_count, column_count)
        far_field = lax.dynamic_slice(field_pad, (zero_index, start_x, start_y, zero_index), (3, wide_x, wide_y, column_count)).reshape(3, wide_x * wide_y, column_count)
        home_modulus = lax.dynamic_slice(bond_modulus, (start_x, start_y), (BLOCK_X, BLOCK_Y)).reshape(home_count)
        far_modulus = lax.dynamic_slice(modulus_pad, (start_x, start_y), (wide_x, wide_y)).reshape(wide_x * wide_y)
        return stiffness_terms(bond_vector, weight, home_modulus, far_modulus, home_field, far_field)
    volumes, bond_blocks = lax.map(first_pass, block_ids)
    volume_grid = volumes.reshape(GX, GY, BLOCK_X, BLOCK_Y, column_count).transpose(0, 2, 1, 3, 4).reshape(NX, NY, column_count)
    bond_grid = bond_blocks.reshape(GX, GY, 3, BLOCK_X, BLOCK_Y, column_count).transpose(2, 0, 3, 1, 4, 5).reshape(3, NX, NY, column_count)
    dilatation = dilation_scale * bulk_modulus[:, :, None] * volume_grid
    dilatation_pad = jnp.pad(dilatation, ((REACH, REACH), (REACH, REACH), (0, 0)))

    def second_pass(block_id):
        bond_vector, weight, start_x, start_y = geometry(block_id)
        home_value = lax.dynamic_slice(dilatation, (start_x, start_y, zero_index), (BLOCK_X, BLOCK_Y, column_count)).reshape(home_count, column_count)
        far_value = lax.dynamic_slice(dilatation_pad, (start_x, start_y, zero_index), (wide_x, wide_y, column_count)).reshape(wide_x * wide_y, column_count)
        return dilatation_terms(bond_vector, weight, home_value, far_value)
    dilatation_blocks = lax.map(second_pass, block_ids)
    dilatation_grid = dilatation_blocks.reshape(GX, GY, 3, BLOCK_X, BLOCK_Y, column_count).transpose(2, 0, 3, 1, 4, 5).reshape(3, NX, NY, column_count)
    images = bond_grid + dilatation_grid + springs[None, :, :, None] * basis
    total_rows = 3.0 * NX * NY
    flat_basis = basis.reshape(-1, column_count)
    flat_images = images.reshape(-1, column_count)
    mass_gram = jnp.einsum('rk,rl->kl', flat_basis, flat_basis, precision=highest) / total_rows
    stiff_gram = jnp.einsum('rk,rl->kl', flat_basis, flat_images, precision=highest) / total_rows
    stiff_gram = 0.5 * (stiff_gram + stiff_gram.T)
    rotate = rotation(mass_gram, stiff_gram, MODES)
    new_modes = jnp.einsum('cxyk,km->cxym', basis, rotate, precision=highest)
    new_images = jnp.einsum('cxyk,km->cxym', images, rotate, precision=highest)
    reduced = jnp.einsum('cxym,cxyn->mn', new_modes, new_images, precision=highest) / total_rows
    return (new_modes.reshape(3, NX, NY * MODES), new_images.reshape(3, NX, NY * MODES), reduced)
```

```python
import jax
import jax.numpy as jnp
from jax import lax
from jax.experimental import pallas as pl
from jax.experimental.pallas import tpu as pltpu
from jax.sharding import PartitionSpec as P


MODES = 64
NCOL = 192
SIDE = 16
HALO = 6
GROUP = 32
STRIPS = 12
FAR = 256
highest = lax.Precision.HIGHEST
f32 = jnp.float32
bf16 = jnp.bfloat16

VMEM = pl.BlockSpec(memory_space=pltpu.VMEM)
PARAMS = pltpu.CompilerParams(vmem_limit_bytes=56 * 1024 * 1024)


def call(kernel, outs, scratch, args, flops, name):
    size = sum(a.size for a in args) + sum(o[0] * o[1] * (o[2] if len(o) > 2 else 1) for o in outs)
    return pl.pallas_call(
        kernel,
        out_shape=[jax.ShapeDtypeStruct(o, f32) for o in outs],
        in_specs=[VMEM] * len(args),
        out_specs=[VMEM] * len(outs),
        scratch_shapes=scratch,
        compiler_params=PARAMS,
        cost_estimate=pl.CostEstimate(flops=flops, bytes_accessed=4 * size, transcendentals=0),
        name=name,
    )(*args)


def pack_x(basis, geo, up, down):
    for out, first, lane in ((up, SIDE - HALO, 256), (down, 0, 384)):
        for c in range(3):
            for j in range(4):
                row = j * 18 + c * 6
                out[row : row + 6, :] = basis[c, first : first + 6, j * 768 : (j + 1) * 768]
        out[72:80, :] = jnp.zeros((8, 768), f32)
        out[72:80, 0:128] = geo[:, lane : lane + 128]


def pack_y(basis, geo, left, right, up, down, own):
    own[...] = jnp.zeros((8, 512), f32)
    for y in range(SIDE):
        at = GROUP * y
        own[:, at : at + 16] = geo[:, 16 * y : 16 * y + 16]
        own[:, at + 16 : at + 22] = left[72:80, 8 * y : 8 * y + 6]
        own[:, at + 22 : at + 28] = right[72:80, 8 * y : 8 * y + 6]
    for out, first in ((up, SIDE - HALO), (down, 0)):
        pieces = ((2, 384, 768, 0), (3, 0, 768, 384)) if first else ((0, 0, 768, 0), (1, 0, 384, 768))
        for c in range(3):
            row = GROUP * c
            out[row : row + 16, :] = basis[c, :, first * NCOL : (first + HALO) * NCOL]
            for j, start, stop, lane in pieces:
                src = j * 18 + c * 6
                width = stop - start
                out[row + 16 : row + 22, lane : lane + width] = left[src : src + 6, start:stop]
                out[row + 22 : row + 28, lane : lane + width] = right[src : src + 6, start:stop]
            out[row + 28 : row + 32, :] = jnp.zeros((4, 1152), f32)
        lanes = slice(first * GROUP, (first + HALO) * GROUP)
        out[28:32, 0:192] = own[0:4, lanes]
        out[60:64, 0:192] = own[4:8, lanes]


def split(value):
    high = value.astype(bf16)
    return high, (value - high.astype(f32)).astype(bf16)


def product(left, right_high, right_low):
    high, low = split(left)
    return (
        jnp.dot(high, right_high, preferred_element_type=f32)
        + jnp.dot(high, right_low, preferred_element_type=f32)
        + jnp.dot(low, right_high, preferred_element_type=f32)
    )


def block_masks(s, table):
    y0 = 2 * s - 4
    lane = lax.broadcasted_iota(jnp.int32, (32, FAR), 1)
    row = lax.broadcasted_iota(jnp.int32, (32, FAR), 0)
    xi = lane & 31
    far_x = jnp.where(xi < 16, 0, jnp.where(xi < 22, -1, 1))
    far_y = ((y0 - 3 + (lane >> 5)) >> 3) - (y0 >> 3)
    home_x = jnp.where(row < 16, 0, jnp.where(row < 22, -1, 1))
    entry = row - jnp.where(row < 16, 0, jnp.where(row < 22, 16, 22))
    entry = jnp.where(entry < 6, entry, -100)
    code = 3 * (far_x - home_x + 1) + far_y + 1
    value = jnp.where(code == entry, table[:, 7:8], 0.0)
    value = value + jnp.where(code == entry + 6, table[:, 6:7], 0.0)
    middle = jnp.sum(value[0:8], axis=0, keepdims=True)
    rest = value[16:32]
    at = lax.broadcasted_iota(jnp.int32, (16, FAR), 0)
    before = jnp.sum(jnp.where(at < 6, rest, 0.0), axis=0, keepdims=True)
    after = jnp.sum(jnp.where(at >= 6, rest, 0.0), axis=0, keepdims=True)
    return middle, before, after


def bonds(far, home):
    vector = [far[j : j + 1, :] - home[:, j : j + 1] for j in range(3)]
    square = vector[0] * vector[0] + vector[1] * vector[1] + vector[2] * vector[2]
    return vector, jnp.maximum(1.0 - square * (1.0 / 9.0), 0.0)


def stiffness(
    basis, left, right, own, below, above, images, grams,
    geo, geo_cols, geo_far, field, high, low, dil_high, dil_low, result,
):
    geo[...] = jnp.zeros((8, 1024), f32)
    geo[:, 256:768] = own[...]
    for part, lane in ((below, 64), (above, 768)):
        geo[0:4, lane : lane + 192] = part[28:32, 0:192]
        geo[4:8, lane : lane + 192] = part[60:64, 0:192]
    lane = lax.broadcasted_iota(jnp.int32, (8, 1024), 1)
    channel = lax.broadcasted_iota(jnp.int32, (8, 1024), 0)
    xi = lane & 31
    at_x = jnp.where(xi < 16, xi, jnp.where(xi < 22, xi - 22, xi - 6))
    at_y = (lane >> 5) - 8
    place = jnp.where(channel == 0, at_x, jnp.where(channel == 1, at_y, 0)).astype(f32)
    placed = geo[...] + place
    geo[...] = placed
    geo_cols[...] = placed.T
    for s in range(STRIPS):
        start = GROUP * (2 * s + 1)
        geo_far[s] = geo[:, start : start + FAR]

    for c in range(3):
        for y in range(SIDE):
            j, t = divmod(y, 4)
            src = j * 18 + c * 6
            row = GROUP * y
            field[c, row : row + 16, :] = basis[c, :, y * NCOL : (y + 1) * NCOL]
            field[c, row + 16 : row + 22, :] = left[src : src + 6, t * NCOL : (t + 1) * NCOL]
            field[c, row + 22 : row + 28, :] = right[src : src + 6, t * NCOL : (t + 1) * NCOL]
            field[c, row + 28 : row + 32, :] = jnp.zeros((4, NCOL), f32)
        for y in range(SIDE):
            row = GROUP * y
            parts = split(field[c, row : row + 32, :])
            high[c, 256 + row : 288 + row, :] = parts[0]
            low[c, 256 + row : 288 + row, :] = parts[1]
        for j in range(HALO):
            for part, first in ((below, 2), (above, 24)):
                row = GROUP * (first + j)
                parts = split(part[GROUP * c : GROUP * (c + 1), j * NCOL : (j + 1) * NCOL])
                high[c, row : row + 32, :] = parts[0]
                low[c, row : row + 32, :] = parts[1]
        for row in (0, 960):
            for ref in (high, low):
                ref[c, row : row + 64, :] = jnp.zeros((64, NCOL), bf16)

    row = lax.broadcasted_iota(jnp.int32, (64, FAR), 0)
    lane = lax.broadcasted_iota(jnp.int32, (64, FAR), 1)
    at_self = lane == row + 96
    home_row = row & 31

    def dilatations(s, carry):
        near = pl.multiple_of(GROUP * (2 * s + 4), 64)
        start = pl.multiple_of(GROUP * (2 * s + 1), 32)
        home = geo_cols[pl.ds(near, 64), :]
        middle, before, after = block_masks(s, home[0:32])
        vector, weight = bonds(geo_far[s], home)
        weight = weight * jnp.where(home_row < 16, middle, jnp.where(home_row < 22, before, after))
        total = jnp.zeros((64, NCOL), f32)
        for j in range(3):
            matrix = weight * vector[j]
            matrix = jnp.where(at_self, -jnp.sum(matrix, axis=1, keepdims=True), matrix)
            total = total + product(
                matrix, high[j, pl.ds(start, FAR), :], low[j, pl.ds(start, FAR), :]
            )
        parts = split(total * (home[:, 4:5] * (1.0 / 27.0)))
        dil_high[pl.ds(near, 64), :] = parts[0]
        dil_low[pl.ds(near, 64), :] = parts[1]
        return carry

    lax.fori_loop(0, STRIPS, dilatations, 0)

    row = lax.broadcasted_iota(jnp.int32, (32, FAR), 0)
    lane = lax.broadcasted_iota(jnp.int32, (32, FAR), 1)
    own_self = lane == row + jnp.where(row < 16, 96, 112)

    def forces(s, carry):
        near = pl.multiple_of(GROUP * (2 * s + 4), 64)
        start = pl.multiple_of(GROUP * (2 * s + 1), 32)
        first = geo_cols[pl.ds(near, 32), :]
        second = geo_cols[pl.ds(near + 32, 16), :]
        home = jnp.concatenate([first[0:16], second], axis=0)
        middle, _, _ = block_masks(s, first)
        far = geo_far[s]
        vector, weight = bonds(far, home)
        weight = weight * middle
        coupling = weight * ((home[:, 3:4] + far[3:4, :]) * (1.0 / 18.0))
        spring = home[:, 5:6]
        pairs = {}
        for i in range(3):
            side = coupling * vector[i]
            for j in range(i, 3):
                matrix = side * vector[j]
                total = jnp.sum(matrix, axis=1, keepdims=True)
                if i == j:
                    total = total + spring
                pairs[i, j] = pairs[j, i] = jnp.where(own_self, total, -matrix)
        image = jnp.zeros((96, NCOL), f32)
        for j in range(3):
            stacked = jnp.concatenate([pairs[i, j] for i in range(3)], axis=0)
            image = image + product(
                stacked, high[j, pl.ds(start, FAR), :], low[j, pl.ds(start, FAR), :]
            )
        sides = []
        for i in range(3):
            matrix = weight * vector[i]
            total = jnp.sum(matrix, axis=1, keepdims=True)
            sides.append(-jnp.where(own_self, total, matrix))
        image = image + product(
            jnp.concatenate(sides, axis=0),
            dil_high[pl.ds(start, FAR), :],
            dil_low[pl.ds(start, FAR), :],
        )
        at = pl.multiple_of(32 * (s - 2), 32)
        for i in range(3):
            result[i, pl.ds(at, 32), :] = image[32 * i : 32 * i + 32]
        return carry

    lax.fori_loop(2, 10, forces, 0)

    for c in range(3):
        for y in range(SIDE):
            images[c, :, y * NCOL : (y + 1) * NCOL] = result[c, 16 * y : 16 * y + 16, :]

    rows = field[...].reshape(3, SIDE, GROUP, NCOL)[:, :, 0:16, :].reshape(768, NCOL)
    image = result[...].reshape(768, NCOL)

    def gram(a, b):
        return lax.dot_general(
            a, b, (((0,), (0,)), ((), ())), precision=highest, preferred_element_type=f32
        )

    mass = gram(rows, rows)
    stiff = gram(rows, image)
    mirror = gram(image, rows)
    at_row = lax.broadcasted_iota(jnp.int32, (NCOL, NCOL), 0)
    at_col = lax.broadcasted_iota(jnp.int32, (NCOL, NCOL), 1)
    grams[0:192, :] = jnp.where(at_row >= at_col, mass, 0.5 * (stiff + mirror))
    diagonal = jnp.sum(jnp.where(at_row == at_col, stiff, 0.0), axis=0, keepdims=True)
    grams[192:200, :] = jnp.broadcast_to(diagonal, (8, NCOL))
    grams[200:256, :] = jnp.zeros((56, NCOL), f32)


def eliminate(ref, step, capture):
    base = 8 * step
    panel = ref[base : base + 8, :]
    columns = [ref[:, base + i : base + i + 1] for i in range(8)]
    at = lax.broadcasted_iota(jnp.int32, panel.shape, 0)
    caught = panel
    for i in range(8):
        pivot = panel[i : i + 1, base + i : base + i + 1]
        row = panel[i : i + 1, :]
        scaled = row * (1.0 / pivot)
        if capture:
            root = lax.rsqrt(pivot)
            root = root * (1.5 - 0.5 * pivot * root * root)
            caught = jnp.where(at == i, row * root, caught)
        panel = jnp.where(at == i, scaled, panel - panel[:, base + i : base + i + 1] * scaled)
    rest = ref[...]
    for i in range(8):
        rest = rest - columns[i] * panel[i : i + 1, :]
    ref[...] = rest
    ref[base : base + 8, :] = panel
    return caught


def rotation(scale, grams, basis, images, modes, mode_images, reduced, square, work, small, factor):
    packed = grams[0:192, :] * scale
    diagonal = grams[192:193, :] * scale
    square[...] = jnp.zeros((256, 256), f32)
    square[0:192, 0:192] = packed
    flipped = square[...].T[0:192, 0:192]
    at_row = lax.broadcasted_iota(jnp.int32, (NCOL, NCOL), 0)
    at_col = lax.broadcasted_iota(jnp.int32, (NCOL, NCOL), 1)
    mass = jnp.where(at_row >= at_col, packed, flipped)
    stiff = jnp.where(at_row < at_col, packed, jnp.where(at_row > at_col, flipped, diagonal))
    work[:, 0:192] = stiff
    work[:, 192:256] = mass[:, 0:64]
    for step in range(24):
        eliminate(work, step, False)
    solved = work[:, 192:256]
    weighted = jnp.dot(mass, solved, precision=highest, preferred_element_type=f32)
    square[0:192, 0:64] = solved
    turned = square[...].T[0:64, 0:192]
    small[:, 0:64] = jnp.dot(turned, weighted, precision=highest, preferred_element_type=f32)
    small[:, 64:256] = turned
    factor[...] = jnp.zeros((128, 384), f32)
    for step in range(8):
        caught = eliminate(small, step, True)[:, 64:256]
        factor[8 * step : 8 * step + 8, 0:192] = caught
        factor[64 + 8 * step : 72 + 8 * step, 192:384] = caught
    rotate = factor[0:64, 0:192]
    across = (((1,), (1,)), ((), ()))
    lifted = lax.dot_general(stiff, rotate, across, precision=highest, preferred_element_type=f32)
    reduced[...] = jnp.dot(rotate, lifted, precision=highest, preferred_element_type=f32)
    both = factor[...]
    for source, out in ((basis, modes), (images, mode_images)):
        for y in range(SIDE // 2):
            value = source[:, :, y * 384 : (y + 1) * 384].reshape(48, 384)
            value = lax.dot_general(value, both, across, precision=highest, preferred_element_type=f32)
            out[:, :, y * 128 : (y + 1) * 128] = value.reshape(3, SIDE, 128)


def exchange(up, down, axis):
    size = lax.axis_size(axis)
    forward = [(i, i + 1) for i in range(size - 1)]
    backward = [(i + 1, i) for i in range(size - 1)]
    return lax.ppermute(up, axis, forward), lax.ppermute(down, axis, backward)


def spread(value, axis):
    size = lax.axis_size(axis)
    return lax.all_to_all(jnp.broadcast_to(value[None], (size,) + value.shape), axis, 0, 0, tiled=True)


def local(basis, offsets, bond_modulus, bulk_modulus, springs, intact):
    slabs = lax.axis_size("slab")
    bands = lax.axis_size("band")
    total_rows = float(3 * SIDE * SIDE * slabs * bands)

    with jax.named_scope("geometry"):
        table = intact[0].astype(f32)
        table = jnp.stack([jnp.pad(table[:, 6:9], ((0, 0), (0, 3))), table[:, 0:6]])
        table = jnp.repeat(table, SIDE // 2, axis=1)
        points = jnp.concatenate(
            [offsets, bond_modulus[None], bulk_modulus[None], springs[None]], axis=0
        ).transpose(0, 2, 1)

        def lanes(part, width):
            pads = width - part.shape[2]
            part = jnp.concatenate(
                [
                    jnp.pad(part, ((0, 0), (0, 0), (0, pads))),
                    jnp.pad(table, ((0, 0), (0, 0), (0, width - 6))),
                ],
                axis=0,
            )
            return part.reshape(8, SIDE * width)

        geo = jnp.concatenate(
            [lanes(points, 16), lanes(points[:, :, SIDE - HALO :], 8), lanes(points[:, :, :HALO], 8)],
            axis=1,
        )

    with jax.named_scope("halo"):
        up, down = call(pack_x, [(80, 768)] * 2, [], (basis, geo), 1000, "pack_x")
        left, right = exchange(up, down, "slab")
        up, down, own = call(
            pack_y, [(96, 1152)] * 2 + [(8, 512)], [], (basis, geo, left, right), 1000, "pack_y"
        )
        below, above = exchange(up, down, "band")

    with jax.named_scope("stiffness"):
        images, grams = call(
            stiffness,
            [(3, SIDE, SIDE * NCOL), (256, NCOL)],
            [
                pltpu.VMEM((8, 1024), f32),
                pltpu.VMEM((1024, 8), f32),
                pltpu.VMEM((STRIPS, 8, FAR), f32),
                pltpu.VMEM((3, 512, NCOL), f32),
                pltpu.VMEM((3, 1024, NCOL), bf16),
                pltpu.VMEM((3, 1024, NCOL), bf16),
                pltpu.VMEM((1024, NCOL), bf16),
                pltpu.VMEM((1024, NCOL), bf16),
                pltpu.VMEM((3, 256, NCOL), f32),
            ],
            (basis, left, right, own, below, above),
            2 * 10**9,
            "stiffness",
        )

    with jax.named_scope("sums"):
        part = lax.all_to_all(grams.reshape(slabs, 256 // slabs, NCOL), "slab", 0, 0, tiled=True)
        part = spread(jnp.sum(part, axis=0), "band")
        part = spread(jnp.sum(part, axis=0), "slab")
        grams = part.reshape(256, NCOL)

    with jax.named_scope("rotation"):
        def kernel(*refs):
            rotation(1.0 / total_rows, *refs)

        modes, mode_images, reduced = call(
            kernel,
            [(3, SIDE, SIDE * MODES)] * 2 + [(MODES, MODES)],
            [
                pltpu.VMEM((256, 256), f32),
                pltpu.VMEM((192, 256), f32),
                pltpu.VMEM((64, 256), f32),
                pltpu.VMEM((128, 384), f32),
            ],
            (grams, basis, images),
            10**9,
            "rotation",
        )
    return modes, mode_images, reduced


def solution(mesh):
    in_specs = (
        P(None, "slab", "band"),
        P(None, "slab", "band"),
        P("slab", "band"),
        P("slab", "band"),
        P("slab", "band"),
        P("slab", "band", None),
    )
    out_specs = (P(None, "slab", "band"), P(None, "slab", "band"), P())
    return jax.shard_map(local, mesh=mesh, in_specs=in_specs, out_specs=out_specs, check_vma=False)
```

```python
import jax
import jax.numpy as jnp
from jax import lax
from jax.experimental import pallas as pl
from jax.experimental.pallas import tpu as pltpu
from jax.sharding import PartitionSpec as P


MODES = 64
NCOL = 192
SIDE = 16
HALO = 6
GROUP = 32
STRIPS = 12
FAR = 256
highest = lax.Precision.HIGHEST
f32 = jnp.float32
bf16 = jnp.bfloat16

VMEM = pl.BlockSpec(memory_space=pltpu.VMEM)
PARAMS = pltpu.CompilerParams(vmem_limit_bytes=56 * 1024 * 1024)


def call(kernel, outs, scratch, args, flops, name):
    size = sum(a.size for a in args) + sum(o[0] * o[1] * (o[2] if len(o) > 2 else 1) for o in outs)
    return pl.pallas_call(
        kernel,
        out_shape=[jax.ShapeDtypeStruct(o, f32) for o in outs],
        in_specs=[VMEM] * len(args),
        out_specs=[VMEM] * len(outs),
        scratch_shapes=scratch,
        compiler_params=PARAMS,
        cost_estimate=pl.CostEstimate(flops=flops, bytes_accessed=4 * size, transcendentals=0),
        name=name,
    )(*args)


def pack_x(basis, geo, up, down):
    for out, first, lane in ((up, SIDE - HALO, 256), (down, 0, 384)):
        for c in range(3):
            for j in range(4):
                row = j * 18 + c * 6
                out[row : row + 6, :] = basis[c, first : first + 6, j * 768 : (j + 1) * 768]
        out[72:80, :] = jnp.zeros((8, 768), f32)
        out[72:80, 0:128] = geo[:, lane : lane + 128]


def pack_y(basis, geo, left, right, up, down, own):
    own[...] = jnp.zeros((8, 512), f32)
    for y in range(SIDE):
        at = GROUP * y
        own[:, at : at + 16] = geo[:, 16 * y : 16 * y + 16]
        own[:, at + 16 : at + 22] = left[72:80, 8 * y : 8 * y + 6]
        own[:, at + 22 : at + 28] = right[72:80, 8 * y : 8 * y + 6]
    for out, first in ((up, SIDE - HALO), (down, 0)):
        pieces = ((2, 384, 768, 0), (3, 0, 768, 384)) if first else ((0, 0, 768, 0), (1, 0, 384, 768))
        for c in range(3):
            row = GROUP * c
            out[row : row + 16, :] = basis[c, :, first * NCOL : (first + HALO) * NCOL]
            for j, start, stop, lane in pieces:
                src = j * 18 + c * 6
                width = stop - start
                out[row + 16 : row + 22, lane : lane + width] = left[src : src + 6, start:stop]
                out[row + 22 : row + 28, lane : lane + width] = right[src : src + 6, start:stop]
            out[row + 28 : row + 32, :] = jnp.zeros((4, 1152), f32)
        lanes = slice(first * GROUP, (first + HALO) * GROUP)
        out[28:32, 0:192] = own[0:4, lanes]
        out[60:64, 0:192] = own[4:8, lanes]


def split(value):
    high = value.astype(bf16)
    return high, (value - high.astype(f32)).astype(bf16)


def product(left, right_high, right_low):
    high, low = split(left)
    return (
        jnp.dot(high, right_high, preferred_element_type=f32)
        + jnp.dot(high, right_low, preferred_element_type=f32)
        + jnp.dot(low, right_high, preferred_element_type=f32)
    )


def block_masks(s, table):
    y0 = 2 * s - 4
    lane = lax.broadcasted_iota(jnp.int32, (32, FAR), 1)
    row = lax.broadcasted_iota(jnp.int32, (32, FAR), 0)
    xi = lane & 31
    far_x = jnp.where(xi < 16, 0, jnp.where(xi < 22, -1, 1))
    far_y = ((y0 - 3 + (lane >> 5)) >> 3) - (y0 >> 3)
    home_x = jnp.where(row < 16, 0, jnp.where(row < 22, -1, 1))
    entry = row - jnp.where(row < 16, 0, jnp.where(row < 22, 16, 22))
    entry = jnp.where(entry < 6, entry, -100)
    code = 3 * (far_x - home_x + 1) + far_y + 1
    value = jnp.where(code == entry, table[:, 7:8], 0.0)
    value = value + jnp.where(code == entry + 6, table[:, 6:7], 0.0)
    middle = jnp.sum(value[0:8], axis=0, keepdims=True)
    rest = value[16:32]
    at = lax.broadcasted_iota(jnp.int32, (16, FAR), 0)
    before = jnp.sum(jnp.where(at < 6, rest, 0.0), axis=0, keepdims=True)
    after = jnp.sum(jnp.where(at >= 6, rest, 0.0), axis=0, keepdims=True)
    return middle, before, after


def bonds(far, home):
    vector = [far[j : j + 1, :] - home[:, j : j + 1] for j in range(3)]
    square = vector[0] * vector[0] + vector[1] * vector[1] + vector[2] * vector[2]
    return vector, jnp.maximum(1.0 - square * (1.0 / 9.0), 0.0)


def stiffness(
    basis, left, right, own, below, above, images, grams,
    geo, geo_cols, geo_far, field, high, low, dil_high, dil_low, result,
):
    geo[...] = jnp.zeros((8, 1024), f32)
    geo[:, 256:768] = own[...]
    for part, lane in ((below, 64), (above, 768)):
        geo[0:4, lane : lane + 192] = part[28:32, 0:192]
        geo[4:8, lane : lane + 192] = part[60:64, 0:192]
    lane = lax.broadcasted_iota(jnp.int32, (8, 1024), 1)
    channel = lax.broadcasted_iota(jnp.int32, (8, 1024), 0)
    xi = lane & 31
    at_x = jnp.where(xi < 16, xi, jnp.where(xi < 22, xi - 22, xi - 6))
    at_y = (lane >> 5) - 8
    place = jnp.where(channel == 0, at_x, jnp.where(channel == 1, at_y, 0)).astype(f32)
    placed = geo[...] + place
    geo[...] = placed
    geo_cols[...] = placed.T
    for s in range(STRIPS):
        start = GROUP * (2 * s + 1)
        geo_far[s] = geo[:, start : start + FAR]

    for c in range(3):
        for y in range(SIDE):
            j, t = divmod(y, 4)
            src = j * 18 + c * 6
            row = GROUP * y
            field[c, row : row + 16, :] = basis[c, :, y * NCOL : (y + 1) * NCOL]
            field[c, row + 16 : row + 22, :] = left[src : src + 6, t * NCOL : (t + 1) * NCOL]
            field[c, row + 22 : row + 28, :] = right[src : src + 6, t * NCOL : (t + 1) * NCOL]
            field[c, row + 28 : row + 32, :] = jnp.zeros((4, NCOL), f32)
        for y in range(SIDE):
            row = GROUP * y
            parts = split(field[c, row : row + 32, :])
            high[c, 256 + row : 288 + row, :] = parts[0]
            low[c, 256 + row : 288 + row, :] = parts[1]
        for j in range(HALO):
            for part, first in ((below, 2), (above, 24)):
                row = GROUP * (first + j)
                parts = split(part[GROUP * c : GROUP * (c + 1), j * NCOL : (j + 1) * NCOL])
                high[c, row : row + 32, :] = parts[0]
                low[c, row : row + 32, :] = parts[1]
        for row in (0, 960):
            for ref in (high, low):
                ref[c, row : row + 64, :] = jnp.zeros((64, NCOL), bf16)

    row = lax.broadcasted_iota(jnp.int32, (64, FAR), 0)
    lane = lax.broadcasted_iota(jnp.int32, (64, FAR), 1)
    at_self = lane == row + 96
    home_row = row & 31

    def dilatations(s, carry):
        near = pl.multiple_of(GROUP * (2 * s + 4), 64)
        start = pl.multiple_of(GROUP * (2 * s + 1), 32)
        home = geo_cols[pl.ds(near, 64), :]
        middle, before, after = block_masks(s, home[0:32])
        vector, weight = bonds(geo_far[s], home)
        weight = weight * jnp.where(home_row < 16, middle, jnp.where(home_row < 22, before, after))
        total = jnp.zeros((64, NCOL), f32)
        for j in range(3):
            matrix = weight * vector[j]
            matrix = jnp.where(at_self, -jnp.sum(matrix, axis=1, keepdims=True), matrix)
            total = total + product(
                matrix, high[j, pl.ds(start, FAR), :], low[j, pl.ds(start, FAR), :]
            )
        parts = split(total * (home[:, 4:5] * (1.0 / 27.0)))
        dil_high[pl.ds(near, 64), :] = parts[0]
        dil_low[pl.ds(near, 64), :] = parts[1]
        return carry

    lax.fori_loop(0, STRIPS, dilatations, 0)

    row = lax.broadcasted_iota(jnp.int32, (32, FAR), 0)
    lane = lax.broadcasted_iota(jnp.int32, (32, FAR), 1)
    own_self = lane == row + jnp.where(row < 16, 96, 112)

    def forces(s, carry):
        near = pl.multiple_of(GROUP * (2 * s + 4), 64)
        start = pl.multiple_of(GROUP * (2 * s + 1), 32)
        first = geo_cols[pl.ds(near, 32), :]
        second = geo_cols[pl.ds(near + 32, 16), :]
        home = jnp.concatenate([first[0:16], second], axis=0)
        middle, _, _ = block_masks(s, first)
        far = geo_far[s]
        vector, weight = bonds(far, home)
        weight = weight * middle
        coupling = weight * ((home[:, 3:4] + far[3:4, :]) * (1.0 / 18.0))
        spring = home[:, 5:6]
        pairs = {}
        for i in range(3):
            side = coupling * vector[i]
            for j in range(i, 3):
                matrix = side * vector[j]
                total = jnp.sum(matrix, axis=1, keepdims=True)
                if i == j:
                    total = total + spring
                pairs[i, j] = pairs[j, i] = jnp.where(own_self, total, -matrix)
        image = jnp.zeros((96, NCOL), f32)
        for j in range(3):
            stacked = jnp.concatenate([pairs[i, j] for i in range(3)], axis=0)
            image = image + product(
                stacked, high[j, pl.ds(start, FAR), :], low[j, pl.ds(start, FAR), :]
            )
        sides = []
        for i in range(3):
            matrix = weight * vector[i]
            total = jnp.sum(matrix, axis=1, keepdims=True)
            sides.append(-jnp.where(own_self, total, matrix))
        image = image + product(
            jnp.concatenate(sides, axis=0),
            dil_high[pl.ds(start, FAR), :],
            dil_low[pl.ds(start, FAR), :],
        )
        at = pl.multiple_of(32 * (s - 2), 32)
        for i in range(3):
            result[i, pl.ds(at, 32), :] = image[32 * i : 32 * i + 32]
        return carry

    lax.fori_loop(2, 10, forces, 0)

    for c in range(3):
        for y in range(SIDE):
            images[c, :, y * NCOL : (y + 1) * NCOL] = result[c, 16 * y : 16 * y + 16, :]

    rows = field[...].reshape(3, SIDE, GROUP, NCOL)[:, :, 0:16, :].reshape(768, NCOL)
    image = result[...].reshape(768, NCOL)

    def gram(a, b):
        return lax.dot_general(
            a, b, (((0,), (0,)), ((), ())), precision=highest, preferred_element_type=f32
        )

    mass = gram(rows, rows)
    stiff = gram(rows, image)
    mirror = gram(image, rows)
    at_row = lax.broadcasted_iota(jnp.int32, (NCOL, NCOL), 0)
    at_col = lax.broadcasted_iota(jnp.int32, (NCOL, NCOL), 1)
    grams[0:192, :] = jnp.where(at_row >= at_col, mass, 0.5 * (stiff + mirror))
    diagonal = jnp.sum(jnp.where(at_row == at_col, stiff, 0.0), axis=0, keepdims=True)
    grams[192:200, :] = jnp.broadcast_to(diagonal, (8, NCOL))
    grams[200:256, :] = jnp.zeros((56, NCOL), f32)


def lanes_of(tile, column):
    half = tile[column // 128]
    at = column % 128
    return jnp.broadcast_to(half[:, at : at + 1], (8, 128))


def row_of(value, row):
    return jnp.broadcast_to(value[row : row + 1, :], (8, 128))


def reduce_block(ref, row0, col0, out):
    at = lax.broadcasted_iota(jnp.int32, (8, 128), 0)
    tiles = []
    for q in range(8):
        row = row0 + 8 * q
        tiles.append([ref[row : row + 8, 0:128], ref[row : row + 8, 128:256]])
    pivots = [lanes_of(tiles[0], col0 + j) for j in range(8)]
    for t in range(8):
        first = col0 + 8 * t
        others = [q for q in range(8) if q != t]
        if out is not None:
            others = [q for q in others if q > t]
        columns = {q: [lanes_of(tiles[q], first + i) for i in range(8)] for q in others}
        ahead, following = [], []
        if t < 7:
            ahead = [lanes_of(tiles[t], first + 8 + j) for j in range(8)]
            following = [lanes_of(tiles[t + 1], first + 8 + j) for j in range(8)]
        panel = tiles[t]
        caught = list(panel)
        for i in range(8):
            pivot = row_of(pivots[i], i)
            inverse = 1.0 / pivot
            factor = pivots[i]
            chosen = at == i

            def step(value):
                row = row_of(value, i) * inverse
                return jnp.where(chosen, row, value - factor * row)

            if out is not None:
                root = lax.rsqrt(pivot)
                root = root * (1.5 - 0.5 * pivot * root * root)
                caught = [jnp.where(chosen, row_of(p, i) * root, c) for p, c in zip(panel, caught)]
            pivots = [step(p) if j > i else p for j, p in enumerate(pivots)]
            ahead = [step(p) for p in ahead]
            panel = [step(p) for p in panel]
        tiles[t] = panel
        if out is not None:
            out(t, caught)
        if t < 7:
            pivots = following
            for i in range(8):
                pivots = [
                    p - columns[t + 1][i] * row_of(a, i) for p, a in zip(pivots, ahead)
                ]
        for i in range(8):
            rows = [row_of(p, i) for p in panel]
            for q in others:
                tiles[q] = [v - columns[q][i] * r for v, r in zip(tiles[q], rows)]
    if out is None:
        for q in range(8):
            row = row0 + 8 * q
            ref[row : row + 8, 0:128] = tiles[q][0]
            ref[row : row + 8, 128:256] = tiles[q][1]


def rotation(scale, grams, basis, images, modes, mode_images, reduced, square, work, small, factor):
    packed = grams[0:192, :] * scale
    diagonal = grams[192:193, :] * scale
    square[...] = jnp.zeros((256, 256), f32)
    square[0:192, 0:192] = packed
    flipped = square[...].T[0:192, 0:192]
    at_row = lax.broadcasted_iota(jnp.int32, (NCOL, NCOL), 0)
    at_col = lax.broadcasted_iota(jnp.int32, (NCOL, NCOL), 1)
    mass = jnp.where(at_row >= at_col, packed, flipped)
    stiff = jnp.where(at_row < at_col, packed, jnp.where(at_row > at_col, flipped, diagonal))
    work[:, 0:192] = stiff
    work[:, 192:256] = mass[:, 0:64]
    for block in range(3):
        base = 64 * block
        reduce_block(work, base, base, None)
        reduced_rows = work[base : base + 64, :]
        for other in range(3):
            if other != block:
                rows = slice(64 * other, 64 * other + 64)
                work[rows, :] = work[rows, :] - jnp.dot(
                    work[rows, base : base + 64],
                    reduced_rows,
                    precision=highest,
                    preferred_element_type=f32,
                )
    solved = work[:, 192:256]
    weighted = jnp.dot(mass, solved, precision=highest, preferred_element_type=f32)
    square[0:192, 0:64] = solved
    turned = square[...].T[0:64, 0:192]
    small[:, 0:64] = jnp.dot(turned, weighted, precision=highest, preferred_element_type=f32)
    small[:, 64:256] = turned
    factor[...] = jnp.zeros((128, 384), f32)

    def keep(t, caught):
        value = jnp.concatenate(caught, axis=1)[:, 64:256]
        factor[8 * t : 8 * t + 8, 0:192] = value
        factor[64 + 8 * t : 72 + 8 * t, 192:384] = value

    reduce_block(small, 0, 0, keep)
    rotate = factor[0:64, 0:192]
    across = (((1,), (1,)), ((), ()))
    lifted = lax.dot_general(stiff, rotate, across, precision=highest, preferred_element_type=f32)
    reduced[...] = jnp.dot(rotate, lifted, precision=highest, preferred_element_type=f32)
    both = factor[...]
    for source, out in ((basis, modes), (images, mode_images)):
        for y in range(SIDE // 2):
            value = source[:, :, y * 384 : (y + 1) * 384].reshape(48, 384)
            value = lax.dot_general(value, both, across, precision=highest, preferred_element_type=f32)
            out[:, :, y * 128 : (y + 1) * 128] = value.reshape(3, SIDE, 128)


def exchange(up, down, axis):
    size = lax.axis_size(axis)
    forward = [(i, i + 1) for i in range(size - 1)]
    backward = [(i + 1, i) for i in range(size - 1)]
    return lax.ppermute(up, axis, forward), lax.ppermute(down, axis, backward)


def spread(value, axis):
    size = lax.axis_size(axis)
    return lax.all_to_all(jnp.broadcast_to(value[None], (size,) + value.shape), axis, 0, 0, tiled=True)


def local(basis, offsets, bond_modulus, bulk_modulus, springs, intact):
    slabs = lax.axis_size("slab")
    bands = lax.axis_size("band")
    total_rows = float(3 * SIDE * SIDE * slabs * bands)

    with jax.named_scope("geometry"):
        table = intact[0].astype(f32)
        table = jnp.stack([jnp.pad(table[:, 6:9], ((0, 0), (0, 3))), table[:, 0:6]])
        table = jnp.repeat(table, SIDE // 2, axis=1)
        points = jnp.concatenate(
            [offsets, bond_modulus[None], bulk_modulus[None], springs[None]], axis=0
        ).transpose(0, 2, 1)

        def lanes(part, width):
            pads = width - part.shape[2]
            part = jnp.concatenate(
                [
                    jnp.pad(part, ((0, 0), (0, 0), (0, pads))),
                    jnp.pad(table, ((0, 0), (0, 0), (0, width - 6))),
                ],
                axis=0,
            )
            return part.reshape(8, SIDE * width)

        geo = jnp.concatenate(
            [lanes(points, 16), lanes(points[:, :, SIDE - HALO :], 8), lanes(points[:, :, :HALO], 8)],
            axis=1,
        )

    with jax.named_scope("halo"):
        up, down = call(pack_x, [(80, 768)] * 2, [], (basis, geo), 1000, "pack_x")
        left, right = exchange(up, down, "slab")
        up, down, own = call(
            pack_y, [(96, 1152)] * 2 + [(8, 512)], [], (basis, geo, left, right), 1000, "pack_y"
        )
        below, above = exchange(up, down, "band")

    with jax.named_scope("stiffness"):
        images, grams = call(
            stiffness,
            [(3, SIDE, SIDE * NCOL), (256, NCOL)],
            [
                pltpu.VMEM((8, 1024), f32),
                pltpu.VMEM((1024, 8), f32),
                pltpu.VMEM((STRIPS, 8, FAR), f32),
                pltpu.VMEM((3, 512, NCOL), f32),
                pltpu.VMEM((3, 1024, NCOL), bf16),
                pltpu.VMEM((3, 1024, NCOL), bf16),
                pltpu.VMEM((1024, NCOL), bf16),
                pltpu.VMEM((1024, NCOL), bf16),
                pltpu.VMEM((3, 256, NCOL), f32),
            ],
            (basis, left, right, own, below, above),
            2 * 10**9,
            "stiffness",
        )

    with jax.named_scope("sums"):
        part = lax.all_to_all(grams.reshape(slabs, 256 // slabs, NCOL), "slab", 0, 0, tiled=True)
        part = spread(jnp.sum(part, axis=0), "band")
        part = spread(jnp.sum(part, axis=0), "slab")
        grams = part.reshape(256, NCOL)

    with jax.named_scope("rotation"):
        def kernel(*refs):
            rotation(1.0 / total_rows, *refs)

        modes, mode_images, reduced = call(
            kernel,
            [(3, SIDE, SIDE * MODES)] * 2 + [(MODES, MODES)],
            [
                pltpu.VMEM((256, 256), f32),
                pltpu.VMEM((192, 256), f32),
                pltpu.VMEM((64, 256), f32),
                pltpu.VMEM((128, 384), f32),
            ],
            (grams, basis, images),
            10**9,
            "rotation",
        )
    return modes, mode_images, reduced


def solution(mesh):
    in_specs = (
        P(None, "slab", "band"),
        P(None, "slab", "band"),
        P("slab", "band"),
        P("slab", "band"),
        P("slab", "band"),
        P("slab", "band", None),
    )
    out_specs = (P(None, "slab", "band"), P(None, "slab", "band"), P())
    return jax.shard_map(local, mesh=mesh, in_specs=in_specs, out_specs=out_specs, check_vma=False)
```

```python
import jax
import jax.numpy as jnp
from jax import lax
from jax.experimental import pallas as pl
from jax.experimental.pallas import tpu as pltpu
from jax.sharding import PartitionSpec as P


MODES = 64
NCOL = 192
SIDE = 16
HALO = 6
GROUP = 32
STRIPS = 12
FAR = 256
highest = lax.Precision.HIGHEST
f32 = jnp.float32
bf16 = jnp.bfloat16

VMEM = pl.BlockSpec(memory_space=pltpu.VMEM)
PARAMS = pltpu.CompilerParams(vmem_limit_bytes=56 * 1024 * 1024)


def hold(value):
    return pltpu.with_memory_space_constraint(value, pltpu.VMEM)


def call(kernel, outs, scratch, args, flops, name, near=True):
    size = sum(a.size for a in args) + sum(o[0] * o[1] * (o[2] if len(o) > 2 else 1) for o in outs)
    return pl.pallas_call(
        kernel,
        out_shape=[(pltpu.VMEM if near else jax.ShapeDtypeStruct)(o, f32) for o in outs],
        in_specs=[VMEM] * len(args),
        out_specs=[VMEM] * len(outs),
        scratch_shapes=scratch,
        compiler_params=PARAMS,
        cost_estimate=pl.CostEstimate(flops=flops, bytes_accessed=4 * size, transcendentals=0),
        name=name,
    )(*args)


def pack_x(basis, offsets, bond, bulk, springs, intact, up, down, geo, square, table):
    square[...] = jnp.zeros((128, 128), f32)
    for channel in range(3):
        square[16 * channel : 16 * channel + 16, 0:16] = offsets[channel]
    for channel, part in ((3, bond), (4, bulk), (5, springs)):
        square[16 * channel : 16 * channel + 16, 0:16] = part[...]
    table[...] = square[...].T
    for y in range(SIDE):
        for channel in range(6):
            at = 16 * channel
            geo[channel : channel + 1, 16 * y : 16 * y + 16] = table[y : y + 1, at : at + 16]
    lists = intact[...].astype(f32)
    gap = jnp.zeros((1, 4), f32)
    fill = jnp.zeros((1, 3), f32)
    for by in range(2):
        most = lists[0, by : by + 1, 0:6]
        rest = jnp.concatenate([lists[0, by : by + 1, 6:9], fill], axis=1)
        for row, part in ((6, rest), (7, most)):
            pattern = jnp.concatenate([part, gap, part], axis=1)
            pattern = jnp.concatenate([pattern, pattern], axis=1)
            pattern = jnp.concatenate([pattern, pattern], axis=1)
            pattern = jnp.concatenate([pattern, pattern], axis=1)
            geo[row : row + 1, 128 * by : 128 * by + 128] = pattern
    for out, first in ((up, SIDE - HALO), (down, 0)):
        for c in range(3):
            for j in range(4):
                row = j * 18 + c * 6
                out[row : row + 6, :] = basis[c, first : first + 6, j * 768 : (j + 1) * 768]
        out[72:80, :] = jnp.zeros((8, 768), f32)
        out[72:80, 0:256] = geo[...]


def pack_y(basis, geo, left, right, up, down, own):
    own[...] = jnp.zeros((8, 512), f32)
    for y in range(SIDE):
        at = GROUP * y
        own[:, at : at + 16] = geo[:, 16 * y : 16 * y + 16]
        own[:, at + 16 : at + 22] = left[72:80, 16 * y + 10 : 16 * y + 16]
        own[:, at + 22 : at + 28] = right[72:80, 16 * y : 16 * y + 6]
    for out, first in ((up, SIDE - HALO), (down, 0)):
        pieces = ((2, 384, 768, 0), (3, 0, 768, 384)) if first else ((0, 0, 768, 0), (1, 0, 384, 768))
        for c in range(3):
            row = GROUP * c
            out[row : row + 16, :] = basis[c, :, first * NCOL : (first + HALO) * NCOL]
            for j, start, stop, lane in pieces:
                src = j * 18 + c * 6
                width = stop - start
                out[row + 16 : row + 22, lane : lane + width] = left[src : src + 6, start:stop]
                out[row + 22 : row + 28, lane : lane + width] = right[src : src + 6, start:stop]
            out[row + 28 : row + 32, :] = jnp.zeros((4, 1152), f32)
        lanes = slice(first * GROUP, (first + HALO) * GROUP)
        out[28:32, 0:192] = own[0:4, lanes]
        out[60:64, 0:192] = own[4:8, lanes]


def split(value):
    high = value.astype(bf16)
    return high, (value - high.astype(f32)).astype(bf16)


def product(left, right_high, right_low):
    high, low = split(left)
    return (
        jnp.dot(high, right_high, preferred_element_type=f32)
        + jnp.dot(high, right_low, preferred_element_type=f32)
        + jnp.dot(low, right_high, preferred_element_type=f32)
    )


def gram(a, b):
    return lax.dot_general(
        a, b, (((0,), (0,)), ((), ())), precision=highest, preferred_element_type=f32
    )


def prepare(basis, rows, mass):
    for c in range(3):
        for y in range(SIDE):
            row = 256 * c + 16 * y
            rows[row : row + 16, :] = basis[c, :, y * NCOL : (y + 1) * NCOL]
    value = rows[...]
    mass[...] = gram(value, value)


def block_masks(s, table):
    y0 = 2 * s - 4
    lane = lax.broadcasted_iota(jnp.int32, (32, FAR), 1)
    row = lax.broadcasted_iota(jnp.int32, (32, FAR), 0)
    xi = lane & 31
    far_x = jnp.where(xi < 16, 0, jnp.where(xi < 22, -1, 1))
    far_y = ((y0 - 3 + (lane >> 5)) >> 3) - (y0 >> 3)
    home_x = jnp.where(row < 16, 0, jnp.where(row < 22, -1, 1))
    entry = row - jnp.where(row < 16, 0, jnp.where(row < 22, 16, 22))
    entry = jnp.where(entry < 6, entry, -100)
    code = 3 * (far_x - home_x + 1) + far_y + 1
    value = jnp.where(code == entry, table[:, 7:8], 0.0)
    value = value + jnp.where(code == entry + 6, table[:, 6:7], 0.0)
    middle = jnp.sum(value[0:8], axis=0, keepdims=True)
    rest = value[16:32]
    at = lax.broadcasted_iota(jnp.int32, (16, FAR), 0)
    before = jnp.sum(jnp.where(at < 6, rest, 0.0), axis=0, keepdims=True)
    after = jnp.sum(jnp.where(at >= 6, rest, 0.0), axis=0, keepdims=True)
    return middle, before, after


def bonds(far, home):
    vector = [far[j : j + 1, :] - home[:, j : j + 1] for j in range(3)]
    square = vector[0] * vector[0] + vector[1] * vector[1] + vector[2] * vector[2]
    return vector, jnp.maximum(1.0 - square * (1.0 / 9.0), 0.0)


def stiffness(
    rows, mass, left, right, own, below, above, images, grams,
    geo, geo_cols, geo_far, field, high, low, dil_high, dil_low, result,
):
    geo[...] = jnp.zeros((8, 1024), f32)
    geo[:, 256:768] = own[...]
    for part, lane in ((below, 64), (above, 768)):
        geo[0:4, lane : lane + 192] = part[28:32, 0:192]
        geo[4:8, lane : lane + 192] = part[60:64, 0:192]
    lane = lax.broadcasted_iota(jnp.int32, (8, 1024), 1)
    channel = lax.broadcasted_iota(jnp.int32, (8, 1024), 0)
    xi = lane & 31
    at_x = jnp.where(xi < 16, xi, jnp.where(xi < 22, xi - 22, xi - 6))
    at_y = (lane >> 5) - 8
    place = jnp.where(channel == 0, at_x, jnp.where(channel == 1, at_y, 0)).astype(f32)
    placed = geo[...] + place
    geo[...] = placed
    geo_cols[...] = placed.T
    for s in range(STRIPS):
        start = GROUP * (2 * s + 1)
        geo_far[s] = geo[:, start : start + FAR]

    for c in range(3):
        for y in range(SIDE):
            j, t = divmod(y, 4)
            src = j * 18 + c * 6
            row = GROUP * y
            field[c, row : row + 16, :] = rows[256 * c + 16 * y : 256 * c + 16 * y + 16, :]
            field[c, row + 16 : row + 22, :] = left[src : src + 6, t * NCOL : (t + 1) * NCOL]
            field[c, row + 22 : row + 28, :] = right[src : src + 6, t * NCOL : (t + 1) * NCOL]
            field[c, row + 28 : row + 32, :] = jnp.zeros((4, NCOL), f32)
        for y in range(SIDE):
            row = GROUP * y
            parts = split(field[c, row : row + 32, :])
            high[c, 256 + row : 288 + row, :] = parts[0]
            low[c, 256 + row : 288 + row, :] = parts[1]
        for j in range(HALO):
            for part, first in ((below, 2), (above, 24)):
                row = GROUP * (first + j)
                parts = split(part[GROUP * c : GROUP * (c + 1), j * NCOL : (j + 1) * NCOL])
                high[c, row : row + 32, :] = parts[0]
                low[c, row : row + 32, :] = parts[1]
        for row in (0, 960):
            for ref in (high, low):
                ref[c, row : row + 64, :] = jnp.zeros((64, NCOL), bf16)

    row = lax.broadcasted_iota(jnp.int32, (64, FAR), 0)
    lane = lax.broadcasted_iota(jnp.int32, (64, FAR), 1)
    at_self = lane == row + 96
    home_row = row & 31

    def dilatations(s, carry):
        near = pl.multiple_of(GROUP * (2 * s + 4), 64)
        start = pl.multiple_of(GROUP * (2 * s + 1), 32)
        home = geo_cols[pl.ds(near, 64), :]
        middle, before, after = block_masks(s, home[0:32])
        vector, weight = bonds(geo_far[s], home)
        weight = weight * jnp.where(home_row < 16, middle, jnp.where(home_row < 22, before, after))
        total = jnp.zeros((64, NCOL), f32)
        for j in range(3):
            matrix = weight * vector[j]
            matrix = jnp.where(at_self, -jnp.sum(matrix, axis=1, keepdims=True), matrix)
            total = total + product(
                matrix, high[j, pl.ds(start, FAR), :], low[j, pl.ds(start, FAR), :]
            )
        parts = split(total * (home[:, 4:5] * (1.0 / 27.0)))
        dil_high[pl.ds(near, 64), :] = parts[0]
        dil_low[pl.ds(near, 64), :] = parts[1]
        return carry

    lax.fori_loop(0, STRIPS, dilatations, 0, unroll=6)

    row = lax.broadcasted_iota(jnp.int32, (32, FAR), 0)
    lane = lax.broadcasted_iota(jnp.int32, (32, FAR), 1)
    own_self = lane == row + jnp.where(row < 16, 96, 112)

    def forces(s, carry):
        near = pl.multiple_of(GROUP * (2 * s + 4), 64)
        start = pl.multiple_of(GROUP * (2 * s + 1), 32)
        first = geo_cols[pl.ds(near, 32), :]
        second = geo_cols[pl.ds(near + 32, 16), :]
        home = jnp.concatenate([first[0:16], second], axis=0)
        middle, _, _ = block_masks(s, first)
        far = geo_far[s]
        vector, weight = bonds(far, home)
        weight = weight * middle
        coupling = weight * ((home[:, 3:4] + far[3:4, :]) * (1.0 / 18.0))
        spring = home[:, 5:6]
        pairs = {}
        for i in range(3):
            side = coupling * vector[i]
            for j in range(i, 3):
                matrix = side * vector[j]
                total = jnp.sum(matrix, axis=1, keepdims=True)
                if i == j:
                    total = total + spring
                pairs[i, j] = pairs[j, i] = jnp.where(own_self, total, -matrix)
        image = jnp.zeros((96, NCOL), f32)
        for j in range(3):
            stacked = jnp.concatenate([pairs[i, j] for i in range(3)], axis=0)
            image = image + product(
                stacked, high[j, pl.ds(start, FAR), :], low[j, pl.ds(start, FAR), :]
            )
        sides = []
        for i in range(3):
            matrix = weight * vector[i]
            total = jnp.sum(matrix, axis=1, keepdims=True)
            sides.append(-jnp.where(own_self, total, matrix))
        image = image + product(
            jnp.concatenate(sides, axis=0),
            dil_high[pl.ds(start, FAR), :],
            dil_low[pl.ds(start, FAR), :],
        )
        at = pl.multiple_of(32 * (s - 2), 32)
        for i in range(3):
            result[i, pl.ds(at, 32), :] = image[32 * i : 32 * i + 32]
        return carry

    lax.fori_loop(2, 10, forces, 0, unroll=4)

    for c in range(3):
        for y in range(SIDE):
            images[c, :, y * NCOL : (y + 1) * NCOL] = result[c, 16 * y : 16 * y + 16, :]

    stiff = gram(rows[...], result[...].reshape(768, NCOL))
    at_row = lax.broadcasted_iota(jnp.int32, (NCOL, NCOL), 0)
    at_col = lax.broadcasted_iota(jnp.int32, (NCOL, NCOL), 1)
    grams[0:192, :] = jnp.where(at_row >= at_col, mass[...], stiff)
    diagonal = jnp.sum(jnp.where(at_row == at_col, stiff, 0.0), axis=0, keepdims=True)
    grams[192:200, :] = jnp.broadcast_to(diagonal, (8, NCOL))
    grams[200:256, :] = jnp.zeros((56, NCOL), f32)


def lanes_of(tile, column):
    half = tile[column // 128]
    at = column % 128
    return jnp.broadcast_to(half[:, at : at + 1], (8, 128))


def row_of(value, row):
    return jnp.broadcast_to(value[row : row + 1, :], (8, 128))


def reduce_block(ref, row0, col0, out):
    at = lax.broadcasted_iota(jnp.int32, (8, 128), 0)
    tiles = []
    for q in range(8):
        row = row0 + 8 * q
        tiles.append([ref[row : row + 8, 0:128], ref[row : row + 8, 128:256]])
    pivots = [lanes_of(tiles[0], col0 + j) for j in range(8)]
    for t in range(8):
        first = col0 + 8 * t
        others = [q for q in range(8) if q != t]
        if out is not None:
            others = [q for q in others if q > t]
        columns = {q: [lanes_of(tiles[q], first + i) for i in range(8)] for q in others}
        ahead, following = [], []
        if t < 7:
            ahead = [lanes_of(tiles[t], first + 8 + j) for j in range(8)]
            following = [lanes_of(tiles[t + 1], first + 8 + j) for j in range(8)]
        panel = tiles[t]
        caught = list(panel)
        for i in range(8):
            pivot = row_of(pivots[i], i)
            inverse = 1.0 / pivot
            factor = pivots[i]
            chosen = at == i

            def step(value):
                row = row_of(value, i) * inverse
                return jnp.where(chosen, row, value - factor * row)

            if out is not None:
                root = lax.rsqrt(pivot)
                root = root * (1.5 - 0.5 * pivot * root * root)
                caught = [jnp.where(chosen, row_of(p, i) * root, c) for p, c in zip(panel, caught)]
            pivots = [step(p) if j > i else p for j, p in enumerate(pivots)]
            ahead = [step(p) for p in ahead]
            panel = [step(p) for p in panel]
        tiles[t] = panel
        if out is not None:
            out(t, caught)
        if t < 7:
            pivots = following
            for i in range(8):
                pivots = [
                    p - columns[t + 1][i] * row_of(a, i) for p, a in zip(pivots, ahead)
                ]
        for i in range(8):
            rows = [row_of(p, i) for p in panel]
            for q in others:
                tiles[q] = [v - columns[q][i] * r for v, r in zip(tiles[q], rows)]
    if out is None:
        for q in range(8):
            row = row0 + 8 * q
            ref[row : row + 8, 0:128] = tiles[q][0]
            ref[row : row + 8, 128:256] = tiles[q][1]


def rotation(scale, grams, basis, images, modes, mode_images, reduced, square, work, small, factor):
    packed = grams[0:192, :] * scale
    diagonal = grams[192:193, :] * scale
    square[...] = jnp.zeros((256, 256), f32)
    square[0:192, 0:192] = packed
    flipped = square[...].T[0:192, 0:192]
    at_row = lax.broadcasted_iota(jnp.int32, (NCOL, NCOL), 0)
    at_col = lax.broadcasted_iota(jnp.int32, (NCOL, NCOL), 1)
    mass = jnp.where(at_row >= at_col, packed, flipped)
    stiff = jnp.where(at_row < at_col, packed, jnp.where(at_row > at_col, flipped, diagonal))
    work[:, 0:192] = stiff
    work[:, 192:256] = mass[:, 0:64]
    for block in range(3):
        base = 64 * block
        reduce_block(work, base, base, None)
        reduced_rows = work[base : base + 64, :]
        for other in range(3):
            if other != block:
                rows = slice(64 * other, 64 * other + 64)
                work[rows, :] = work[rows, :] - jnp.dot(
                    work[rows, base : base + 64],
                    reduced_rows,
                    precision=highest,
                    preferred_element_type=f32,
                )
    solved = work[:, 192:256]
    weighted = jnp.dot(mass, solved, precision=highest, preferred_element_type=f32)
    square[0:192, 0:64] = solved
    turned = square[...].T[0:64, 0:192]
    small[:, 0:64] = jnp.dot(turned, weighted, precision=highest, preferred_element_type=f32)
    small[:, 64:256] = turned
    factor[...] = jnp.zeros((128, 384), f32)

    def keep(t, caught):
        value = jnp.concatenate(caught, axis=1)[:, 64:256]
        factor[8 * t : 8 * t + 8, 0:192] = value
        factor[64 + 8 * t : 72 + 8 * t, 192:384] = value

    reduce_block(small, 0, 0, keep)
    rotate = factor[0:64, 0:192]
    across = (((1,), (1,)), ((), ()))
    lifted = lax.dot_general(stiff, rotate, across, precision=highest, preferred_element_type=f32)
    reduced[...] = jnp.dot(rotate, lifted, precision=highest, preferred_element_type=f32)
    both = factor[...]
    for source, out in ((basis, modes), (images, mode_images)):
        for y in range(SIDE // 2):
            value = source[:, :, y * 384 : (y + 1) * 384].reshape(48, 384)
            value = lax.dot_general(value, both, across, precision=highest, preferred_element_type=f32)
            out[:, :, y * 128 : (y + 1) * 128] = value.reshape(3, SIDE, 128)


def exchange(up, down, axis):
    size = lax.axis_size(axis)
    forward = [(i, i + 1) for i in range(size - 1)]
    backward = [(i + 1, i) for i in range(size - 1)]
    return lax.ppermute(up, axis, forward), lax.ppermute(down, axis, backward)


def spread(value, axis):
    size = lax.axis_size(axis)
    return lax.all_to_all(jnp.broadcast_to(value[None], (size,) + value.shape), axis, 0, 0, tiled=True)


def local(basis, offsets, bond_modulus, bulk_modulus, springs, intact):
    slabs = lax.axis_size("slab")
    bands = lax.axis_size("band")
    total_rows = float(3 * SIDE * SIDE * slabs * bands)
    basis = hold(basis)

    with jax.named_scope("halo"):
        up, down, geo = call(
            pack_x,
            [(80, 768)] * 2 + [(8, 256)],
            [pltpu.VMEM((128, 128), f32)] * 2,
            (basis, offsets, bond_modulus, bulk_modulus, springs, intact),
            1000,
            "pack_x",
        )
        left, right = exchange(up, down, "slab")
        rows, mass = call(
            prepare, [(768, NCOL), (NCOL, NCOL)], [], (basis,), 3 * 10**8, "prepare"
        )
        up, down, own = call(
            pack_y, [(96, 1152)] * 2 + [(8, 512)], [], (basis, hold(geo), hold(left), hold(right)), 1000, "pack_y"
        )
        below, above = exchange(up, down, "band")

    with jax.named_scope("stiffness"):
        images, grams = call(
            stiffness,
            [(3, SIDE, SIDE * NCOL), (256, NCOL)],
            [
                pltpu.VMEM((8, 1024), f32),
                pltpu.VMEM((1024, 8), f32),
                pltpu.VMEM((STRIPS, 8, FAR), f32),
                pltpu.VMEM((3, 512, NCOL), f32),
                pltpu.VMEM((3, 1024, NCOL), bf16),
                pltpu.VMEM((3, 1024, NCOL), bf16),
                pltpu.VMEM((1024, NCOL), bf16),
                pltpu.VMEM((1024, NCOL), bf16),
                pltpu.VMEM((3, 256, NCOL), f32),
            ],
            (hold(rows), hold(mass), hold(left), hold(right), hold(own), hold(below), hold(above)),
            2 * 10**9,
            "stiffness",
        )

    with jax.named_scope("sums"):
        part = lax.all_to_all(grams.reshape(slabs, 256 // slabs, NCOL), "slab", 0, 0, tiled=True)
        part = spread(jnp.sum(part, axis=0), "band")
        part = spread(jnp.sum(part, axis=0), "slab")
        grams = part.reshape(256, NCOL)

    with jax.named_scope("rotation"):
        def kernel(*refs):
            rotation(1.0 / total_rows, *refs)

        modes, mode_images, reduced = call(
            kernel,
            [(3, SIDE, SIDE * MODES)] * 2 + [(MODES, MODES)],
            [
                pltpu.VMEM((256, 256), f32),
                pltpu.VMEM((192, 256), f32),
                pltpu.VMEM((64, 256), f32),
                pltpu.VMEM((128, 384), f32),
            ],
            (hold(grams), basis, hold(images)),
            10**9,
            "rotation",
            False,
        )
    return modes, mode_images, reduced


def solution(mesh):
    in_specs = (
        P(None, "slab", "band"),
        P(None, "slab", "band"),
        P("slab", "band"),
        P("slab", "band"),
        P("slab", "band"),
        P("slab", "band", None),
    )
    out_specs = (P(None, "slab", "band"), P(None, "slab", "band"), P())
    return jax.shard_map(local, mesh=mesh, in_specs=in_specs, out_specs=out_specs, check_vma=False)
```

```python
import jax
import jax.numpy as jnp
from jax import lax
from jax.experimental import pallas as pl
from jax.experimental.pallas import tpu as pltpu
from jax.sharding import PartitionSpec as P


MODES = 64
NCOL = 192
SIDE = 16
HALO = 6
GROUP = 32
STRIPS = 12
FAR = 256
highest = lax.Precision.HIGHEST
f32 = jnp.float32
bf16 = jnp.bfloat16

VMEM = pl.BlockSpec(memory_space=pltpu.VMEM)
PARAMS = pltpu.CompilerParams(vmem_limit_bytes=56 * 1024 * 1024)


def hold(value):
    return pltpu.with_memory_space_constraint(value, pltpu.VMEM)


def call(kernel, outs, scratch, args, flops, name, near=True):
    outs = [(o, f32) if isinstance(o[0], int) else o for o in outs]
    size = sum(a.size for a in args)
    return pl.pallas_call(
        kernel,
        out_shape=[(pltpu.VMEM if near else jax.ShapeDtypeStruct)(*o) for o in outs],
        in_specs=[VMEM] * len(args),
        out_specs=[VMEM] * len(outs),
        scratch_shapes=scratch,
        compiler_params=PARAMS,
        cost_estimate=pl.CostEstimate(flops=flops, bytes_accessed=4 * size, transcendentals=0),
        name=name,
    )(*args)


def pack_x(basis, offsets, bond, bulk, springs, intact, up, down, geo, square, table):
    square[...] = jnp.zeros((128, 128), f32)
    for channel in range(3):
        square[16 * channel : 16 * channel + 16, 0:16] = offsets[channel]
    for channel, part in ((3, bond), (4, bulk), (5, springs)):
        square[16 * channel : 16 * channel + 16, 0:16] = part[...]
    table[...] = square[...].T
    for y in range(SIDE):
        for channel in range(6):
            at = 16 * channel
            geo[channel : channel + 1, 16 * y : 16 * y + 16] = table[y : y + 1, at : at + 16]
    lists = intact[...].astype(f32)
    gap = jnp.zeros((1, 4), f32)
    fill = jnp.zeros((1, 3), f32)
    for by in range(2):
        most = lists[0, by : by + 1, 0:6]
        rest = jnp.concatenate([lists[0, by : by + 1, 6:9], fill], axis=1)
        for row, part in ((6, rest), (7, most)):
            pattern = jnp.concatenate([part, gap, part], axis=1)
            pattern = jnp.concatenate([pattern, pattern], axis=1)
            pattern = jnp.concatenate([pattern, pattern], axis=1)
            pattern = jnp.concatenate([pattern, pattern], axis=1)
            geo[row : row + 1, 128 * by : 128 * by + 128] = pattern
    for out, first in ((up, SIDE - HALO), (down, 0)):
        for c in range(3):
            for j in range(4):
                row = j * 18 + c * 6
                out[row : row + 6, :] = basis[c, first : first + 6, j * 768 : (j + 1) * 768]
        out[72:80, :] = jnp.zeros((8, 768), f32)
        out[72:80, 0:256] = geo[...]


def pack_y(basis, geo, left, right, up, down, own):
    own[...] = jnp.zeros((8, 512), f32)
    for y in range(SIDE):
        at = GROUP * y
        own[:, at : at + 16] = geo[:, 16 * y : 16 * y + 16]
        own[:, at + 16 : at + 22] = left[72:80, 16 * y + 10 : 16 * y + 16]
        own[:, at + 22 : at + 28] = right[72:80, 16 * y : 16 * y + 6]
    for out, first in ((up, SIDE - HALO), (down, 0)):
        pieces = ((2, 384, 768, 0), (3, 0, 768, 384)) if first else ((0, 0, 768, 0), (1, 0, 384, 768))
        for c in range(3):
            row = GROUP * c
            out[row : row + 16, :] = basis[c, :, first * NCOL : (first + HALO) * NCOL]
            for j, start, stop, lane in pieces:
                src = j * 18 + c * 6
                width = stop - start
                out[row + 16 : row + 22, lane : lane + width] = left[src : src + 6, start:stop]
                out[row + 22 : row + 28, lane : lane + width] = right[src : src + 6, start:stop]
            out[row + 28 : row + 32, :] = jnp.zeros((4, 1152), f32)
        lanes = slice(first * GROUP, (first + HALO) * GROUP)
        out[28:32, 0:192] = own[0:4, lanes]
        out[60:64, 0:192] = own[4:8, lanes]


def split(value):
    high = value.astype(bf16)
    return high, (value - high.astype(f32)).astype(bf16)


def product(left, right_high, right_low):
    high, low = split(left)
    return (
        jnp.dot(high, right_high, preferred_element_type=f32)
        + jnp.dot(high, right_low, preferred_element_type=f32)
        + jnp.dot(low, right_high, preferred_element_type=f32)
    )


def gram(a, b):
    return lax.dot_general(
        a, b, (((0,), (0,)), ((), ())), precision=highest, preferred_element_type=f32
    )


def prepare(basis, rows, mass):
    for c in range(3):
        for y in range(SIDE):
            row = 256 * c + 16 * y
            rows[row : row + 16, :] = basis[c, :, y * NCOL : (y + 1) * NCOL]
    value = rows[...]
    mass[...] = gram(value, value)


def block_masks(s, table):
    y0 = 2 * s - 4
    lane = lax.broadcasted_iota(jnp.int32, (32, FAR), 1)
    row = lax.broadcasted_iota(jnp.int32, (32, FAR), 0)
    xi = lane & 31
    far_x = jnp.where(xi < 16, 0, jnp.where(xi < 22, -1, 1))
    far_y = ((y0 - 3 + (lane >> 5)) >> 3) - (y0 >> 3)
    home_x = jnp.where(row < 16, 0, jnp.where(row < 22, -1, 1))
    entry = row - jnp.where(row < 16, 0, jnp.where(row < 22, 16, 22))
    entry = jnp.where(entry < 6, entry, -100)
    code = 3 * (far_x - home_x + 1) + far_y + 1
    value = jnp.where(code == entry, table[:, 7:8], 0.0)
    value = value + jnp.where(code == entry + 6, table[:, 6:7], 0.0)
    middle = jnp.sum(value[0:8], axis=0, keepdims=True)
    rest = value[16:32]
    at = lax.broadcasted_iota(jnp.int32, (16, FAR), 0)
    before = jnp.sum(jnp.where(at < 6, rest, 0.0), axis=0, keepdims=True)
    after = jnp.sum(jnp.where(at >= 6, rest, 0.0), axis=0, keepdims=True)
    return middle, before, after


def bonds(far, home):
    vector = [far[j : j + 1, :] - home[:, j : j + 1] for j in range(3)]
    square = vector[0] * vector[0] + vector[1] * vector[1] + vector[2] * vector[2]
    return vector, jnp.maximum(1.0 - square * (1.0 / 9.0), 0.0)


def locate(own, below, above, geo, geo_cols, geo_far, strips):
    geo[...] = jnp.zeros((8, 1024), f32)
    geo[:, 256:768] = own[...]
    for part, lane in ((below, 64), (above, 768)):
        if part is not None:
            geo[0:4, lane : lane + 192] = part[28:32, 0:192]
            geo[4:8, lane : lane + 192] = part[60:64, 0:192]
    lane = lax.broadcasted_iota(jnp.int32, (8, 1024), 1)
    channel = lax.broadcasted_iota(jnp.int32, (8, 1024), 0)
    xi = lane & 31
    at_x = jnp.where(xi < 16, xi, jnp.where(xi < 22, xi - 22, xi - 6))
    at_y = (lane >> 5) - 8
    place = jnp.where(channel == 0, at_x, jnp.where(channel == 1, at_y, 0)).astype(f32)
    placed = geo[...] + place
    geo[...] = placed
    geo_cols[...] = placed.T
    for s in strips:
        start = GROUP * (2 * s + 1)
        geo_far[s] = geo[:, start : start + FAR]


def rows_of(s):
    near = pl.multiple_of(GROUP * (2 * s + 4), 64)
    start = pl.multiple_of(GROUP * (2 * s + 1), 32)
    return near, start


def dilatation(s, geo_cols, geo_far, high, low, shift):
    row = lax.broadcasted_iota(jnp.int32, (64, FAR), 0)
    lane = lax.broadcasted_iota(jnp.int32, (64, FAR), 1)
    home_row = row & 31
    near, start = rows_of(s)
    home = geo_cols[pl.ds(near, 64), :]
    middle, before, after = block_masks(s, home[0:32])
    vector, weight = bonds(geo_far[s], home)
    weight = weight * jnp.where(home_row < 16, middle, jnp.where(home_row < 22, before, after))
    far = pl.ds(pl.multiple_of(start - shift, 32), FAR)
    total = jnp.zeros((64, NCOL), f32)
    for j in range(3):
        matrix = weight * vector[j]
        matrix = jnp.where(lane == row + 96, -jnp.sum(matrix, axis=1, keepdims=True), matrix)
        total = total + product(matrix, high[j, far, :], low[j, far, :])
    return split(total * (home[:, 4:5] * (1.0 / 27.0)))


def own_bonds(s, geo_cols, geo_far):
    row = lax.broadcasted_iota(jnp.int32, (32, FAR), 0)
    lane = lax.broadcasted_iota(jnp.int32, (32, FAR), 1)
    at_self = lane == row + jnp.where(row < 16, 96, 112)
    near, _ = rows_of(s)
    first = geo_cols[pl.ds(near, 32), :]
    second = geo_cols[pl.ds(near + 32, 16), :]
    home = jnp.concatenate([first[0:16], second], axis=0)
    middle, _, _ = block_masks(s, first)
    vector, weight = bonds(geo_far[s], home)
    return home, vector, weight * middle, at_self


def bond_forces(s, tied, geo_far, high, low, shift):
    home, vector, weight, at_self = tied
    coupling = weight * ((home[:, 3:4] + geo_far[s, 3:4, :]) * (1.0 / 18.0))
    spring = home[:, 5:6]
    pairs = {}
    for i in range(3):
        side = coupling * vector[i]
        for j in range(i, 3):
            matrix = side * vector[j]
            total = jnp.sum(matrix, axis=1, keepdims=True)
            if i == j:
                total = total + spring
            pairs[i, j] = pairs[j, i] = jnp.where(at_self, total, -matrix)
    _, start = rows_of(s)
    far = pl.ds(pl.multiple_of(start - shift, 32), FAR)
    image = jnp.zeros((96, NCOL), f32)
    for j in range(3):
        stacked = jnp.concatenate([pairs[i, j] for i in range(3)], axis=0)
        image = image + product(stacked, high[j, far, :], low[j, far, :])
    return image


def dilatation_forces(s, tied, dil_high, dil_low):
    _, vector, weight, at_self = tied
    sides = []
    for i in range(3):
        matrix = weight * vector[i]
        total = jnp.sum(matrix, axis=1, keepdims=True)
        sides.append(-jnp.where(at_self, total, matrix))
    _, start = rows_of(s)
    far = pl.ds(start, FAR)
    return product(jnp.concatenate(sides, axis=0), dil_high[far, :], dil_low[far, :])


def inner(
    rows, left, right, own, high, low, dil_high, dil_low, forces,
    geo, geo_cols, geo_far, field,
):
    locate(own, None, None, geo, geo_cols, geo_far, range(4, 8))
    for c in range(3):
        for y in range(SIDE):
            j, t = divmod(y, 4)
            src = j * 18 + c * 6
            row = GROUP * y
            point = 256 * c + 16 * y
            field[c, row : row + 16, :] = rows[point : point + 16, :]
            field[c, row + 16 : row + 22, :] = left[src : src + 6, t * NCOL : (t + 1) * NCOL]
            field[c, row + 22 : row + 28, :] = right[src : src + 6, t * NCOL : (t + 1) * NCOL]
            field[c, row + 28 : row + 32, :] = jnp.zeros((4, NCOL), f32)
        for y in range(SIDE):
            row = GROUP * y
            parts = split(field[c, row : row + 32, :])
            high[c, row : row + 32, :] = parts[0]
            low[c, row : row + 32, :] = parts[1]

    def middle(s, carry):
        at = pl.ds(pl.multiple_of(64 * (s - 4), 64), 64)
        parts = dilatation(s, geo_cols, geo_far, high, low, 256)
        dil_high[at, :] = parts[0]
        dil_low[at, :] = parts[1]
        tied = own_bonds(s, geo_cols, geo_far)
        image = bond_forces(s, tied, geo_far, high, low, 256)
        at = pl.ds(pl.multiple_of(32 * (s - 4), 32), 32)
        for i in range(3):
            forces[i, at, :] = image[32 * i : 32 * i + 32]
        return carry

    lax.fori_loop(4, 8, middle, 0, unroll=2)


def stiffness(
    rows, mass, own, below, above, high_own, low_own, dil_high_own, dil_low_own, forces,
    result, grams,
    geo, geo_cols, geo_far, high, low, dil_high, dil_low,
):
    locate(own, below, above, geo, geo_cols, geo_far, range(STRIPS))
    for c in range(3):
        high[c, 256:768, :] = high_own[c]
        low[c, 256:768, :] = low_own[c]
        for j in range(HALO):
            for part, first in ((below, 2), (above, 24)):
                row = GROUP * (first + j)
                parts = split(part[GROUP * c : GROUP * (c + 1), j * NCOL : (j + 1) * NCOL])
                high[c, row : row + 32, :] = parts[0]
                low[c, row : row + 32, :] = parts[1]
        for row in (0, 960):
            for ref in (high, low):
                ref[c, row : row + 64, :] = jnp.zeros((64, NCOL), bf16)
    dil_high[384:640, :] = dil_high_own[...]
    dil_low[384:640, :] = dil_low_own[...]

    def ends(i, carry):
        s = i + 4 * (i // 4)
        near, _ = rows_of(s)
        parts = dilatation(s, geo_cols, geo_far, high, low, 0)
        dil_high[pl.ds(near, 64), :] = parts[0]
        dil_low[pl.ds(near, 64), :] = parts[1]
        return carry

    lax.fori_loop(0, 8, ends, 0, unroll=4)

    def images(i, carry):
        tasks = []
        for s, whole in ((4 + i, False), (2 + i + 4 * (i // 2), True)):
            tied = own_bonds(s, geo_cols, geo_far)
            image = dilatation_forces(s, tied, dil_high, dil_low)
            if whole:
                image = image + bond_forces(s, tied, geo_far, high, low, 0)
            else:
                at = pl.ds(pl.multiple_of(32 * (s - 4), 32), 32)
                image = image + jnp.concatenate([forces[k, at, :] for k in range(3)], axis=0)
            tasks.append((s, image))
        for s, image in tasks:
            at = pl.multiple_of(32 * (s - 2), 32)
            for k in range(3):
                result[pl.ds(pl.multiple_of(at + 256 * k, 32), 32), :] = image[32 * k : 32 * k + 32]
        return carry

    lax.fori_loop(0, 4, images, 0, unroll=2)

    stiff = gram(rows[...], result[...])
    at_row = lax.broadcasted_iota(jnp.int32, (NCOL, NCOL), 0)
    at_col = lax.broadcasted_iota(jnp.int32, (NCOL, NCOL), 1)
    grams[0:192, :] = jnp.where(at_row >= at_col, mass[...], stiff)
    diagonal = jnp.sum(jnp.where(at_row == at_col, stiff, 0.0), axis=0, keepdims=True)
    grams[192:200, :] = jnp.broadcast_to(diagonal, (8, NCOL))
    grams[200:256, :] = jnp.zeros((56, NCOL), f32)


def lanes_of(tile, column):
    half = tile[column // 128]
    at = column % 128
    return jnp.broadcast_to(half[:, at : at + 1], (8, 128))


def row_of(value, row):
    return jnp.broadcast_to(value[row : row + 1, :], (8, 128))


def reduce_block(ref, row0, col0, out):
    at = lax.broadcasted_iota(jnp.int32, (8, 128), 0)
    tiles = []
    for q in range(8):
        row = row0 + 8 * q
        tiles.append([ref[row : row + 8, 0:128], ref[row : row + 8, 128:256]])
    pivots = [lanes_of(tiles[0], col0 + j) for j in range(8)]
    for t in range(8):
        first = col0 + 8 * t
        others = [q for q in range(8) if q != t]
        if out is not None:
            others = [q for q in others if q > t]
        columns = {q: [lanes_of(tiles[q], first + i) for i in range(8)] for q in others}
        ahead, following = [], []
        if t < 7:
            ahead = [lanes_of(tiles[t], first + 8 + j) for j in range(8)]
            following = [lanes_of(tiles[t + 1], first + 8 + j) for j in range(8)]
        panel = tiles[t]
        caught = list(panel)
        for i in range(8):
            pivot = row_of(pivots[i], i)
            inverse = 1.0 / pivot
            factor = pivots[i]
            chosen = at == i

            def step(value):
                row = row_of(value, i) * inverse
                return jnp.where(chosen, row, value - factor * row)

            if out is not None:
                root = lax.rsqrt(pivot)
                root = root * (1.5 - 0.5 * pivot * root * root)
                caught = [jnp.where(chosen, row_of(p, i) * root, c) for p, c in zip(panel, caught)]
            pivots = [step(p) if j > i else p for j, p in enumerate(pivots)]
            ahead = [step(p) for p in ahead]
            panel = [step(p) for p in panel]
        tiles[t] = panel
        if out is not None:
            out(t, caught)
        if t < 7:
            pivots = following
            for i in range(8):
                pivots = [
                    p - columns[t + 1][i] * row_of(a, i) for p, a in zip(pivots, ahead)
                ]
        for i in range(8):
            rows = [row_of(p, i) for p in panel]
            for q in others:
                tiles[q] = [v - columns[q][i] * r for v, r in zip(tiles[q], rows)]
    if out is None:
        for q in range(8):
            row = row0 + 8 * q
            ref[row : row + 8, 0:128] = tiles[q][0]
            ref[row : row + 8, 128:256] = tiles[q][1]


def rotation(scale, grams, rows, images, modes, mode_images, reduced, square, work, small, factor):
    packed = grams[0:192, :] * scale
    diagonal = grams[192:193, :] * scale
    square[...] = jnp.zeros((256, 256), f32)
    square[0:192, 0:192] = packed
    flipped = square[...].T[0:192, 0:192]
    at_row = lax.broadcasted_iota(jnp.int32, (NCOL, NCOL), 0)
    at_col = lax.broadcasted_iota(jnp.int32, (NCOL, NCOL), 1)
    mass = jnp.where(at_row >= at_col, packed, flipped)
    stiff = jnp.where(at_row < at_col, packed, jnp.where(at_row > at_col, flipped, diagonal))
    work[:, 0:192] = stiff
    work[:, 192:256] = mass[:, 0:64]
    for block in range(3):
        base = 64 * block
        reduce_block(work, base, base, None)
        reduced_rows = work[base : base + 64, :]
        for other in range(3):
            if other != block:
                part = slice(64 * other, 64 * other + 64)
                work[part, :] = work[part, :] - jnp.dot(
                    work[part, base : base + 64],
                    reduced_rows,
                    precision=highest,
                    preferred_element_type=f32,
                )
    solved = work[:, 192:256]
    weighted = jnp.dot(mass, solved, precision=highest, preferred_element_type=f32)
    square[0:192, 0:64] = solved
    turned = square[...].T[0:64, 0:192]
    small[:, 0:64] = jnp.dot(turned, weighted, precision=highest, preferred_element_type=f32)
    small[:, 64:256] = turned

    def keep(t, caught):
        factor[8 * t : 8 * t + 8, :] = jnp.concatenate(caught, axis=1)[:, 64:256]

    reduce_block(small, 0, 0, keep)
    rotate = factor[...]
    blank = jnp.zeros((64, NCOL), f32)
    even = split(jnp.concatenate([rotate, blank], axis=0))
    odd = split(jnp.concatenate([blank, rotate], axis=0))
    across = (((1,), (1,)), ((), ()))

    def dot(left, right):
        return lax.dot_general(left, right, across, preferred_element_type=f32)

    for source, out in ((rows, modes), (images, mode_images)):
        value = source[...].reshape(24, 2, SIDE, NCOL)
        total = jnp.zeros((384, 128), f32)
        for at, (high, low) in ((0, even), (1, odd)):
            first, second = split(value[:, at].reshape(384, NCOL))
            total = total + dot(first, high) + dot(first, low) + dot(second, high)
        for c in range(3):
            for y in range(SIDE // 2):
                row = 128 * c + 16 * y
                out[c, :, 128 * y : 128 * y + 128] = total[row : row + 16]
    lifted = lax.dot_general(stiff, rotate, across, precision=highest, preferred_element_type=f32)
    reduced[...] = jnp.dot(rotate, lifted, precision=highest, preferred_element_type=f32)


def exchange(up, down, axis):
    size = lax.axis_size(axis)
    forward = [(i, i + 1) for i in range(size - 1)]
    backward = [(i + 1, i) for i in range(size - 1)]
    return lax.ppermute(up, axis, forward), lax.ppermute(down, axis, backward)


def spread(value, axis):
    size = lax.axis_size(axis)
    return lax.all_to_all(jnp.broadcast_to(value[None], (size,) + value.shape), axis, 0, 0, tiled=True)


def local(basis, offsets, bond_modulus, bulk_modulus, springs, intact):
    slabs = lax.axis_size("slab")
    bands = lax.axis_size("band")
    total_rows = float(3 * SIDE * SIDE * slabs * bands)
    basis = hold(basis)

    with jax.named_scope("halo"):
        up, down, geo = call(
            pack_x,
            [(80, 768)] * 2 + [(8, 256)],
            [pltpu.VMEM((128, 128), f32)] * 2,
            (basis, offsets, bond_modulus, bulk_modulus, springs, intact),
            1000,
            "pack_x",
        )
        left, right = exchange(up, down, "slab")
        rows, mass = call(
            prepare, [(768, NCOL), (NCOL, NCOL)], [], (basis,), 3 * 10**8, "prepare"
        )
        up, down, own = call(
            pack_y, [(96, 1152)] * 2 + [(8, 512)], [], (basis, hold(geo), hold(left), hold(right)), 1000, "pack_y"
        )
        below, above = exchange(up, down, "band")

    with jax.named_scope("stiffness"):
        rows, mass, left, right, own = [hold(a) for a in (rows, mass, left, right, own)]
        places = [
            pltpu.VMEM((8, 1024), f32),
            pltpu.VMEM((1024, 8), f32),
            pltpu.VMEM((STRIPS, 8, FAR), f32),
        ]
        middle = call(
            inner,
            [((3, 512, NCOL), bf16)] * 2 + [((256, NCOL), bf16)] * 2 + [((3, 128, NCOL), f32)],
            places + [pltpu.VMEM((3, 512, NCOL), f32)],
            (rows, left, right, own),
            10**9,
            "inner",
        )
        images, grams = call(
            stiffness,
            [(768, NCOL), (256, NCOL)],
            places
            + [pltpu.VMEM((3, 1024, NCOL), bf16)] * 2
            + [pltpu.VMEM((1024, NCOL), bf16)] * 2,
            (rows, mass, own, hold(below), hold(above), *[hold(a) for a in middle]),
            2 * 10**9,
            "stiffness",
        )

    with jax.named_scope("sums"):
        part = lax.all_to_all(grams.reshape(slabs, 256 // slabs, NCOL), "slab", 0, 0, tiled=True)
        part = spread(jnp.sum(part, axis=0), "band")
        part = spread(jnp.sum(part, axis=0), "slab")
        grams = part.reshape(256, NCOL)

    with jax.named_scope("rotation"):
        def kernel(*refs):
            rotation(1.0 / total_rows, *refs)

        modes, mode_images, reduced = call(
            kernel,
            [(3, SIDE, SIDE * MODES)] * 2 + [(MODES, MODES)],
            [
                pltpu.VMEM((256, 256), f32),
                pltpu.VMEM((192, 256), f32),
                pltpu.VMEM((64, 256), f32),
                pltpu.VMEM((64, NCOL), f32),
            ],
            (hold(grams), hold(rows), hold(images)),
            10**9,
            "rotation",
            False,
        )
    return modes, mode_images, reduced


def solution(mesh):
    in_specs = (
        P(None, "slab", "band"),
        P(None, "slab", "band"),
        P("slab", "band"),
        P("slab", "band"),
        P("slab", "band"),
        P("slab", "band", None),
    )
    out_specs = (P(None, "slab", "band"), P(None, "slab", "band"), P())
    return jax.shard_map(local, mesh=mesh, in_specs=in_specs, out_specs=out_specs, check_vma=False)
```

```python
import jax
import jax.numpy as jnp
from jax import lax
from jax.experimental import pallas as pl
from jax.experimental.pallas import tpu as pltpu
from jax.sharding import PartitionSpec as P


MODES = 64
NCOL = 192
SIDE = 16
HALO = 6
GROUP = 32
RING = 28
STRIPS = 12
FAR = 256
highest = lax.Precision.HIGHEST
f32 = jnp.float32
bf16 = jnp.bfloat16

VMEM = pl.BlockSpec(memory_space=pltpu.VMEM)
PARAMS = pltpu.CompilerParams(vmem_limit_bytes=56 * 1024 * 1024)


def hold(value):
    return pltpu.with_memory_space_constraint(value, pltpu.VMEM)


def call(kernel, outs, scratch, args, flops, name, near=True):
    outs = [(o, f32) if isinstance(o[0], int) else o for o in outs]
    size = sum(a.size for a in args)
    return pl.pallas_call(
        kernel,
        out_shape=[(pltpu.VMEM if near else jax.ShapeDtypeStruct)(*o) for o in outs],
        in_specs=[VMEM] * len(args),
        out_specs=[VMEM] * len(outs),
        scratch_shapes=scratch,
        compiler_params=PARAMS,
        cost_estimate=pl.CostEstimate(flops=flops, bytes_accessed=4 * size, transcendentals=0),
        name=name,
    )(*args)


def pack_x(basis, offsets, bond, bulk, springs, intact, up, down, geo, square, table):
    square[...] = jnp.zeros((128, 128), f32)
    for channel in range(3):
        square[16 * channel : 16 * channel + 16, 0:16] = offsets[channel]
    for channel, part in ((3, bond), (4, bulk), (5, springs)):
        square[16 * channel : 16 * channel + 16, 0:16] = part[...]
    table[...] = square[...].T
    for y in range(SIDE):
        for channel in range(6):
            at = 16 * channel
            geo[channel : channel + 1, 16 * y : 16 * y + 16] = table[y : y + 1, at : at + 16]
    lists = intact[...].astype(f32)
    gap = jnp.zeros((1, 4), f32)
    fill = jnp.zeros((1, 3), f32)
    for by in range(2):
        most = lists[0, by : by + 1, 0:6]
        rest = jnp.concatenate([lists[0, by : by + 1, 6:9], fill], axis=1)
        for row, part in ((6, rest), (7, most)):
            pattern = jnp.concatenate([part, gap, part], axis=1)
            pattern = jnp.concatenate([pattern, pattern], axis=1)
            pattern = jnp.concatenate([pattern, pattern], axis=1)
            pattern = jnp.concatenate([pattern, pattern], axis=1)
            geo[row : row + 1, 128 * by : 128 * by + 128] = pattern
    for out, first in ((up, SIDE - HALO), (down, 0)):
        for c in range(3):
            for j in range(8):
                row = j * 18 + c * 6
                out[row : row + 6, :] = basis[c, first : first + 6, j * 384 : (j + 1) * 384]
        out[144:152, 0:256] = geo[...]
        out[144:152, 256:384] = jnp.zeros((8, 128), f32)


def pack_y(basis, geo, left, right, up, down, own):
    own[...] = jnp.zeros((8, 512), f32)
    for y in range(SIDE):
        at = GROUP * y
        own[:, at : at + 16] = geo[:, 16 * y : 16 * y + 16]
        own[:, at + 16 : at + 22] = left[144:152, 16 * y + 10 : 16 * y + 16]
        own[:, at + 22 : at + 28] = right[144:152, 16 * y : 16 * y + 6]
    for out, first in ((up, SIDE - HALO), (down, 0)):
        for c in range(3):
            row = RING * c
            out[row : row + 16, :] = basis[c, :, first * NCOL : (first + HALO) * NCOL]
            for j in range(HALO // 2):
                src = (first // 2 + j) * 18 + c * 6
                lanes = slice(384 * j, 384 * j + 384)
                out[row + 16 : row + 22, lanes] = left[src : src + 6, :]
                out[row + 22 : row + 28, lanes] = right[src : src + 6, :]
        lanes = slice(first * GROUP, (first + HALO) * GROUP)
        out[84:88, :] = jnp.zeros((4, 1152), f32)
        out[84:88, 0:192] = own[0:4, lanes]
        out[84:88, 256:448] = own[4:8, lanes]


def split(value):
    high = value.astype(bf16)
    return high, (value - high.astype(f32)).astype(bf16)


def product(left, right_high, right_low):
    high, low = split(left)
    return (
        jnp.dot(high, right_high, preferred_element_type=f32)
        + jnp.dot(high, right_low, preferred_element_type=f32)
        + jnp.dot(low, right_high, preferred_element_type=f32)
    )


def gram(a, b):
    return lax.dot_general(
        a, b, (((0,), (0,)), ((), ())), precision=highest, preferred_element_type=f32
    )


def prepare(basis, rows, mass):
    for c in range(3):
        for y in range(SIDE):
            row = 256 * c + 16 * y
            rows[row : row + 16, :] = basis[c, :, y * NCOL : (y + 1) * NCOL]
    value = rows[...]
    mass[...] = gram(value, value)


def block_masks(s, table):
    y0 = 2 * s - 4
    lane = lax.broadcasted_iota(jnp.int32, (32, FAR), 1)
    row = lax.broadcasted_iota(jnp.int32, (32, FAR), 0)
    xi = lane & 31
    far_x = jnp.where(xi < 16, 0, jnp.where(xi < 22, -1, 1))
    far_y = ((y0 - 3 + (lane >> 5)) >> 3) - (y0 >> 3)
    home_x = jnp.where(row < 16, 0, jnp.where(row < 22, -1, 1))
    entry = row - jnp.where(row < 16, 0, jnp.where(row < 22, 16, 22))
    entry = jnp.where(entry < 6, entry, -100)
    code = 3 * (far_x - home_x + 1) + far_y + 1
    value = jnp.where(code == entry, table[:, 7:8], 0.0)
    value = value + jnp.where(code == entry + 6, table[:, 6:7], 0.0)
    middle = jnp.sum(value[0:8], axis=0, keepdims=True)
    rest = value[16:32]
    at = lax.broadcasted_iota(jnp.int32, (16, FAR), 0)
    before = jnp.sum(jnp.where(at < 6, rest, 0.0), axis=0, keepdims=True)
    after = jnp.sum(jnp.where(at >= 6, rest, 0.0), axis=0, keepdims=True)
    return middle, before, after


def bonds(far, home):
    vector = [far[j : j + 1, :] - home[:, j : j + 1] for j in range(3)]
    square = vector[0] * vector[0] + vector[1] * vector[1] + vector[2] * vector[2]
    return vector, jnp.maximum(1.0 - square * (1.0 / 9.0), 0.0)


def locate(own, below, above, geo, geo_cols, geo_far, strips):
    geo[...] = jnp.zeros((8, 1024), f32)
    geo[:, 256:768] = own[...]
    for part, lane in ((below, 64), (above, 768)):
        if part is not None:
            geo[0:4, lane : lane + 192] = part[84:88, 0:192]
            geo[4:8, lane : lane + 192] = part[84:88, 256:448]
    lane = lax.broadcasted_iota(jnp.int32, (8, 1024), 1)
    channel = lax.broadcasted_iota(jnp.int32, (8, 1024), 0)
    xi = lane & 31
    at_x = jnp.where(xi < 16, xi, jnp.where(xi < 22, xi - 22, xi - 6))
    at_y = (lane >> 5) - 8
    place = jnp.where(channel == 0, at_x, jnp.where(channel == 1, at_y, 0)).astype(f32)
    placed = geo[...] + place
    geo[...] = placed
    geo_cols[...] = placed.T
    for s in strips:
        start = GROUP * (2 * s + 1)
        geo_far[s] = geo[:, start : start + FAR]


def rows_of(s):
    near = pl.multiple_of(GROUP * (2 * s + 4), 64)
    start = pl.multiple_of(GROUP * (2 * s + 1), 32)
    return near, start


def dilatation(s, geo_cols, geo_far, high, low, shift):
    row = lax.broadcasted_iota(jnp.int32, (64, FAR), 0)
    lane = lax.broadcasted_iota(jnp.int32, (64, FAR), 1)
    home_row = row & 31
    near, start = rows_of(s)
    home = geo_cols[pl.ds(near, 64), :]
    middle, before, after = block_masks(s, home[0:32])
    vector, weight = bonds(geo_far[s], home)
    weight = weight * jnp.where(home_row < 16, middle, jnp.where(home_row < 22, before, after))
    far = pl.ds(pl.multiple_of(start - shift, 32), FAR)
    total = jnp.zeros((64, NCOL), f32)
    for j in range(3):
        matrix = weight * vector[j]
        matrix = jnp.where(lane == row + 96, -jnp.sum(matrix, axis=1, keepdims=True), matrix)
        total = total + product(matrix, high[j, far, :], low[j, far, :])
    return split(total * (home[:, 4:5] * (1.0 / 27.0)))


def own_bonds(s, geo_cols, geo_far):
    row = lax.broadcasted_iota(jnp.int32, (32, FAR), 0)
    lane = lax.broadcasted_iota(jnp.int32, (32, FAR), 1)
    at_self = lane == row + jnp.where(row < 16, 96, 112)
    near, _ = rows_of(s)
    first = geo_cols[pl.ds(near, 32), :]
    second = geo_cols[pl.ds(near + 32, 16), :]
    home = jnp.concatenate([first[0:16], second], axis=0)
    middle, _, _ = block_masks(s, first)
    vector, weight = bonds(geo_far[s], home)
    return home, vector, weight * middle, at_self


def bond_forces(s, tied, geo_far, high, low, shift):
    home, vector, weight, at_self = tied
    coupling = weight * ((home[:, 3:4] + geo_far[s, 3:4, :]) * (1.0 / 18.0))
    spring = home[:, 5:6]
    pairs = {}
    for i in range(3):
        side = coupling * vector[i]
        for j in range(i, 3):
            matrix = side * vector[j]
            total = jnp.sum(matrix, axis=1, keepdims=True)
            if i == j:
                total = total + spring
            pairs[i, j] = pairs[j, i] = jnp.where(at_self, total, -matrix)
    _, start = rows_of(s)
    far = pl.ds(pl.multiple_of(start - shift, 32), FAR)
    image = jnp.zeros((96, NCOL), f32)
    for j in range(3):
        stacked = jnp.concatenate([pairs[i, j] for i in range(3)], axis=0)
        image = image + product(stacked, high[j, far, :], low[j, far, :])
    return image


def dilatation_forces(s, tied, dil_high, dil_low):
    _, vector, weight, at_self = tied
    sides = []
    for i in range(3):
        matrix = weight * vector[i]
        total = jnp.sum(matrix, axis=1, keepdims=True)
        sides.append(-jnp.where(at_self, total, matrix))
    _, start = rows_of(s)
    far = pl.ds(start, FAR)
    return product(jnp.concatenate(sides, axis=0), dil_high[far, :], dil_low[far, :])


def inner(
    rows, left, right, own, high, low, dil_high, dil_low, forces,
    geo, geo_cols, geo_far, field,
):
    locate(own, None, None, geo, geo_cols, geo_far, range(4, 8))
    for c in range(3):
        for y in range(SIDE):
            j, t = divmod(y, 2)
            src = j * 18 + c * 6
            row = GROUP * y
            point = 256 * c + 16 * y
            field[c, row : row + 16, :] = rows[point : point + 16, :]
            field[c, row + 16 : row + 22, :] = left[src : src + 6, t * NCOL : (t + 1) * NCOL]
            field[c, row + 22 : row + 28, :] = right[src : src + 6, t * NCOL : (t + 1) * NCOL]
            field[c, row + 28 : row + 32, :] = jnp.zeros((4, NCOL), f32)
        for y in range(SIDE):
            row = GROUP * y
            parts = split(field[c, row : row + 32, :])
            high[c, row : row + 32, :] = parts[0]
            low[c, row : row + 32, :] = parts[1]

    def middle(s, carry):
        at = pl.ds(pl.multiple_of(64 * (s - 4), 64), 64)
        parts = dilatation(s, geo_cols, geo_far, high, low, 256)
        dil_high[at, :] = parts[0]
        dil_low[at, :] = parts[1]
        tied = own_bonds(s, geo_cols, geo_far)
        image = bond_forces(s, tied, geo_far, high, low, 256)
        at = pl.ds(pl.multiple_of(32 * (s - 4), 32), 32)
        for i in range(3):
            forces[i, at, :] = image[32 * i : 32 * i + 32]
        return carry

    lax.fori_loop(4, 8, middle, 0, unroll=2)


def stiffness(
    rows, mass, own, below, above, high_own, low_own, dil_high_own, dil_low_own, forces,
    result, grams,
    geo, geo_cols, geo_far, high, low, dil_high, dil_low,
):
    locate(own, below, above, geo, geo_cols, geo_far, range(STRIPS))
    for c in range(3):
        high[c, 256:768, :] = high_own[c]
        low[c, 256:768, :] = low_own[c]
        for j in range(HALO):
            for part, first in ((below, 2), (above, 24)):
                row = GROUP * (first + j)
                parts = split(part[RING * c : RING * c + GROUP, j * NCOL : (j + 1) * NCOL])
                high[c, row : row + 32, :] = parts[0]
                low[c, row : row + 32, :] = parts[1]
        for row in (0, 960):
            for ref in (high, low):
                ref[c, row : row + 64, :] = jnp.zeros((64, NCOL), bf16)
    dil_high[384:640, :] = dil_high_own[...]
    dil_low[384:640, :] = dil_low_own[...]

    def ends(i, carry):
        s = i + 4 * (i // 4)
        near, _ = rows_of(s)
        parts = dilatation(s, geo_cols, geo_far, high, low, 0)
        dil_high[pl.ds(near, 64), :] = parts[0]
        dil_low[pl.ds(near, 64), :] = parts[1]
        return carry

    lax.fori_loop(0, 8, ends, 0, unroll=4)

    def images(i, carry):
        tasks = []
        for s, whole in ((4 + i, False), (2 + i + 4 * (i // 2), True)):
            tied = own_bonds(s, geo_cols, geo_far)
            image = dilatation_forces(s, tied, dil_high, dil_low)
            if whole:
                image = image + bond_forces(s, tied, geo_far, high, low, 0)
            else:
                at = pl.ds(pl.multiple_of(32 * (s - 4), 32), 32)
                image = image + jnp.concatenate([forces[k, at, :] for k in range(3)], axis=0)
            tasks.append((s, image))
        for s, image in tasks:
            at = pl.multiple_of(32 * (s - 2), 32)
            for k in range(3):
                result[pl.ds(pl.multiple_of(at + 256 * k, 32), 32), :] = image[32 * k : 32 * k + 32]
        return carry

    lax.fori_loop(0, 4, images, 0, unroll=2)

    stiff = gram(rows[...], result[...])
    at_row = lax.broadcasted_iota(jnp.int32, (NCOL, NCOL), 0)
    at_col = lax.broadcasted_iota(jnp.int32, (NCOL, NCOL), 1)
    packed = jnp.where(at_row >= at_col, mass[...], stiff)
    diagonal = jnp.sum(jnp.where(at_row == at_col, stiff, 0.0), axis=0, keepdims=True)
    grams[0:192, :] = packed[:, 0:128]
    grams[192:288, 0:64] = packed[0:96, 128:192]
    grams[192:288, 64:128] = packed[96:192, 128:192]
    grams[288:320, :] = jnp.zeros((32, 128), f32)
    grams[288:289, :] = diagonal[:, 0:128]
    grams[289:290, 0:64] = diagonal[:, 128:192]


def lanes_of(tile, column):
    half = tile[column // 128 - 2 + len(tile)]
    at = column % 128
    return jnp.broadcast_to(half[:, at : at + 1], (8, 128))


def row_of(value, row):
    return jnp.broadcast_to(value[row : row + 1, :], (8, 128))


def reduce_block(ref, row0, col0, halves, out):
    at = lax.broadcasted_iota(jnp.int32, (8, 128), 0)
    tiles = []
    for q in range(8):
        row = row0 + 8 * q
        tiles.append([ref[row : row + 8, 128 * h : 128 * h + 128] for h in halves])
    pivots = [lanes_of(tiles[0], col0 + j) for j in range(8)]
    for t in range(8):
        first = col0 + 8 * t
        others = [q for q in range(8) if q != t]
        if out is not None:
            others = [q for q in others if q > t]
        columns = {q: [lanes_of(tiles[q], first + i) for i in range(8)] for q in others}
        ahead, following = [], []
        if t < 7:
            ahead = [lanes_of(tiles[t], first + 8 + j) for j in range(8)]
            following = [lanes_of(tiles[t + 1], first + 8 + j) for j in range(8)]
        panel = tiles[t]
        caught = list(panel)
        for i in range(8):
            pivot = row_of(pivots[i], i)
            inverse = 1.0 / pivot
            chosen = at == i
            factor = jnp.where(chosen, -inverse, pivots[i] * inverse)

            def step(value):
                return jnp.where(chosen, 0.0, value) - factor * row_of(value, i)

            if out is not None:
                root = lax.rsqrt(pivot)
                root = root * (1.5 - 0.5 * pivot * root * root)
                caught = [jnp.where(chosen, row_of(p, i) * root, c) for p, c in zip(panel, caught)]
            pivots = [step(p) if j > i else p for j, p in enumerate(pivots)]
            ahead = [step(p) for p in ahead]
            panel = [step(p) for p in panel]
        tiles[t] = panel
        if out is not None:
            out(t, caught)
        if t < 7:
            pivots = following
            for i in range(8):
                pivots = [
                    p - columns[t + 1][i] * row_of(a, i) for p, a in zip(pivots, ahead)
                ]
        for i in range(8):
            rows = [row_of(p, i) for p in panel]
            for q in others:
                tiles[q] = [v - columns[q][i] * r for v, r in zip(tiles[q], rows)]
    if out is None:
        for q in range(8):
            row = row0 + 8 * q
            for h, value in zip(halves, tiles[q]):
                ref[row : row + 8, 128 * h : 128 * h + 128] = value


def rotation(scale, grams, rows, images, modes, mode_images, reduced, square, work, small, factor):
    square[...] = jnp.zeros((256, 256), f32)
    square[0:192, 0:128] = grams[0:192, :] * scale
    square[0:96, 128:192] = grams[192:288, 0:64] * scale
    square[96:192, 128:192] = grams[192:288, 64:128] * scale
    packed = square[0:192, 0:192]
    diagonal = jnp.concatenate([grams[288:289, :], grams[289:290, 0:64]], axis=1) * scale
    flipped = square[...].T[0:192, 0:192]
    at_row = lax.broadcasted_iota(jnp.int32, (NCOL, NCOL), 0)
    at_col = lax.broadcasted_iota(jnp.int32, (NCOL, NCOL), 1)
    mass = jnp.where(at_row >= at_col, packed, flipped)
    stiff = jnp.where(at_row < at_col, packed, jnp.where(at_row > at_col, flipped, diagonal))
    work[:, 0:192] = stiff
    work[:, 192:256] = mass[:, 0:64]
    for block in range(3):
        base = 64 * block
        halves = (1,) if block == 2 else (0, 1)
        lanes = slice(128 * halves[0], 256)
        reduce_block(work, base, base, halves, None)
        rest = [slice(64 * other, 64 * other + 64) for other in range(3) if other != block]
        change = jnp.dot(
            jnp.concatenate([work[part, base : base + 64] for part in rest], axis=0),
            work[base : base + 64, lanes],
            precision=highest,
            preferred_element_type=f32,
        )
        work[rest[0], lanes] = work[rest[0], lanes] - change[0:64]
        work[rest[1], lanes] = work[rest[1], lanes] - change[64:128]
    solved = work[:, 192:256]
    weighted = jnp.dot(mass, solved, precision=highest, preferred_element_type=f32)
    square[0:192, 0:64] = solved
    turned = square[...].T[0:64, 0:192]
    small[:, 0:64] = jnp.dot(turned, weighted, precision=highest, preferred_element_type=f32)
    small[:, 64:256] = turned

    def keep(t, caught):
        factor[8 * t : 8 * t + 8, :] = jnp.concatenate(caught, axis=1)[:, 64:256]

    reduce_block(small, 0, 0, (0, 1), keep)
    rotate = factor[...]
    blank = jnp.zeros((64, NCOL), f32)
    even = split(jnp.concatenate([rotate, blank], axis=0))
    odd = split(jnp.concatenate([blank, rotate], axis=0))
    across = (((1,), (1,)), ((), ()))

    def dot(left, right):
        return lax.dot_general(left, right, across, preferred_element_type=f32)

    for source, out in ((rows, modes), (images, mode_images)):
        value = source[...].reshape(24, 2, SIDE, NCOL)
        total = jnp.zeros((384, 128), f32)
        for at, (high, low) in ((0, even), (1, odd)):
            first, second = split(value[:, at].reshape(384, NCOL))
            total = total + dot(first, high) + dot(first, low) + dot(second, high)
        for c in range(3):
            for y in range(SIDE // 2):
                row = 128 * c + 16 * y
                out[c, :, 128 * y : 128 * y + 128] = total[row : row + 16]
    lifted = lax.dot_general(stiff, rotate, across, precision=highest, preferred_element_type=f32)
    reduced[...] = jnp.dot(rotate, lifted, precision=highest, preferred_element_type=f32)


def exchange(up, down, axis):
    size = lax.axis_size(axis)
    forward = [(i, i + 1) for i in range(size - 1)]
    backward = [(i + 1, i) for i in range(size - 1)]
    return lax.ppermute(up, axis, forward), lax.ppermute(down, axis, backward)


def spread(value, axis):
    size = lax.axis_size(axis)
    return lax.all_to_all(jnp.broadcast_to(value[None], (size,) + value.shape), axis, 0, 0, tiled=True)


def local(basis, offsets, bond_modulus, bulk_modulus, springs, intact):
    slabs = lax.axis_size("slab")
    bands = lax.axis_size("band")
    total_rows = float(3 * SIDE * SIDE * slabs * bands)

    with jax.named_scope("halo"):
        up, down, geo = call(
            pack_x,
            [(152, 384)] * 2 + [(8, 256)],
            [pltpu.VMEM((128, 128), f32)] * 2,
            (basis, offsets, bond_modulus, bulk_modulus, springs, intact),
            1000,
            "pack_x",
        )
        left, right = exchange(up, down, "slab")
        rows, mass = call(
            prepare, [(768, NCOL), (NCOL, NCOL)], [], (hold(basis),), 3 * 10**8, "prepare"
        )
        up, down, own = call(
            pack_y, [(88, 1152)] * 2 + [(8, 512)], [], (hold(basis), hold(geo), hold(left), hold(right)), 1000, "pack_y"
        )
        below, above = exchange(up, down, "band")

    with jax.named_scope("stiffness"):
        rows, mass, left, right, own = [hold(a) for a in (rows, mass, left, right, own)]
        places = [
            pltpu.VMEM((8, 1024), f32),
            pltpu.VMEM((1024, 8), f32),
            pltpu.VMEM((STRIPS, 8, FAR), f32),
        ]
        middle = call(
            inner,
            [((3, 512, NCOL), bf16)] * 2 + [((256, NCOL), bf16)] * 2 + [((3, 128, NCOL), f32)],
            places + [pltpu.VMEM((3, 512, NCOL), f32)],
            (rows, left, right, own),
            10**9,
            "inner",
        )
        images, grams = call(
            stiffness,
            [(768, NCOL), (320, 128)],
            places
            + [pltpu.VMEM((3, 1024, NCOL), bf16)] * 2
            + [pltpu.VMEM((1024, NCOL), bf16)] * 2,
            (rows, mass, own, hold(below), hold(above), *[hold(a) for a in middle]),
            2 * 10**9,
            "stiffness",
        )

    with jax.named_scope("sums"):
        part = lax.all_to_all(grams.reshape(slabs, 1, 40960 // slabs), "slab", 0, 0, tiled=True)
        part = spread(jnp.sum(part, axis=0), "band")
        part = spread(jnp.sum(part, axis=0), "slab")
        grams = part.reshape(320, 128)

    with jax.named_scope("rotation"):
        def kernel(*refs):
            rotation(1.0 / total_rows, *refs)

        modes, mode_images, reduced = call(
            kernel,
            [(3, SIDE, SIDE * MODES)] * 2 + [(MODES, MODES)],
            [
                pltpu.VMEM((256, 256), f32),
                pltpu.VMEM((192, 256), f32),
                pltpu.VMEM((64, 256), f32),
                pltpu.VMEM((64, NCOL), f32),
            ],
            (hold(grams), hold(rows), hold(images)),
            10**9,
            "rotation",
            False,
        )
    return modes, mode_images, reduced


def solution(mesh):
    in_specs = (
        P(None, "slab", "band"),
        P(None, "slab", "band"),
        P("slab", "band"),
        P("slab", "band"),
        P("slab", "band"),
        P("slab", "band", None),
    )
    out_specs = (P(None, "slab", "band"), P(None, "slab", "band"), P())
    return jax.shard_map(local, mesh=mesh, in_specs=in_specs, out_specs=out_specs, check_vma=False)
```

```python
import jax
import jax.numpy as jnp
from jax import lax
from jax.experimental import pallas as pl
from jax.experimental.pallas import tpu as pltpu
from jax.sharding import PartitionSpec as P


MODES = 64
NCOL = 192
SIDE = 16
HALO = 6
GROUP = 32
RING = 28
STRIPS = 12
FAR = 256
f32 = jnp.float32
bf16 = jnp.bfloat16

VMEM = pl.BlockSpec(memory_space=pltpu.VMEM)
PARAMS = pltpu.CompilerParams(vmem_limit_bytes=56 * 1024 * 1024)


def hold(value):
    return pltpu.with_memory_space_constraint(value, pltpu.VMEM)


def call(kernel, outs, scratch, args, flops, name, near=True):
    outs = [(o, f32) if isinstance(o[0], int) else o for o in outs]
    size = sum(a.size for a in args)
    return pl.pallas_call(
        kernel,
        out_shape=[(pltpu.VMEM if near else jax.ShapeDtypeStruct)(*o) for o in outs],
        in_specs=[VMEM] * len(args),
        out_specs=[VMEM] * len(outs),
        scratch_shapes=scratch,
        compiler_params=PARAMS,
        cost_estimate=pl.CostEstimate(flops=flops, bytes_accessed=4 * size, transcendentals=0),
        name=name,
    )(*args)


def pack_x(basis, offsets, bond, bulk, springs, intact, up, down, geo, square, table):
    square[...] = jnp.zeros((128, 128), f32)
    for channel in range(3):
        square[16 * channel : 16 * channel + 16, 0:16] = offsets[channel]
    for channel, part in ((3, bond), (4, bulk), (5, springs)):
        square[16 * channel : 16 * channel + 16, 0:16] = part[...]
    table[...] = square[...].T
    for y in range(SIDE):
        for channel in range(6):
            at = 16 * channel
            geo[channel : channel + 1, 16 * y : 16 * y + 16] = table[y : y + 1, at : at + 16]
    lists = intact[...].astype(f32)
    gap = jnp.zeros((1, 4), f32)
    fill = jnp.zeros((1, 3), f32)
    for by in range(2):
        most = lists[0, by : by + 1, 0:6]
        rest = jnp.concatenate([lists[0, by : by + 1, 6:9], fill], axis=1)
        for row, part in ((6, rest), (7, most)):
            pattern = jnp.concatenate([part, gap, part], axis=1)
            pattern = jnp.concatenate([pattern, pattern], axis=1)
            pattern = jnp.concatenate([pattern, pattern], axis=1)
            pattern = jnp.concatenate([pattern, pattern], axis=1)
            geo[row : row + 1, 128 * by : 128 * by + 128] = pattern
    for out, first in ((up, SIDE - HALO), (down, 0)):
        for c in range(3):
            for j in range(8):
                row = j * 18 + c * 6
                out[row : row + 6, :] = basis[c, first : first + 6, j * 384 : (j + 1) * 384]
        out[144:152, 0:256] = geo[...]
        out[144:152, 256:384] = jnp.zeros((8, 128), f32)


def pack_y(basis, geo, left, right, up, down, own):
    own[...] = jnp.zeros((8, 512), f32)
    for y in range(SIDE):
        at = GROUP * y
        own[:, at : at + 16] = geo[:, 16 * y : 16 * y + 16]
        own[:, at + 16 : at + 22] = left[144:152, 16 * y + 10 : 16 * y + 16]
        own[:, at + 22 : at + 28] = right[144:152, 16 * y : 16 * y + 6]
    for out, first in ((up, SIDE - HALO), (down, 0)):
        for c in range(3):
            row = RING * c
            out[row : row + 16, :] = basis[c, :, first * NCOL : (first + HALO) * NCOL]
            for j in range(HALO // 2):
                src = (first // 2 + j) * 18 + c * 6
                lanes = slice(384 * j, 384 * j + 384)
                out[row + 16 : row + 22, lanes] = left[src : src + 6, :]
                out[row + 22 : row + 28, lanes] = right[src : src + 6, :]
        lanes = slice(first * GROUP, (first + HALO) * GROUP)
        out[84:88, :] = jnp.zeros((4, 1152), f32)
        out[84:88, 0:192] = own[0:4, lanes]
        out[84:88, 256:448] = own[4:8, lanes]


def split(value):
    high = value.astype(bf16)
    return high, (value - high.astype(f32)).astype(bf16)


def product(left, right_high, right_low):
    count = left.shape[0]
    parts = split(left)
    both = jnp.dot(jnp.concatenate(parts, axis=0), right_high, preferred_element_type=f32)
    rest = jnp.dot(parts[0], right_low, preferred_element_type=f32)
    return both[0:count] + both[count:] + rest


def split3(value):
    high, rest = split(value)
    middle, low = split(value - high.astype(f32))
    return high, middle, low


def exact(left, right, across=False):
    if left.dtype == f32:
        left = jnp.concatenate(split3(left), axis=0)
    count = left.shape[0] // 3
    dims = (((1,), (1 if across else 0,)), ((), ()))
    total = None
    for k, part in reversed(list(enumerate(split3(right)))):
        value = lax.dot_general(
            left[0 : (3 - k) * count], part, dims, preferred_element_type=f32
        )
        for m in reversed(range(3 - k)):
            piece = value[m * count : (m + 1) * count]
            total = piece if total is None else total + piece
    return total


def prepare(basis, rows, turned, mass, wide):
    wide[...] = jnp.zeros((768, 256), f32)
    for c in range(3):
        for y in range(SIDE):
            row = 256 * c + 16 * y
            value = basis[c, :, y * NCOL : (y + 1) * NCOL]
            rows[row : row + 16, :] = value
            wide[row : row + 16, 0:NCOL] = value
    parts = split3(wide[...].T[0:NCOL, :])
    for k in range(3):
        turned[k * NCOL : (k + 1) * NCOL, :] = parts[k]
    mass[...] = exact(turned[...], rows[...])


def block_masks(s, table):
    y0 = 2 * s - 4
    lane = lax.broadcasted_iota(jnp.int32, (32, FAR), 1)
    row = lax.broadcasted_iota(jnp.int32, (32, FAR), 0)
    xi = lane & 31
    far_x = jnp.where(xi < 16, 0, jnp.where(xi < 22, -1, 1))
    far_y = ((y0 - 3 + (lane >> 5)) >> 3) - (y0 >> 3)
    home_x = jnp.where(row < 16, 0, jnp.where(row < 22, -1, 1))
    entry = row - jnp.where(row < 16, 0, jnp.where(row < 22, 16, 22))
    entry = jnp.where(entry < 6, entry, -100)
    code = 3 * (far_x - home_x + 1) + far_y + 1
    value = jnp.where(code == entry, table[:, 7:8], 0.0)
    value = value + jnp.where(code == entry + 6, table[:, 6:7], 0.0)
    middle = jnp.sum(value[0:8], axis=0, keepdims=True)
    rest = value[16:32]
    at = lax.broadcasted_iota(jnp.int32, (16, FAR), 0)
    before = jnp.sum(jnp.where(at < 6, rest, 0.0), axis=0, keepdims=True)
    after = jnp.sum(jnp.where(at >= 6, rest, 0.0), axis=0, keepdims=True)
    return middle, before, after


def bonds(far, home):
    vector = [far[j : j + 1, :] - home[:, j : j + 1] for j in range(3)]
    square = vector[0] * vector[0] + vector[1] * vector[1] + vector[2] * vector[2]
    return vector, jnp.maximum(1.0 - square * (1.0 / 9.0), 0.0)


def locate(own, below, above, geo, geo_cols, geo_far, strips):
    geo[...] = jnp.zeros((8, 1024), f32)
    geo[:, 256:768] = own[...]
    for part, lane in ((below, 64), (above, 768)):
        if part is not None:
            geo[0:4, lane : lane + 192] = part[84:88, 0:192]
            geo[4:8, lane : lane + 192] = part[84:88, 256:448]
    lane = lax.broadcasted_iota(jnp.int32, (8, 1024), 1)
    channel = lax.broadcasted_iota(jnp.int32, (8, 1024), 0)
    xi = lane & 31
    at_x = jnp.where(xi < 16, xi, jnp.where(xi < 22, xi - 22, xi - 6))
    at_y = (lane >> 5) - 8
    place = jnp.where(channel == 0, at_x, jnp.where(channel == 1, at_y, 0)).astype(f32)
    placed = geo[...] + place
    geo[...] = placed
    geo_cols[...] = placed.T
    for s in strips:
        start = GROUP * (2 * s + 1)
        geo_far[s] = geo[:, start : start + FAR]


def rows_of(s):
    near = pl.multiple_of(GROUP * (2 * s + 4), 64)
    start = pl.multiple_of(GROUP * (2 * s + 1), 32)
    return near, start


def dilatation(s, geo_cols, geo_far, high, low, shift):
    row = lax.broadcasted_iota(jnp.int32, (64, FAR), 0)
    lane = lax.broadcasted_iota(jnp.int32, (64, FAR), 1)
    home_row = row & 31
    near, start = rows_of(s)
    home = geo_cols[pl.ds(near, 64), :]
    middle, before, after = block_masks(s, home[0:32])
    vector, weight = bonds(geo_far[s], home)
    weight = weight * jnp.where(home_row < 16, middle, jnp.where(home_row < 22, before, after))
    far = pl.ds(pl.multiple_of(start - shift, 32), FAR)
    total = jnp.zeros((64, NCOL), f32)
    for j in range(3):
        matrix = weight * vector[j]
        matrix = jnp.where(lane == row + 96, -jnp.sum(matrix, axis=1, keepdims=True), matrix)
        total = total + product(matrix, high[j, far, :], low[j, far, :])
    return split(total * (home[:, 4:5] * (1.0 / 27.0)))


def own_bonds(s, geo_cols, geo_far):
    row = lax.broadcasted_iota(jnp.int32, (32, FAR), 0)
    lane = lax.broadcasted_iota(jnp.int32, (32, FAR), 1)
    at_self = lane == row + jnp.where(row < 16, 96, 112)
    near, _ = rows_of(s)
    first = geo_cols[pl.ds(near, 32), :]
    second = geo_cols[pl.ds(near + 32, 16), :]
    home = jnp.concatenate([first[0:16], second], axis=0)
    middle, _, _ = block_masks(s, first)
    vector, weight = bonds(geo_far[s], home)
    return home, vector, weight * middle, at_self


def bond_forces(s, tied, geo_far, high, low, shift):
    home, vector, weight, at_self = tied
    coupling = weight * ((home[:, 3:4] + geo_far[s, 3:4, :]) * (1.0 / 18.0))
    spring = home[:, 5:6]
    pairs = {}
    for i in range(3):
        side = coupling * vector[i]
        for j in range(i, 3):
            matrix = side * vector[j]
            total = jnp.sum(matrix, axis=1, keepdims=True)
            if i == j:
                total = total + spring
            pairs[i, j] = pairs[j, i] = jnp.where(at_self, total, -matrix)
    _, start = rows_of(s)
    far = pl.ds(pl.multiple_of(start - shift, 32), FAR)
    image = jnp.zeros((96, NCOL), f32)
    for j in range(3):
        stacked = jnp.concatenate([pairs[i, j] for i in range(3)], axis=0)
        image = image + product(stacked, high[j, far, :], low[j, far, :])
    return image


def dilatation_forces(s, tied, dil_high, dil_low):
    _, vector, weight, at_self = tied
    sides = []
    for i in range(3):
        matrix = weight * vector[i]
        total = jnp.sum(matrix, axis=1, keepdims=True)
        sides.append(-jnp.where(at_self, total, matrix))
    _, start = rows_of(s)
    far = pl.ds(start, FAR)
    return product(jnp.concatenate(sides, axis=0), dil_high[far, :], dil_low[far, :])


def inner(
    rows, left, right, own, high, low, dil_high, dil_low, forces,
    geo, geo_cols, geo_far, field,
):
    locate(own, None, None, geo, geo_cols, geo_far, range(4, 8))
    for c in range(3):
        for y in range(SIDE):
            j, t = divmod(y, 2)
            src = j * 18 + c * 6
            row = GROUP * y
            point = 256 * c + 16 * y
            field[c, row : row + 16, :] = rows[point : point + 16, :]
            field[c, row + 16 : row + 22, :] = left[src : src + 6, t * NCOL : (t + 1) * NCOL]
            field[c, row + 22 : row + 28, :] = right[src : src + 6, t * NCOL : (t + 1) * NCOL]
            field[c, row + 28 : row + 32, :] = jnp.zeros((4, NCOL), f32)
        for y in range(SIDE):
            row = GROUP * y
            parts = split(field[c, row : row + 32, :])
            high[c, row : row + 32, :] = parts[0]
            low[c, row : row + 32, :] = parts[1]

    def middle(s, carry):
        at = pl.ds(pl.multiple_of(64 * (s - 4), 64), 64)
        parts = dilatation(s, geo_cols, geo_far, high, low, 256)
        dil_high[at, :] = parts[0]
        dil_low[at, :] = parts[1]
        tied = own_bonds(s, geo_cols, geo_far)
        image = bond_forces(s, tied, geo_far, high, low, 256)
        at = pl.ds(pl.multiple_of(32 * (s - 4), 32), 32)
        for i in range(3):
            forces[i, at, :] = image[32 * i : 32 * i + 32]
        return carry

    lax.fori_loop(4, 8, middle, 0, unroll=2)


def stiffness(
    turned, mass, own, below, above, high_own, low_own, dil_high_own, dil_low_own, forces,
    result, grams,
    geo, geo_cols, geo_far, high, low, dil_high, dil_low,
):
    locate(own, below, above, geo, geo_cols, geo_far, range(STRIPS))
    for c in range(3):
        high[c, 256:768, :] = high_own[c]
        low[c, 256:768, :] = low_own[c]
        for j in range(HALO):
            for part, first in ((below, 2), (above, 24)):
                row = GROUP * (first + j)
                parts = split(part[RING * c : RING * c + GROUP, j * NCOL : (j + 1) * NCOL])
                high[c, row : row + 32, :] = parts[0]
                low[c, row : row + 32, :] = parts[1]
        for row in (0, 960):
            for ref in (high, low):
                ref[c, row : row + 64, :] = jnp.zeros((64, NCOL), bf16)
    dil_high[384:640, :] = dil_high_own[...]
    dil_low[384:640, :] = dil_low_own[...]

    def ends(i, carry):
        s = i + 4 * (i // 4)
        near, _ = rows_of(s)
        parts = dilatation(s, geo_cols, geo_far, high, low, 0)
        dil_high[pl.ds(near, 64), :] = parts[0]
        dil_low[pl.ds(near, 64), :] = parts[1]
        return carry

    lax.fori_loop(0, 8, ends, 0, unroll=4)

    def images(i, carry):
        tasks = []
        for s, whole in ((4 + i, False), (2 + i + 4 * (i // 2), True)):
            tied = own_bonds(s, geo_cols, geo_far)
            image = dilatation_forces(s, tied, dil_high, dil_low)
            if whole:
                image = image + bond_forces(s, tied, geo_far, high, low, 0)
            else:
                at = pl.ds(pl.multiple_of(32 * (s - 4), 32), 32)
                image = image + jnp.concatenate([forces[k, at, :] for k in range(3)], axis=0)
            tasks.append((s, image))
        for s, image in tasks:
            at = pl.multiple_of(32 * (s - 2), 32)
            for k in range(3):
                result[pl.ds(pl.multiple_of(at + 256 * k, 32), 32), :] = image[32 * k : 32 * k + 32]
        return carry

    lax.fori_loop(0, 4, images, 0, unroll=2)

    stiff = exact(turned[...], result[...])
    at_row = lax.broadcasted_iota(jnp.int32, (NCOL, NCOL), 0)
    at_col = lax.broadcasted_iota(jnp.int32, (NCOL, NCOL), 1)
    packed = jnp.where(at_row >= at_col, mass[...], stiff)
    diagonal = jnp.sum(jnp.where(at_row == at_col, stiff, 0.0), axis=0, keepdims=True)
    grams[0:192, :] = packed[:, 0:128]
    grams[192:288, 0:64] = packed[0:96, 128:192]
    grams[192:288, 64:128] = packed[96:192, 128:192]
    grams[288:320, :] = jnp.zeros((32, 128), f32)
    grams[288:289, :] = diagonal[:, 0:128]
    grams[289:290, 0:64] = diagonal[:, 128:192]


def lanes_of(tile, column):
    half = tile[column // 128 - 2 + len(tile)]
    at = column % 128
    return jnp.broadcast_to(half[:, at : at + 1], (8, 128))


def row_of(value, row):
    return jnp.broadcast_to(value[row : row + 1, :], (8, 128))


def reduce_block(ref, row0, col0, halves, out):
    at = lax.broadcasted_iota(jnp.int32, (8, 128), 0)
    tiles = []
    for q in range(8):
        row = row0 + 8 * q
        tiles.append([ref[row : row + 8, 128 * h : 128 * h + 128] for h in halves])
    pivots = [lanes_of(tiles[0], col0 + j) for j in range(8)]
    for t in range(8):
        first = col0 + 8 * t
        others = [q for q in range(8) if q != t]
        if out is not None:
            others = [q for q in others if q > t]
        columns = {q: [lanes_of(tiles[q], first + i) for i in range(8)] for q in others}
        ahead, following = [], []
        if t < 7:
            ahead = [lanes_of(tiles[t], first + 8 + j) for j in range(8)]
            following = [lanes_of(tiles[t + 1], first + 8 + j) for j in range(8)]
        panel = tiles[t]
        caught = list(panel)
        for i in range(8):
            pivot = row_of(pivots[i], i)
            inverse = 1.0 / pivot
            chosen = at == i
            factor = jnp.where(chosen, -inverse, pivots[i] * inverse)

            def step(value):
                return jnp.where(chosen, 0.0, value) - factor * row_of(value, i)

            if out is not None:
                root = lax.rsqrt(pivot)
                root = root * (1.5 - 0.5 * pivot * root * root)
                caught = [jnp.where(chosen, row_of(p, i) * root, c) for p, c in zip(panel, caught)]
            pivots = [step(p) if j > i else p for j, p in enumerate(pivots)]
            ahead = [step(p) for p in ahead]
            panel = [step(p) for p in panel]
        tiles[t] = panel
        if out is not None:
            out(t, caught)
        if t < 7:
            pivots = following
            for i in range(8):
                pivots = [
                    p - columns[t + 1][i] * row_of(a, i) for p, a in zip(pivots, ahead)
                ]
        for i in range(8):
            rows = [row_of(p, i) for p in panel]
            for q in others:
                tiles[q] = [v - columns[q][i] * r for v, r in zip(tiles[q], rows)]
    if out is None:
        for q in range(8):
            row = row0 + 8 * q
            for h, value in zip(halves, tiles[q]):
                ref[row : row + 8, 128 * h : 128 * h + 128] = value


def rotation(scale, grams, rows, images, modes, mode_images, reduced, square, work, small, factor):
    square[...] = jnp.zeros((256, 256), f32)
    square[0:192, 0:128] = grams[0:192, :] * scale
    square[0:96, 128:192] = grams[192:288, 0:64] * scale
    square[96:192, 128:192] = grams[192:288, 64:128] * scale
    packed = square[0:192, 0:192]
    diagonal = jnp.concatenate([grams[288:289, :], grams[289:290, 0:64]], axis=1) * scale
    flipped = square[...].T[0:192, 0:192]
    at_row = lax.broadcasted_iota(jnp.int32, (NCOL, NCOL), 0)
    at_col = lax.broadcasted_iota(jnp.int32, (NCOL, NCOL), 1)
    mass = jnp.where(at_row >= at_col, packed, flipped)
    stiff = jnp.where(at_row < at_col, packed, jnp.where(at_row > at_col, flipped, diagonal))
    work[:, 0:192] = stiff
    work[:, 192:256] = mass[:, 0:64]
    for block in range(3):
        base = 64 * block
        halves = (1,) if block == 2 else (0, 1)
        lanes = slice(128 * halves[0], 256)
        reduce_block(work, base, base, halves, None)
        rest = [slice(64 * other, 64 * other + 64) for other in range(3) if other != block]
        change = exact(
            jnp.concatenate([work[part, base : base + 64] for part in rest], axis=0),
            work[base : base + 64, lanes],
        )
        work[rest[0], lanes] = work[rest[0], lanes] - change[0:64]
        work[rest[1], lanes] = work[rest[1], lanes] - change[64:128]
    solved = work[:, 192:256]
    weighted = exact(mass, solved)
    square[0:192, 0:64] = solved
    turned = square[...].T[0:64, 0:192]
    small[:, 0:64] = exact(turned, weighted)
    small[:, 64:256] = turned

    def keep(t, caught):
        factor[8 * t : 8 * t + 8, :] = jnp.concatenate(caught, axis=1)[:, 64:256]

    reduce_block(small, 0, 0, (0, 1), keep)
    rotate = factor[...]
    blank = jnp.zeros((64, NCOL), f32)
    even = split(jnp.concatenate([rotate, blank], axis=0))
    odd = split(jnp.concatenate([blank, rotate], axis=0))
    across = (((1,), (1,)), ((), ()))

    def dot(left, right):
        return lax.dot_general(left, right, across, preferred_element_type=f32)

    for source, out in ((rows, modes), (images, mode_images)):
        value = source[...].reshape(24, 2, SIDE, NCOL)
        total = jnp.zeros((384, 128), f32)
        for at, (high, low) in ((0, even), (1, odd)):
            parts = split(value[:, at].reshape(384, NCOL))
            both = dot(jnp.concatenate(parts, axis=0), high)
            total = total + both[0:384] + both[384:] + dot(parts[0], low)
        for c in range(3):
            for y in range(SIDE // 2):
                row = 128 * c + 16 * y
                out[c, :, 128 * y : 128 * y + 128] = total[row : row + 16]
    lifted = exact(stiff, rotate, True)
    reduced[...] = exact(rotate, lifted)


def exchange(up, down, axis):
    size = lax.axis_size(axis)
    forward = [(i, i + 1) for i in range(size - 1)]
    backward = [(i + 1, i) for i in range(size - 1)]
    return lax.ppermute(up, axis, forward), lax.ppermute(down, axis, backward)


def spread(value, axis):
    size = lax.axis_size(axis)
    return lax.all_to_all(jnp.broadcast_to(value[None], (size,) + value.shape), axis, 0, 0, tiled=True)


def local(basis, offsets, bond_modulus, bulk_modulus, springs, intact):
    slabs = lax.axis_size("slab")
    bands = lax.axis_size("band")
    total_rows = float(3 * SIDE * SIDE * slabs * bands)

    with jax.named_scope("halo"):
        up, down, geo = call(
            pack_x,
            [(152, 384)] * 2 + [(8, 256)],
            [pltpu.VMEM((128, 128), f32)] * 2,
            (basis, offsets, bond_modulus, bulk_modulus, springs, intact),
            1000,
            "pack_x",
        )
        left, right = exchange(up, down, "slab")
        rows, turned, mass = call(
            prepare,
            [(768, NCOL), ((3 * NCOL, 768), bf16), (NCOL, NCOL)],
            [pltpu.VMEM((768, 256), f32)],
            (hold(basis),),
            3 * 10**8,
            "prepare",
        )
        up, down, own = call(
            pack_y, [(88, 1152)] * 2 + [(8, 512)], [], (hold(basis), hold(geo), hold(left), hold(right)), 1000, "pack_y"
        )
        below, above = exchange(up, down, "band")

    with jax.named_scope("stiffness"):
        rows, turned, mass, left, right, own = [
            hold(a) for a in (rows, turned, mass, left, right, own)
        ]
        places = [
            pltpu.VMEM((8, 1024), f32),
            pltpu.VMEM((1024, 8), f32),
            pltpu.VMEM((STRIPS, 8, FAR), f32),
        ]
        middle = call(
            inner,
            [((3, 512, NCOL), bf16)] * 2 + [((256, NCOL), bf16)] * 2 + [((3, 128, NCOL), f32)],
            places + [pltpu.VMEM((3, 512, NCOL), f32)],
            (rows, left, right, own),
            10**9,
            "inner",
        )
        images, grams = call(
            stiffness,
            [(768, NCOL), (320, 128)],
            places
            + [pltpu.VMEM((3, 1024, NCOL), bf16)] * 2
            + [pltpu.VMEM((1024, NCOL), bf16)] * 2,
            (turned, mass, own, hold(below), hold(above), *[hold(a) for a in middle]),
            2 * 10**9,
            "stiffness",
        )

    with jax.named_scope("sums"):
        part = lax.all_to_all(grams.reshape(slabs, 1, 40960 // slabs), "slab", 0, 0, tiled=True)
        part = spread(jnp.sum(part, axis=0), "band")
        part = spread(jnp.sum(part, axis=0), "slab")
        grams = part.reshape(320, 128)

    with jax.named_scope("rotation"):
        def kernel(*refs):
            rotation(1.0 / total_rows, *refs)

        modes, mode_images, reduced = call(
            kernel,
            [(3, SIDE, SIDE * MODES)] * 2 + [(MODES, MODES)],
            [
                pltpu.VMEM((256, 256), f32),
                pltpu.VMEM((192, 256), f32),
                pltpu.VMEM((64, 256), f32),
                pltpu.VMEM((64, NCOL), f32),
            ],
            (hold(grams), hold(rows), hold(images)),
            10**9,
            "rotation",
            False,
        )
    return modes, mode_images, reduced


def solution(mesh):
    in_specs = (
        P(None, "slab", "band"),
        P(None, "slab", "band"),
        P("slab", "band"),
        P("slab", "band"),
        P("slab", "band"),
        P("slab", "band", None),
    )
    out_specs = (P(None, "slab", "band"), P(None, "slab", "band"), P())
    return jax.shard_map(local, mesh=mesh, in_specs=in_specs, out_specs=out_specs, check_vma=False)
```

```python
import jax
import jax.numpy as jnp
from jax import lax
from jax.experimental import pallas as pl
from jax.experimental.pallas import tpu as pltpu
from jax.sharding import PartitionSpec as P


MODES = 64
NCOL = 192
SIDE = 16
HALO = 6
GROUP = 32
RING = 28
STRIPS = 12
FAR = 256
f32 = jnp.float32
bf16 = jnp.bfloat16

VMEM = pl.BlockSpec(memory_space=pltpu.VMEM)


def hold(value):
    return pltpu.with_memory_space_constraint(value, pltpu.VMEM)


def call(kernel, outs, scratch, args, flops, name, near=True, room=24):
    outs = [(o, f32) if isinstance(o[0], int) else o for o in outs]
    size = sum(a.size for a in args)
    return pl.pallas_call(
        kernel,
        out_shape=[(pltpu.VMEM if near else jax.ShapeDtypeStruct)(*o) for o in outs],
        in_specs=[VMEM] * len(args),
        out_specs=[VMEM] * len(outs),
        scratch_shapes=scratch,
        compiler_params=pltpu.CompilerParams(vmem_limit_bytes=room * 1024 * 1024),
        cost_estimate=pl.CostEstimate(flops=flops, bytes_accessed=4 * size, transcendentals=0),
        name=name,
    )(*args)


def pack_x(basis, offsets, bond, bulk, springs, intact, up, down, geo, square, table):
    square[...] = jnp.zeros((128, 128), f32)
    for channel in range(3):
        square[16 * channel : 16 * channel + 16, 0:16] = offsets[channel]
    for channel, part in ((3, bond), (4, bulk), (5, springs)):
        square[16 * channel : 16 * channel + 16, 0:16] = part[...]
    table[...] = square[...].T
    for y in range(SIDE):
        for channel in range(6):
            at = 16 * channel
            geo[channel : channel + 1, 16 * y : 16 * y + 16] = table[y : y + 1, at : at + 16]
    lists = intact[...].astype(f32)
    gap = jnp.zeros((1, 4), f32)
    fill = jnp.zeros((1, 3), f32)
    for by in range(2):
        most = lists[0, by : by + 1, 0:6]
        rest = jnp.concatenate([lists[0, by : by + 1, 6:9], fill], axis=1)
        for row, part in ((6, rest), (7, most)):
            pattern = jnp.concatenate([part, gap, part], axis=1)
            pattern = jnp.concatenate([pattern, pattern], axis=1)
            pattern = jnp.concatenate([pattern, pattern], axis=1)
            pattern = jnp.concatenate([pattern, pattern], axis=1)
            geo[row : row + 1, 128 * by : 128 * by + 128] = pattern
    for out, first in ((up, SIDE - HALO), (down, 0)):
        for c in range(3):
            for j in range(8):
                row = j * 18 + c * 6
                out[row : row + 6, :] = basis[c, first : first + 6, j * 384 : (j + 1) * 384]
        out[144:152, 0:256] = geo[...]
        out[144:152, 256:384] = jnp.zeros((8, 128), f32)


def pack_y(basis, geo, left, right, up, down, own):
    own[...] = jnp.zeros((8, 512), f32)
    for y in range(SIDE):
        at = GROUP * y
        own[:, at : at + 16] = geo[:, 16 * y : 16 * y + 16]
        own[:, at + 16 : at + 22] = left[144:152, 16 * y + 10 : 16 * y + 16]
        own[:, at + 22 : at + 28] = right[144:152, 16 * y : 16 * y + 6]
    for out, first in ((up, SIDE - HALO), (down, 0)):
        for c in range(3):
            row = RING * c
            out[row : row + 16, :] = basis[c, :, first * NCOL : (first + HALO) * NCOL]
            for j in range(HALO // 2):
                src = (first // 2 + j) * 18 + c * 6
                lanes = slice(384 * j, 384 * j + 384)
                out[row + 16 : row + 22, lanes] = left[src : src + 6, :]
                out[row + 22 : row + 28, lanes] = right[src : src + 6, :]
        lanes = slice(first * GROUP, (first + HALO) * GROUP)
        out[84:88, :] = jnp.zeros((4, 1152), f32)
        out[84:88, 0:192] = own[0:4, lanes]
        out[84:88, 256:448] = own[4:8, lanes]


def split(value):
    high = value.astype(bf16)
    return high, (value - high.astype(f32)).astype(bf16)


def product(left, right_high, right_low):
    count = left.shape[0]
    parts = split(left)
    both = jnp.dot(jnp.concatenate(parts, axis=0), right_high, preferred_element_type=f32)
    rest = jnp.dot(parts[0], right_low, preferred_element_type=f32)
    return both[0:count] + both[count:] + rest


def split3(value):
    high, rest = split(value)
    middle, low = split(value - high.astype(f32))
    return high, middle, low


def exact(left, right, across=False):
    if left.dtype == f32:
        left = jnp.concatenate(split3(left), axis=0)
    count = left.shape[0] // 3
    dims = (((1,), (1 if across else 0,)), ((), ()))
    total = None
    for k, part in reversed(list(enumerate(split3(right)))):
        value = lax.dot_general(
            left[0 : (3 - k) * count], part, dims, preferred_element_type=f32
        )
        for m in reversed(range(3 - k)):
            piece = value[m * count : (m + 1) * count]
            total = piece if total is None else total + piece
    return total


def prepare(basis, rows, turned, mass, wide):
    wide[...] = jnp.zeros((768, 256), f32)
    for c in range(3):
        for y in range(SIDE):
            row = 256 * c + 16 * y
            value = basis[c, :, y * NCOL : (y + 1) * NCOL]
            rows[row : row + 16, :] = value
            wide[row : row + 16, 0:NCOL] = value
    parts = split3(wide[...].T[0:NCOL, :])
    for k in range(3):
        turned[k * NCOL : (k + 1) * NCOL, :] = parts[k]
    mass[...] = exact(turned[...], rows[...])


def block_masks(s, table):
    y0 = 2 * s - 4
    lane = lax.broadcasted_iota(jnp.int32, (32, FAR), 1)
    row = lax.broadcasted_iota(jnp.int32, (32, FAR), 0)
    xi = lane & 31
    far_x = jnp.where(xi < 16, 0, jnp.where(xi < 22, -1, 1))
    far_y = ((y0 - 3 + (lane >> 5)) >> 3) - (y0 >> 3)
    home_x = jnp.where(row < 16, 0, jnp.where(row < 22, -1, 1))
    entry = row - jnp.where(row < 16, 0, jnp.where(row < 22, 16, 22))
    entry = jnp.where(entry < 6, entry, -100)
    code = 3 * (far_x - home_x + 1) + far_y + 1
    value = jnp.where(code == entry, table[:, 7:8], 0.0)
    value = value + jnp.where(code == entry + 6, table[:, 6:7], 0.0)
    middle = jnp.sum(value[0:8], axis=0, keepdims=True)
    rest = value[16:32]
    at = lax.broadcasted_iota(jnp.int32, (16, FAR), 0)
    before = jnp.sum(jnp.where(at < 6, rest, 0.0), axis=0, keepdims=True)
    after = jnp.sum(jnp.where(at >= 6, rest, 0.0), axis=0, keepdims=True)
    return middle, before, after


def bonds(far, home):
    vector = [far[j : j + 1, :] - home[:, j : j + 1] for j in range(3)]
    square = vector[0] * vector[0] + vector[1] * vector[1] + vector[2] * vector[2]
    return vector, jnp.maximum(1.0 - square * (1.0 / 9.0), 0.0)


def locate(own, below, above, geo, geo_cols, geo_far, strips):
    geo[...] = jnp.zeros((8, 1024), f32)
    geo[:, 256:768] = own[...]
    for part, lane in ((below, 64), (above, 768)):
        if part is not None:
            geo[0:4, lane : lane + 192] = part[84:88, 0:192]
            geo[4:8, lane : lane + 192] = part[84:88, 256:448]
    lane = lax.broadcasted_iota(jnp.int32, (8, 1024), 1)
    channel = lax.broadcasted_iota(jnp.int32, (8, 1024), 0)
    xi = lane & 31
    at_x = jnp.where(xi < 16, xi, jnp.where(xi < 22, xi - 22, xi - 6))
    at_y = (lane >> 5) - 8
    place = jnp.where(channel == 0, at_x, jnp.where(channel == 1, at_y, 0)).astype(f32)
    placed = geo[...] + place
    geo[...] = placed
    geo_cols[...] = placed.T
    for s in strips:
        start = GROUP * (2 * s + 1)
        geo_far[s] = geo[:, start : start + FAR]


def rows_of(s):
    near = pl.multiple_of(GROUP * (2 * s + 4), 64)
    start = pl.multiple_of(GROUP * (2 * s + 1), 32)
    return near, start


def dilatation(s, geo_cols, geo_far, high, low, shift):
    row = lax.broadcasted_iota(jnp.int32, (64, FAR), 0)
    lane = lax.broadcasted_iota(jnp.int32, (64, FAR), 1)
    home_row = row & 31
    near, start = rows_of(s)
    home = geo_cols[pl.ds(near, 64), :]
    middle, before, after = block_masks(s, home[0:32])
    vector, weight = bonds(geo_far[s], home)
    weight = weight * jnp.where(home_row < 16, middle, jnp.where(home_row < 22, before, after))
    far = pl.ds(pl.multiple_of(start - shift, 32), FAR)
    total = jnp.zeros((64, NCOL), f32)
    for j in range(3):
        matrix = weight * vector[j]
        matrix = jnp.where(lane == row + 96, -jnp.sum(matrix, axis=1, keepdims=True), matrix)
        total = total + product(matrix, high[j, far, :], low[j, far, :])
    return split(total * (home[:, 4:5] * (1.0 / 27.0)))


def own_bonds(s, geo_cols, geo_far):
    row = lax.broadcasted_iota(jnp.int32, (32, FAR), 0)
    lane = lax.broadcasted_iota(jnp.int32, (32, FAR), 1)
    at_self = lane == row + jnp.where(row < 16, 96, 112)
    near, _ = rows_of(s)
    first = geo_cols[pl.ds(near, 32), :]
    second = geo_cols[pl.ds(near + 32, 16), :]
    home = jnp.concatenate([first[0:16], second], axis=0)
    middle, _, _ = block_masks(s, first)
    vector, weight = bonds(geo_far[s], home)
    return home, vector, weight * middle, at_self


def bond_forces(s, tied, geo_far, high, low, shift):
    home, vector, weight, at_self = tied
    coupling = weight * ((home[:, 3:4] + geo_far[s, 3:4, :]) * (1.0 / 18.0))
    spring = home[:, 5:6]
    pairs = {}
    for i in range(3):
        side = coupling * vector[i]
        for j in range(i, 3):
            matrix = side * vector[j]
            total = jnp.sum(matrix, axis=1, keepdims=True)
            if i == j:
                total = total + spring
            pairs[i, j] = pairs[j, i] = jnp.where(at_self, total, -matrix)
    _, start = rows_of(s)
    far = pl.ds(pl.multiple_of(start - shift, 32), FAR)
    image = jnp.zeros((96, NCOL), f32)
    for j in range(3):
        stacked = jnp.concatenate([pairs[i, j] for i in range(3)], axis=0)
        image = image + product(stacked, high[j, far, :], low[j, far, :])
    return image


def dilatation_forces(s, tied, dil_high, dil_low):
    _, vector, weight, at_self = tied
    sides = []
    for i in range(3):
        matrix = weight * vector[i]
        total = jnp.sum(matrix, axis=1, keepdims=True)
        sides.append(-jnp.where(at_self, total, matrix))
    _, start = rows_of(s)
    far = pl.ds(start, FAR)
    return product(jnp.concatenate(sides, axis=0), dil_high[far, :], dil_low[far, :])


def inner(
    rows, left, right, own, high, low, dil_high, dil_low, forces,
    geo, geo_cols, geo_far, field,
):
    locate(own, None, None, geo, geo_cols, geo_far, range(4, 8))
    for c in range(3):
        for y in range(SIDE):
            j, t = divmod(y, 2)
            src = j * 18 + c * 6
            row = GROUP * y
            point = 256 * c + 16 * y
            field[c, row : row + 16, :] = rows[point : point + 16, :]
            field[c, row + 16 : row + 22, :] = left[src : src + 6, t * NCOL : (t + 1) * NCOL]
            field[c, row + 22 : row + 28, :] = right[src : src + 6, t * NCOL : (t + 1) * NCOL]
            field[c, row + 28 : row + 32, :] = jnp.zeros((4, NCOL), f32)
        for y in range(SIDE):
            row = GROUP * y
            parts = split(field[c, row : row + 32, :])
            high[c, row : row + 32, :] = parts[0]
            low[c, row : row + 32, :] = parts[1]

    def middle(s, carry):
        at = pl.ds(pl.multiple_of(64 * (s - 4), 64), 64)
        parts = dilatation(s, geo_cols, geo_far, high, low, 256)
        dil_high[at, :] = parts[0]
        dil_low[at, :] = parts[1]
        tied = own_bonds(s, geo_cols, geo_far)
        image = bond_forces(s, tied, geo_far, high, low, 256)
        at = pl.ds(pl.multiple_of(32 * (s - 4), 32), 32)
        for i in range(3):
            forces[i, at, :] = image[32 * i : 32 * i + 32]
        return carry

    lax.fori_loop(4, 8, middle, 0, unroll=2)


def stiffness(
    turned, mass, own, below, above, high_own, low_own, dil_high_own, dil_low_own, forces,
    result, grams,
    geo, geo_cols, geo_far, high, low, dil_high, dil_low,
):
    locate(own, below, above, geo, geo_cols, geo_far, range(STRIPS))
    for c in range(3):
        high[c, 256:768, :] = high_own[c]
        low[c, 256:768, :] = low_own[c]
        for j in range(HALO):
            for part, first in ((below, 2), (above, 24)):
                row = GROUP * (first + j)
                parts = split(part[RING * c : RING * c + GROUP, j * NCOL : (j + 1) * NCOL])
                high[c, row : row + 32, :] = parts[0]
                low[c, row : row + 32, :] = parts[1]
        for row in (0, 960):
            for ref in (high, low):
                ref[c, row : row + 64, :] = jnp.zeros((64, NCOL), bf16)
    dil_high[384:640, :] = dil_high_own[...]
    dil_low[384:640, :] = dil_low_own[...]

    def ends(i, carry):
        s = i + 4 * (i // 4)
        near, _ = rows_of(s)
        parts = dilatation(s, geo_cols, geo_far, high, low, 0)
        dil_high[pl.ds(near, 64), :] = parts[0]
        dil_low[pl.ds(near, 64), :] = parts[1]
        return carry

    lax.fori_loop(0, 8, ends, 0, unroll=4)

    def images(i, carry):
        tasks = []
        for s, whole in ((4 + i, False), (2 + i + 4 * (i // 2), True)):
            tied = own_bonds(s, geo_cols, geo_far)
            image = dilatation_forces(s, tied, dil_high, dil_low)
            if whole:
                image = image + bond_forces(s, tied, geo_far, high, low, 0)
            else:
                at = pl.ds(pl.multiple_of(32 * (s - 4), 32), 32)
                image = image + jnp.concatenate([forces[k, at, :] for k in range(3)], axis=0)
            tasks.append((s, image))
        for s, image in tasks:
            at = pl.multiple_of(32 * (s - 2), 32)
            for k in range(3):
                result[pl.ds(pl.multiple_of(at + 256 * k, 32), 32), :] = image[32 * k : 32 * k + 32]
        return carry

    lax.fori_loop(0, 4, images, 0, unroll=2)

    stiff = exact(turned[...], result[...])
    at_row = lax.broadcasted_iota(jnp.int32, (NCOL, NCOL), 0)
    at_col = lax.broadcasted_iota(jnp.int32, (NCOL, NCOL), 1)
    packed = jnp.where(at_row >= at_col, mass[...], stiff)
    diagonal = jnp.sum(jnp.where(at_row == at_col, stiff, 0.0), axis=0, keepdims=True)
    grams[0:192, :] = packed[:, 0:128]
    grams[192:288, 0:64] = packed[0:96, 128:192]
    grams[192:288, 64:128] = packed[96:192, 128:192]
    grams[288:320, :] = jnp.zeros((32, 128), f32)
    grams[288:289, :] = diagonal[:, 0:128]
    grams[289:290, 0:64] = diagonal[:, 128:192]


def lanes_of(tile, column):
    half = tile[column // 128 - 2 + len(tile)]
    at = column % 128
    return jnp.broadcast_to(half[:, at : at + 1], (8, 128))


def row_of(value, row):
    return jnp.broadcast_to(value[row : row + 1, :], (8, 128))


def reduce_block(ref, row0, col0, halves, out):
    at = lax.broadcasted_iota(jnp.int32, (8, 128), 0)
    tiles = []
    for q in range(8):
        row = row0 + 8 * q
        tiles.append([ref[row : row + 8, 128 * h : 128 * h + 128] for h in halves])
    pivots = [lanes_of(tiles[0], col0 + j) for j in range(8)]
    for t in range(8):
        first = col0 + 8 * t
        others = [q for q in range(8) if q != t]
        if out is not None:
            others = [q for q in others if q > t]
        columns = {q: [lanes_of(tiles[q], first + i) for i in range(8)] for q in others}
        ahead, following = [], []
        if t < 7:
            ahead = [lanes_of(tiles[t], first + 8 + j) for j in range(8)]
            following = [lanes_of(tiles[t + 1], first + 8 + j) for j in range(8)]
        panel = tiles[t]
        caught = list(panel)
        for i in range(8):
            pivot = row_of(pivots[i], i)
            inverse = 1.0 / pivot
            chosen = at == i
            factor = jnp.where(chosen, -inverse, pivots[i] * inverse)

            def step(value):
                return jnp.where(chosen, 0.0, value) - factor * row_of(value, i)

            if out is not None:
                root = lax.rsqrt(pivot)
                root = root * (1.5 - 0.5 * pivot * root * root)
                caught = [jnp.where(chosen, row_of(p, i) * root, c) for p, c in zip(panel, caught)]
            pivots = [step(p) if j > i else p for j, p in enumerate(pivots)]
            ahead = [step(p) for p in ahead]
            panel = [step(p) for p in panel]
        tiles[t] = panel
        if out is not None:
            out(t, caught)
        if t < 7:
            pivots = following
            for i in range(8):
                pivots = [
                    p - columns[t + 1][i] * row_of(a, i) for p, a in zip(pivots, ahead)
                ]
        for i in range(8):
            rows = [row_of(p, i) for p in panel]
            for q in others:
                tiles[q] = [v - columns[q][i] * r for v, r in zip(tiles[q], rows)]
    if out is None:
        for q in range(8):
            row = row0 + 8 * q
            for h, value in zip(halves, tiles[q]):
                ref[row : row + 8, 128 * h : 128 * h + 128] = value


def rotation(scale, grams, rows, images, modes, mode_images, reduced, square, work, small, factor):
    square[...] = jnp.zeros((256, 256), f32)
    square[0:192, 0:128] = grams[0:192, :] * scale
    square[0:96, 128:192] = grams[192:288, 0:64] * scale
    square[96:192, 128:192] = grams[192:288, 64:128] * scale
    packed = square[0:192, 0:192]
    diagonal = jnp.concatenate([grams[288:289, :], grams[289:290, 0:64]], axis=1) * scale
    flipped = square[...].T[0:192, 0:192]
    at_row = lax.broadcasted_iota(jnp.int32, (NCOL, NCOL), 0)
    at_col = lax.broadcasted_iota(jnp.int32, (NCOL, NCOL), 1)
    mass = jnp.where(at_row >= at_col, packed, flipped)
    stiff = jnp.where(at_row < at_col, packed, jnp.where(at_row > at_col, flipped, diagonal))
    work[:, 0:192] = stiff
    work[:, 192:256] = mass[:, 0:64]
    for block in range(3):
        base = 64 * block
        halves = (1,) if block == 2 else (0, 1)
        lanes = slice(128 * halves[0], 256)
        reduce_block(work, base, base, halves, None)
        rest = [slice(64 * other, 64 * other + 64) for other in range(3) if other != block]
        change = exact(
            jnp.concatenate([work[part, base : base + 64] for part in rest], axis=0),
            work[base : base + 64, lanes],
        )
        work[rest[0], lanes] = work[rest[0], lanes] - change[0:64]
        work[rest[1], lanes] = work[rest[1], lanes] - change[64:128]
    solved = work[:, 192:256]
    weighted = exact(mass, solved)
    square[0:192, 0:64] = solved
    turned = square[...].T[0:64, 0:192]
    small[:, 0:64] = exact(turned, weighted)
    small[:, 64:256] = turned

    def keep(t, caught):
        factor[8 * t : 8 * t + 8, :] = jnp.concatenate(caught, axis=1)[:, 64:256]

    reduce_block(small, 0, 0, (0, 1), keep)
    rotate = factor[...]
    blank = jnp.zeros((64, NCOL), f32)
    even = split(jnp.concatenate([rotate, blank], axis=0))
    odd = split(jnp.concatenate([blank, rotate], axis=0))
    across = (((1,), (1,)), ((), ()))

    def dot(left, right):
        return lax.dot_general(left, right, across, preferred_element_type=f32)

    for source, out in ((rows, modes), (images, mode_images)):
        value = source[...].reshape(24, 2, SIDE, NCOL)
        total = jnp.zeros((384, 128), f32)
        for at, (high, low) in ((0, even), (1, odd)):
            parts = split(value[:, at].reshape(384, NCOL))
            both = dot(jnp.concatenate(parts, axis=0), high)
            total = total + both[0:384] + both[384:] + dot(parts[0], low)
        for c in range(3):
            for y in range(SIDE // 2):
                row = 128 * c + 16 * y
                out[c, :, 128 * y : 128 * y + 128] = total[row : row + 16]
    lifted = exact(stiff, rotate, True)
    reduced[...] = exact(rotate, lifted)


def exchange(up, down, axis):
    size = lax.axis_size(axis)
    forward = [(i, i + 1) for i in range(size - 1)]
    backward = [(i + 1, i) for i in range(size - 1)]
    return lax.ppermute(up, axis, forward), lax.ppermute(down, axis, backward)


def spread(value, axis):
    size = lax.axis_size(axis)
    return lax.all_to_all(jnp.broadcast_to(value[None], (size,) + value.shape), axis, 0, 0, tiled=True)


def local(basis, offsets, bond_modulus, bulk_modulus, springs, intact):
    slabs = lax.axis_size("slab")
    bands = lax.axis_size("band")
    total_rows = float(3 * SIDE * SIDE * slabs * bands)

    with jax.named_scope("halo"):
        up, down, geo = call(
            pack_x,
            [(152, 384)] * 2 + [(8, 256)],
            [pltpu.VMEM((128, 128), f32)] * 2,
            (basis, offsets, bond_modulus, bulk_modulus, springs, intact),
            1000,
            "pack_x",
            room=56,
        )
        left, right = exchange(up, down, "slab")
        rows, turned, mass = call(
            prepare,
            [(768, NCOL), ((3 * NCOL, 768), bf16), (NCOL, NCOL)],
            [pltpu.VMEM((768, 256), f32)],
            (hold(basis),),
            3 * 10**8,
            "prepare",
        )
        up, down, own = call(
            pack_y, [(88, 1152)] * 2 + [(8, 512)], [], (hold(basis), hold(geo), hold(left), hold(right)), 1000, "pack_y"
        )
        below, above = exchange(up, down, "band")

    with jax.named_scope("stiffness"):
        rows, turned, mass, left, right, own = [
            hold(a) for a in (rows, turned, mass, left, right, own)
        ]
        places = [
            pltpu.VMEM((8, 1024), f32),
            pltpu.VMEM((1024, 8), f32),
            pltpu.VMEM((STRIPS, 8, FAR), f32),
        ]
        middle = call(
            inner,
            [((3, 512, NCOL), bf16)] * 2 + [((256, NCOL), bf16)] * 2 + [((3, 128, NCOL), f32)],
            places + [pltpu.VMEM((3, 512, NCOL), f32)],
            (rows, left, right, own),
            10**9,
            "inner",
        )
        images, grams = call(
            stiffness,
            [(768, NCOL), (320, 128)],
            places
            + [pltpu.VMEM((3, 1024, NCOL), bf16)] * 2
            + [pltpu.VMEM((1024, NCOL), bf16)] * 2,
            (turned, mass, own, hold(below), hold(above), *[hold(a) for a in middle]),
            2 * 10**9,
            "stiffness",
        )

    with jax.named_scope("sums"):
        part = lax.all_to_all(grams.reshape(slabs, 1, 40960 // slabs), "slab", 0, 0, tiled=True)
        part = spread(jnp.sum(part, axis=0), "band")
        part = spread(jnp.sum(part, axis=0), "slab")
        grams = part.reshape(320, 128)

    with jax.named_scope("rotation"):
        def kernel(*refs):
            rotation(1.0 / total_rows, *refs)

        modes, mode_images, reduced = call(
            kernel,
            [(3, SIDE, SIDE * MODES)] * 2 + [(MODES, MODES)],
            [
                pltpu.VMEM((256, 256), f32),
                pltpu.VMEM((192, 256), f32),
                pltpu.VMEM((64, 256), f32),
                pltpu.VMEM((64, NCOL), f32),
            ],
            (hold(grams), hold(rows), hold(images)),
            10**9,
            "rotation",
            False,
        )
    return modes, mode_images, reduced


def solution(mesh):
    in_specs = (
        P(None, "slab", "band"),
        P(None, "slab", "band"),
        P("slab", "band"),
        P("slab", "band"),
        P("slab", "band"),
        P("slab", "band", None),
    )
    out_specs = (P(None, "slab", "band"), P(None, "slab", "band"), P())
    return jax.shard_map(local, mesh=mesh, in_specs=in_specs, out_specs=out_specs, check_vma=False)
```

```python
import jax
import jax.numpy as jnp
from jax import lax
from jax.experimental import pallas as pl
from jax.experimental.pallas import tpu as pltpu
from jax.sharding import PartitionSpec as P


MODES = 64
NCOL = 192
SIDE = 16
HALO = 6
GROUP = 32
RING = 28
STRIPS = 12
FAR = 256
f32 = jnp.float32
bf16 = jnp.bfloat16

VMEM = pl.BlockSpec(memory_space=pltpu.VMEM)


def hold(value):
    return pltpu.with_memory_space_constraint(value, pltpu.VMEM)


def call(kernel, outs, scratch, args, flops, name, near=True, room=24):
    outs = [(o, f32) if isinstance(o[0], int) else o for o in outs]
    size = sum(a.size for a in args)
    return pl.pallas_call(
        kernel,
        out_shape=[(pltpu.VMEM if near else jax.ShapeDtypeStruct)(*o) for o in outs],
        in_specs=[VMEM] * len(args),
        out_specs=[VMEM] * len(outs),
        scratch_shapes=scratch,
        compiler_params=pltpu.CompilerParams(vmem_limit_bytes=room * 1024 * 1024),
        cost_estimate=pl.CostEstimate(flops=flops, bytes_accessed=4 * size, transcendentals=0),
        name=name,
    )(*args)


def pack_x(basis, offsets, bond, bulk, springs, intact, up, down, geo, square, table):
    square[...] = jnp.zeros((128, 128), f32)
    for channel in range(3):
        square[16 * channel : 16 * channel + 16, 0:16] = offsets[channel]
    for channel, part in ((3, bond), (4, bulk), (5, springs)):
        square[16 * channel : 16 * channel + 16, 0:16] = part[...]
    table[...] = square[...].T
    for y in range(SIDE):
        for channel in range(6):
            at = 16 * channel
            geo[channel : channel + 1, 16 * y : 16 * y + 16] = table[y : y + 1, at : at + 16]
    lists = intact[...].astype(f32)
    gap = jnp.zeros((1, 4), f32)
    fill = jnp.zeros((1, 3), f32)
    for by in range(2):
        most = lists[0, by : by + 1, 0:6]
        rest = jnp.concatenate([lists[0, by : by + 1, 6:9], fill], axis=1)
        for row, part in ((6, rest), (7, most)):
            pattern = jnp.concatenate([part, gap, part], axis=1)
            pattern = jnp.concatenate([pattern, pattern], axis=1)
            pattern = jnp.concatenate([pattern, pattern], axis=1)
            pattern = jnp.concatenate([pattern, pattern], axis=1)
            geo[row : row + 1, 128 * by : 128 * by + 128] = pattern
    for out, first in ((up, SIDE - HALO), (down, 0)):
        for c in range(3):
            for j in range(8):
                row = j * 18 + c * 6
                out[row : row + 6, :] = basis[c, first : first + 6, j * 384 : (j + 1) * 384]
        out[144:152, 0:256] = geo[...]
        out[144:152, 256:384] = jnp.zeros((8, 128), f32)


def pack_y(basis, geo, left, right, up, down, own):
    own[...] = jnp.zeros((8, 512), f32)
    for y in range(SIDE):
        at = GROUP * y
        own[:, at : at + 16] = geo[:, 16 * y : 16 * y + 16]
        own[:, at + 16 : at + 22] = left[144:152, 16 * y + 10 : 16 * y + 16]
        own[:, at + 22 : at + 28] = right[144:152, 16 * y : 16 * y + 6]
    for out, first in ((up, SIDE - HALO), (down, 0)):
        for c in range(3):
            row = RING * c
            out[row : row + 16, :] = basis[c, :, first * NCOL : (first + HALO) * NCOL]
            for j in range(HALO // 2):
                src = (first // 2 + j) * 18 + c * 6
                lanes = slice(384 * j, 384 * j + 384)
                out[row + 16 : row + 22, lanes] = left[src : src + 6, :]
                out[row + 22 : row + 28, lanes] = right[src : src + 6, :]
        lanes = slice(first * GROUP, (first + HALO) * GROUP)
        out[84:88, :] = jnp.zeros((4, 1152), f32)
        out[84:88, 0:192] = own[0:4, lanes]
        out[84:88, 256:448] = own[4:8, lanes]


def split(value):
    high = value.astype(bf16)
    return high, (value - high.astype(f32)).astype(bf16)


def product(left, right_high, right_low):
    count = left.shape[0]
    parts = split(left)
    both = jnp.dot(jnp.concatenate(parts, axis=0), right_high, preferred_element_type=f32)
    rest = jnp.dot(parts[0], right_low, preferred_element_type=f32)
    return both[0:count] + both[count:] + rest


def split3(value):
    high, rest = split(value)
    middle, low = split(value - high.astype(f32))
    return high, middle, low


def exact(left, right, across=False):
    if left.dtype == f32:
        left = jnp.concatenate(split3(left), axis=0)
    count = left.shape[0] // 3
    dims = (((1,), (1 if across else 0,)), ((), ()))
    total = None
    for k, part in reversed(list(enumerate(split3(right)))):
        value = lax.dot_general(
            left[0 : (3 - k) * count], part, dims, preferred_element_type=f32
        )
        for m in reversed(range(3 - k)):
            piece = value[m * count : (m + 1) * count]
            total = piece if total is None else total + piece
    return total


def prepare(basis, rows, turned, mass, wide):
    wide[...] = jnp.zeros((768, 256), f32)
    for c in range(3):
        for y in range(SIDE):
            row = 256 * c + 16 * y
            value = basis[c, :, y * NCOL : (y + 1) * NCOL]
            rows[row : row + 16, :] = value
            wide[row : row + 16, 0:NCOL] = value
    parts = split3(wide[...].T[0:NCOL, :])
    for k in range(3):
        turned[k * NCOL : (k + 1) * NCOL, :] = parts[k]
    mass[...] = exact(turned[...], rows[...])


def block_masks(s, table):
    y0 = 2 * s - 4
    lane = lax.broadcasted_iota(jnp.int32, (32, FAR), 1)
    row = lax.broadcasted_iota(jnp.int32, (32, FAR), 0)
    xi = lane & 31
    far_x = jnp.where(xi < 16, 0, jnp.where(xi < 22, -1, 1))
    far_y = ((y0 - 3 + (lane >> 5)) >> 3) - (y0 >> 3)
    home_x = jnp.where(row < 16, 0, jnp.where(row < 22, -1, 1))
    entry = row - jnp.where(row < 16, 0, jnp.where(row < 22, 16, 22))
    entry = jnp.where(entry < 6, entry, -100)
    code = 3 * (far_x - home_x + 1) + far_y + 1
    value = jnp.where(code == entry, table[:, 7:8], 0.0)
    value = value + jnp.where(code == entry + 6, table[:, 6:7], 0.0)
    middle = jnp.sum(value[0:8], axis=0, keepdims=True)
    rest = value[16:32]
    at = lax.broadcasted_iota(jnp.int32, (16, FAR), 0)
    before = jnp.sum(jnp.where(at < 6, rest, 0.0), axis=0, keepdims=True)
    after = jnp.sum(jnp.where(at >= 6, rest, 0.0), axis=0, keepdims=True)
    return middle, before, after


def bonds(far, home):
    vector = [far[j : j + 1, :] - home[:, j : j + 1] for j in range(3)]
    square = vector[0] * vector[0] + vector[1] * vector[1] + vector[2] * vector[2]
    return vector, jnp.maximum(1.0 - square * (1.0 / 9.0), 0.0)


def locate(own, below, above, geo, geo_cols, geo_far, strips):
    geo[...] = jnp.zeros((8, 1024), f32)
    geo[:, 256:768] = own[...]
    for part, lane in ((below, 64), (above, 768)):
        if part is not None:
            geo[0:4, lane : lane + 192] = part[84:88, 0:192]
            geo[4:8, lane : lane + 192] = part[84:88, 256:448]
    lane = lax.broadcasted_iota(jnp.int32, (8, 1024), 1)
    channel = lax.broadcasted_iota(jnp.int32, (8, 1024), 0)
    xi = lane & 31
    at_x = jnp.where(xi < 16, xi, jnp.where(xi < 22, xi - 22, xi - 6))
    at_y = (lane >> 5) - 8
    place = jnp.where(channel == 0, at_x, jnp.where(channel == 1, at_y, 0)).astype(f32)
    placed = geo[...] + place
    geo[...] = placed
    geo_cols[...] = placed.T
    for s in strips:
        start = GROUP * (2 * s + 1)
        geo_far[s] = geo[:, start : start + FAR]


def rows_of(s):
    near = pl.multiple_of(GROUP * (2 * s + 4), 64)
    start = pl.multiple_of(GROUP * (2 * s + 1), 32)
    return near, start


def dilatation(s, geo_cols, geo_far, high, low, shift):
    row = lax.broadcasted_iota(jnp.int32, (64, FAR), 0)
    lane = lax.broadcasted_iota(jnp.int32, (64, FAR), 1)
    home_row = row & 31
    near, start = rows_of(s)
    home = geo_cols[pl.ds(near, 64), :]
    middle, before, after = block_masks(s, home[0:32])
    vector, weight = bonds(geo_far[s], home)
    weight = weight * jnp.where(home_row < 16, middle, jnp.where(home_row < 22, before, after))
    far = pl.ds(pl.multiple_of(start - shift, 32), FAR)
    total = jnp.zeros((64, NCOL), f32)
    for j in range(3):
        matrix = weight * vector[j]
        matrix = jnp.where(lane == row + 96, -jnp.sum(matrix, axis=1, keepdims=True), matrix)
        total = total + product(matrix, high[j, far, :], low[j, far, :])
    return split(total * (home[:, 4:5] * (1.0 / 27.0)))


def own_bonds(s, geo_cols, geo_far):
    row = lax.broadcasted_iota(jnp.int32, (32, FAR), 0)
    lane = lax.broadcasted_iota(jnp.int32, (32, FAR), 1)
    at_self = lane == row + jnp.where(row < 16, 96, 112)
    near, _ = rows_of(s)
    first = geo_cols[pl.ds(near, 32), :]
    second = geo_cols[pl.ds(near + 32, 16), :]
    home = jnp.concatenate([first[0:16], second], axis=0)
    middle, _, _ = block_masks(s, first)
    vector, weight = bonds(geo_far[s], home)
    return home, vector, weight * middle, at_self


def bond_forces(s, tied, geo_far, high, low, shift):
    home, vector, weight, at_self = tied
    coupling = weight * ((home[:, 3:4] + geo_far[s, 3:4, :]) * (1.0 / 18.0))
    spring = home[:, 5:6]
    pairs = {}
    for i in range(3):
        side = coupling * vector[i]
        for j in range(i, 3):
            matrix = side * vector[j]
            total = jnp.sum(matrix, axis=1, keepdims=True)
            if i == j:
                total = total + spring
            pairs[i, j] = pairs[j, i] = jnp.where(at_self, total, -matrix)
    _, start = rows_of(s)
    far = pl.ds(pl.multiple_of(start - shift, 32), FAR)
    image = jnp.zeros((96, NCOL), f32)
    for j in range(3):
        stacked = jnp.concatenate([pairs[i, j] for i in range(3)], axis=0)
        image = image + product(stacked, high[j, far, :], low[j, far, :])
    return image


def dilatation_forces(s, tied, dil_high, dil_low):
    _, vector, weight, at_self = tied
    sides = []
    for i in range(3):
        matrix = weight * vector[i]
        total = jnp.sum(matrix, axis=1, keepdims=True)
        sides.append(-jnp.where(at_self, total, matrix))
    _, start = rows_of(s)
    far = pl.ds(start, FAR)
    return product(jnp.concatenate(sides, axis=0), dil_high[far, :], dil_low[far, :])


def inner(
    rows, left, right, own, high, low, dil_high, dil_low, forces,
    geo, geo_cols, geo_far, field,
):
    locate(own, None, None, geo, geo_cols, geo_far, range(4, 8))
    for c in range(3):
        for y in range(SIDE):
            j, t = divmod(y, 2)
            src = j * 18 + c * 6
            row = GROUP * y
            point = 256 * c + 16 * y
            field[c, row : row + 16, :] = rows[point : point + 16, :]
            field[c, row + 16 : row + 22, :] = left[src : src + 6, t * NCOL : (t + 1) * NCOL]
            field[c, row + 22 : row + 28, :] = right[src : src + 6, t * NCOL : (t + 1) * NCOL]
            field[c, row + 28 : row + 32, :] = jnp.zeros((4, NCOL), f32)
        for y in range(SIDE):
            row = GROUP * y
            parts = split(field[c, row : row + 32, :])
            high[c, row : row + 32, :] = parts[0]
            low[c, row : row + 32, :] = parts[1]

    def middle(s, carry):
        at = pl.ds(pl.multiple_of(64 * (s - 4), 64), 64)
        parts = dilatation(s, geo_cols, geo_far, high, low, 256)
        dil_high[at, :] = parts[0]
        dil_low[at, :] = parts[1]
        tied = own_bonds(s, geo_cols, geo_far)
        image = bond_forces(s, tied, geo_far, high, low, 256)
        at = pl.ds(pl.multiple_of(32 * (s - 4), 32), 32)
        for i in range(3):
            forces[i, at, :] = image[32 * i : 32 * i + 32]
        return carry

    lax.fori_loop(4, 8, middle, 0, unroll=2)


def stiffness(
    turned, mass, own, below, above, high_own, low_own, dil_high_own, dil_low_own, forces,
    result, grams,
    geo, geo_cols, geo_far, high, low, dil_high, dil_low,
):
    locate(own, below, above, geo, geo_cols, geo_far, range(STRIPS))
    for c in range(3):
        high[c, 256:768, :] = high_own[c]
        low[c, 256:768, :] = low_own[c]
        for j in range(HALO):
            for part, first in ((below, 2), (above, 24)):
                row = GROUP * (first + j)
                parts = split(part[RING * c : RING * c + GROUP, j * NCOL : (j + 1) * NCOL])
                high[c, row : row + 32, :] = parts[0]
                low[c, row : row + 32, :] = parts[1]
        for row in (0, 960):
            for ref in (high, low):
                ref[c, row : row + 64, :] = jnp.zeros((64, NCOL), bf16)
    dil_high[384:640, :] = dil_high_own[...]
    dil_low[384:640, :] = dil_low_own[...]

    def ends(i, carry):
        s = i + 4 * (i // 4)
        near, _ = rows_of(s)
        parts = dilatation(s, geo_cols, geo_far, high, low, 0)
        dil_high[pl.ds(near, 64), :] = parts[0]
        dil_low[pl.ds(near, 64), :] = parts[1]
        return carry

    lax.fori_loop(0, 8, ends, 0, unroll=4)

    def images(i, carry):
        tasks = []
        for s, whole in ((4 + i, False), (2 + i + 4 * (i // 2), True)):
            tied = own_bonds(s, geo_cols, geo_far)
            image = dilatation_forces(s, tied, dil_high, dil_low)
            if whole:
                image = image + bond_forces(s, tied, geo_far, high, low, 0)
            else:
                at = pl.ds(pl.multiple_of(32 * (s - 4), 32), 32)
                image = image + jnp.concatenate([forces[k, at, :] for k in range(3)], axis=0)
            tasks.append((s, image))
        for s, image in tasks:
            at = pl.multiple_of(32 * (s - 2), 32)
            for k in range(3):
                result[pl.ds(pl.multiple_of(at + 256 * k, 32), 32), :] = image[32 * k : 32 * k + 32]
        return carry

    lax.fori_loop(0, 4, images, 0, unroll=2)

    stiff = exact(turned[...], result[...])
    at_row = lax.broadcasted_iota(jnp.int32, (NCOL, NCOL), 0)
    at_col = lax.broadcasted_iota(jnp.int32, (NCOL, NCOL), 1)
    packed = jnp.where(at_row >= at_col, mass[...], stiff)
    diagonal = jnp.sum(jnp.where(at_row == at_col, stiff, 0.0), axis=0, keepdims=True)
    grams[0:192, :] = packed[:, 0:128]
    grams[192:288, 0:64] = packed[0:96, 128:192]
    grams[192:288, 64:128] = packed[96:192, 128:192]
    grams[288:320, :] = jnp.zeros((32, 128), f32)
    grams[288:289, :] = diagonal[:, 0:128]
    grams[289:290, 0:64] = diagonal[:, 128:192]


def lanes_of(tile, column):
    half = tile[column // 128 - 2 + len(tile)]
    at = column % 128
    return jnp.broadcast_to(half[:, at : at + 1], (8, 128))


def row_of(value, row):
    return jnp.broadcast_to(value[row : row + 1, :], (8, 128))


def reduce_block(ref, row0, col0, halves, out):
    at = lax.broadcasted_iota(jnp.int32, (8, 128), 0)
    tiles = []
    for q in range(8):
        row = row0 + 8 * q
        tiles.append([ref[row : row + 8, 128 * h : 128 * h + 128] for h in halves])
    pivots = [lanes_of(tiles[0], col0 + j) for j in range(8)]
    for t in range(8):
        first = col0 + 8 * t
        others = [q for q in range(8) if q != t]
        if out is not None:
            others = [q for q in others if q > t]
        columns = {q: [lanes_of(tiles[q], first + i) for i in range(8)] for q in others}
        ahead, following = [], []
        if t < 7:
            ahead = [lanes_of(tiles[t], first + 8 + j) for j in range(8)]
            following = [lanes_of(tiles[t + 1], first + 8 + j) for j in range(8)]
        panel = tiles[t]
        caught = list(panel)
        for i in range(8):
            pivot = row_of(pivots[i], i)
            inverse = 1.0 / pivot
            chosen = at == i
            factor = jnp.where(chosen, -1.0, pivots[i]) * inverse

            def step(value):
                return jnp.where(chosen, 0.0, value) - factor * row_of(value, i)

            if out is not None:
                root = lax.rsqrt(pivot)
                root = root * (1.5 - 0.5 * pivot * root * root)
                caught = [jnp.where(chosen, row_of(p, i) * root, c) for p, c in zip(panel, caught)]
            pivots = [step(p) if j > i else p for j, p in enumerate(pivots)]
            ahead = [step(p) for p in ahead]
            panel = [step(p) for p in panel]
        tiles[t] = panel
        if out is not None:
            out(t, caught)
        if t < 7:
            pivots = following
            for i in range(8):
                pivots = [
                    p - columns[t + 1][i] * row_of(a, i) for p, a in zip(pivots, ahead)
                ]
        for i in range(8):
            rows = [row_of(p, i) for p in panel]
            for q in others:
                tiles[q] = [v - columns[q][i] * r for v, r in zip(tiles[q], rows)]
    if out is None:
        for q in range(8):
            row = row0 + 8 * q
            for h, value in zip(halves, tiles[q]):
                ref[row : row + 8, 128 * h : 128 * h + 128] = value


def rotation(
    scale, grams, rows, images, modes, mode_images, reduced, square, work, small, factor, moved,
):
    square[...] = jnp.zeros((256, 256), f32)
    square[0:192, 0:128] = grams[0:192, :] * scale
    square[0:96, 128:192] = grams[192:288, 0:64] * scale
    square[96:192, 128:192] = grams[192:288, 64:128] * scale
    packed = square[0:192, 0:192]
    diagonal = jnp.concatenate([grams[288:289, :], grams[289:290, 0:64]], axis=1) * scale
    flipped = square[...].T[0:192, 0:192]
    at_row = lax.broadcasted_iota(jnp.int32, (NCOL, NCOL), 0)
    at_col = lax.broadcasted_iota(jnp.int32, (NCOL, NCOL), 1)
    mass = jnp.where(at_row >= at_col, packed, flipped)
    stiff = jnp.where(at_row < at_col, packed, jnp.where(at_row > at_col, flipped, diagonal))
    work[:, 0:192] = stiff
    work[:, 192:256] = mass[:, 0:64]
    for block in range(3):
        base = 64 * block
        halves = (1,) if block == 2 else (0, 1)
        lanes = slice(128 * halves[0], 256)
        reduce_block(work, base, base, halves, None)
        rest = [slice(64 * other, 64 * other + 64) for other in range(3) if other != block]
        change = exact(
            jnp.concatenate([work[part, base : base + 64] for part in rest], axis=0),
            work[base : base + 64, lanes],
        )
        work[rest[0], lanes] = work[rest[0], lanes] - change[0:64]
        work[rest[1], lanes] = work[rest[1], lanes] - change[64:128]
    solved = work[:, 192:256]
    weighted = exact(mass, solved)
    square[0:192, 0:64] = solved
    turned = square[...].T[0:64, 0:192]
    small[:, 0:64] = exact(turned, weighted)
    at_row = lax.broadcasted_iota(jnp.int32, (64, 64), 0)
    at_col = lax.broadcasted_iota(jnp.int32, (64, 64), 1)
    small[:, 64:128] = jnp.where(at_row == at_col, 1.0, 0.0)
    energy = exact(turned, exact(stiff, solved))
    for k, source in enumerate((rows, images)):
        value = source[...].reshape(24, 2, SIDE, NCOL)
        value = jnp.concatenate([value[:, h].reshape(384, NCOL) for h in range(2)], axis=0)
        value = exact(value, solved)
        parts = split(jnp.concatenate([value[0:384], value[384:768]], axis=1))
        moved[k, 0:384, :] = parts[0]
        moved[k, 384:768, :] = parts[1]
    upper = lax.broadcasted_iota(jnp.int32, (8, 128), 1) < 64

    def keep(t, caught):
        value = caught[0]
        factor[8 * t : 8 * t + 8, :] = jnp.where(upper, pltpu.roll(value, 64, 1), 0.0)
        factor[64 + 8 * t : 72 + 8 * t, :] = jnp.where(upper, 0.0, value)

    reduce_block(small, 0, 0, (0,), keep)
    high, low = split(factor[...])
    across = (((1,), (1,)), ((), ()))

    def dot(left, right):
        return lax.dot_general(left, right, across, preferred_element_type=f32)

    for k, out in enumerate((modes, mode_images)):
        both = dot(moved[k], high)
        total = both[0:384] + both[384:] + dot(moved[k, 0:384], low)
        for c in range(3):
            for y in range(SIDE // 2):
                row = 128 * c + 16 * y
                out[c, :, 128 * y : 128 * y + 128] = total[row : row + 16]
    inverse = factor[0:64, 0:64]
    reduced[...] = exact(exact(inverse, energy), inverse, True)


def exchange(up, down, axis):
    size = lax.axis_size(axis)
    forward = [(i, i + 1) for i in range(size - 1)]
    backward = [(i + 1, i) for i in range(size - 1)]
    return lax.ppermute(up, axis, forward), lax.ppermute(down, axis, backward)


def spread(value, axis):
    size = lax.axis_size(axis)
    return lax.all_to_all(jnp.broadcast_to(value[None], (size,) + value.shape), axis, 0, 0, tiled=True)


def local(basis, offsets, bond_modulus, bulk_modulus, springs, intact):
    slabs = lax.axis_size("slab")
    bands = lax.axis_size("band")
    total_rows = float(3 * SIDE * SIDE * slabs * bands)

    with jax.named_scope("halo"):
        up, down, geo = call(
            pack_x,
            [(152, 384)] * 2 + [(8, 256)],
            [pltpu.VMEM((128, 128), f32)] * 2,
            (basis, offsets, bond_modulus, bulk_modulus, springs, intact),
            1000,
            "pack_x",
            room=56,
        )
        left, right = exchange(up, down, "slab")
        rows, turned, mass = call(
            prepare,
            [(768, NCOL), ((3 * NCOL, 768), bf16), (NCOL, NCOL)],
            [pltpu.VMEM((768, 256), f32)],
            (hold(basis),),
            3 * 10**8,
            "prepare",
        )
        up, down, own = call(
            pack_y, [(88, 1152)] * 2 + [(8, 512)], [], (hold(basis), hold(geo), hold(left), hold(right)), 1000, "pack_y"
        )
        below, above = exchange(up, down, "band")

    with jax.named_scope("stiffness"):
        rows, turned, mass, left, right, own = [
            hold(a) for a in (rows, turned, mass, left, right, own)
        ]
        places = [
            pltpu.VMEM((8, 1024), f32),
            pltpu.VMEM((1024, 8), f32),
            pltpu.VMEM((STRIPS, 8, FAR), f32),
        ]
        middle = call(
            inner,
            [((3, 512, NCOL), bf16)] * 2 + [((256, NCOL), bf16)] * 2 + [((3, 128, NCOL), f32)],
            places + [pltpu.VMEM((3, 512, NCOL), f32)],
            (rows, left, right, own),
            10**9,
            "inner",
        )
        images, grams = call(
            stiffness,
            [(768, NCOL), (320, 128)],
            places
            + [pltpu.VMEM((3, 1024, NCOL), bf16)] * 2
            + [pltpu.VMEM((1024, NCOL), bf16)] * 2,
            (turned, mass, own, hold(below), hold(above), *[hold(a) for a in middle]),
            2 * 10**9,
            "stiffness",
        )

    with jax.named_scope("sums"):
        part = lax.all_to_all(grams.reshape(slabs, 1, 40960 // slabs), "slab", 0, 0, tiled=True)
        part = spread(jnp.sum(part, axis=0), "band")
        part = spread(jnp.sum(part, axis=0), "slab")
        grams = part.reshape(320, 128)

    with jax.named_scope("rotation"):
        def kernel(*refs):
            rotation(1.0 / total_rows, *refs)

        modes, mode_images, reduced = call(
            kernel,
            [(3, SIDE, SIDE * MODES)] * 2 + [(MODES, MODES)],
            [
                pltpu.VMEM((256, 256), f32),
                pltpu.VMEM((192, 256), f32),
                pltpu.VMEM((64, 128), f32),
                pltpu.VMEM((128, 128), f32),
                pltpu.VMEM((2, 768, 128), bf16),
            ],
            (hold(grams), hold(rows), hold(images)),
            10**9,
            "rotation",
            False,
        )
    return modes, mode_images, reduced


def solution(mesh):
    in_specs = (
        P(None, "slab", "band"),
        P(None, "slab", "band"),
        P("slab", "band"),
        P("slab", "band"),
        P("slab", "band"),
        P("slab", "band", None),
    )
    out_specs = (P(None, "slab", "band"), P(None, "slab", "band"), P())
    return jax.shard_map(local, mesh=mesh, in_specs=in_specs, out_specs=out_specs, check_vma=False)
```

```python
import jax
import jax.numpy as jnp
from jax import lax
from jax.experimental import pallas as pl
from jax.experimental.pallas import tpu as pltpu
from jax.sharding import PartitionSpec as P


MODES = 64
NCOL = 192
SIDE = 16
HALO = 6
GROUP = 32
RING = 28
STRIPS = 12
FAR = 256
f32 = jnp.float32
bf16 = jnp.bfloat16

VMEM = pl.BlockSpec(memory_space=pltpu.VMEM)


def hold(value):
    return pltpu.with_memory_space_constraint(value, pltpu.VMEM)


def call(kernel, outs, scratch, args, flops, name, near=True, room=24):
    outs = [(o, f32) if isinstance(o[0], int) else o for o in outs]
    size = sum(a.size for a in args)
    return pl.pallas_call(
        kernel,
        out_shape=[(pltpu.VMEM if near else jax.ShapeDtypeStruct)(*o) for o in outs],
        in_specs=[VMEM] * len(args),
        out_specs=[VMEM] * len(outs),
        scratch_shapes=scratch,
        compiler_params=pltpu.CompilerParams(vmem_limit_bytes=room * 1024 * 1024),
        cost_estimate=pl.CostEstimate(flops=flops, bytes_accessed=4 * size, transcendentals=0),
        name=name,
    )(*args)


def pack_x(basis, offsets, bond, bulk, springs, intact, up, down, geo, square, table):
    square[...] = jnp.zeros((128, 128), f32)
    for channel in range(3):
        square[16 * channel : 16 * channel + 16, 0:16] = offsets[channel]
    for channel, part in ((3, bond), (4, bulk), (5, springs)):
        square[16 * channel : 16 * channel + 16, 0:16] = part[...]
    table[...] = square[...].T
    for y in range(SIDE):
        for channel in range(6):
            at = 16 * channel
            geo[channel : channel + 1, 16 * y : 16 * y + 16] = table[y : y + 1, at : at + 16]
    lists = intact[...].astype(f32)
    gap = jnp.zeros((1, 4), f32)
    fill = jnp.zeros((1, 3), f32)
    for by in range(2):
        most = lists[0, by : by + 1, 0:6]
        rest = jnp.concatenate([lists[0, by : by + 1, 6:9], fill], axis=1)
        for row, part in ((6, rest), (7, most)):
            pattern = jnp.concatenate([part, gap, part], axis=1)
            pattern = jnp.concatenate([pattern, pattern], axis=1)
            pattern = jnp.concatenate([pattern, pattern], axis=1)
            pattern = jnp.concatenate([pattern, pattern], axis=1)
            geo[row : row + 1, 128 * by : 128 * by + 128] = pattern
    for out, first in ((up, SIDE - HALO), (down, 0)):
        for c in range(3):
            for j in range(8):
                row = j * 18 + c * 6
                out[row : row + 6, :] = basis[c, first : first + 6, j * 384 : (j + 1) * 384]
        out[144:152, 0:256] = geo[...]
        out[144:152, 256:384] = jnp.zeros((8, 128), f32)


def pack_y(basis, geo, left, right, up, down, own):
    own[...] = jnp.zeros((8, 512), f32)
    for y in range(SIDE):
        at = GROUP * y
        own[:, at : at + 16] = geo[:, 16 * y : 16 * y + 16]
        own[:, at + 16 : at + 22] = left[144:152, 16 * y + 10 : 16 * y + 16]
        own[:, at + 22 : at + 28] = right[144:152, 16 * y : 16 * y + 6]
    for out, first in ((up, SIDE - HALO), (down, 0)):
        for c in range(3):
            row = RING * c
            out[row : row + 16, :] = basis[c, :, first * NCOL : (first + HALO) * NCOL]
            for j in range(HALO // 2):
                src = (first // 2 + j) * 18 + c * 6
                lanes = slice(384 * j, 384 * j + 384)
                out[row + 16 : row + 22, lanes] = left[src : src + 6, :]
                out[row + 22 : row + 28, lanes] = right[src : src + 6, :]
        lanes = slice(first * GROUP, (first + HALO) * GROUP)
        out[84:88, :] = jnp.zeros((4, 1152), f32)
        out[84:88, 0:192] = own[0:4, lanes]
        out[84:88, 256:448] = own[4:8, lanes]


def split(value):
    high = value.astype(bf16)
    return high, (value - high.astype(f32)).astype(bf16)


def product(left, right_high, right_low):
    count = left.shape[0]
    parts = split(left)
    both = jnp.dot(jnp.concatenate(parts, axis=0), right_high, preferred_element_type=f32)
    rest = jnp.dot(parts[0], right_low, preferred_element_type=f32)
    return both[0:count] + both[count:] + rest


def split3(value):
    high, rest = split(value)
    middle, low = split(value - high.astype(f32))
    return high, middle, low


def exact(left, right, across=False):
    if left.dtype == f32:
        left = jnp.concatenate(split3(left), axis=0)
    count = left.shape[0] // 3
    dims = (((1,), (1 if across else 0,)), ((), ()))
    total = None
    for k, part in reversed(list(enumerate(split3(right)))):
        value = lax.dot_general(
            left[0 : (3 - k) * count], part, dims, preferred_element_type=f32
        )
        for m in reversed(range(3 - k)):
            piece = value[m * count : (m + 1) * count]
            total = piece if total is None else total + piece
    return total


def prepare(basis, rows, turned, mass, wide):
    wide[...] = jnp.zeros((768, 256), f32)
    for c in range(3):
        for y in range(SIDE):
            row = 256 * c + 16 * y
            value = basis[c, :, y * NCOL : (y + 1) * NCOL]
            rows[row : row + 16, :] = value
            wide[row : row + 16, 0:NCOL] = value
    parts = split3(wide[...].T[0:NCOL, :])
    for k in range(3):
        turned[k * NCOL : (k + 1) * NCOL, :] = parts[k]
    mass[...] = exact(turned[...], rows[...])


def block_masks(s, table):
    y0 = 2 * s - 4
    lane = lax.broadcasted_iota(jnp.int32, (32, FAR), 1)
    row = lax.broadcasted_iota(jnp.int32, (32, FAR), 0)
    xi = lane & 31
    far_x = jnp.where(xi < 16, 0, jnp.where(xi < 22, -1, 1))
    far_y = ((y0 - 3 + (lane >> 5)) >> 3) - (y0 >> 3)
    home_x = jnp.where(row < 16, 0, jnp.where(row < 22, -1, 1))
    entry = row - jnp.where(row < 16, 0, jnp.where(row < 22, 16, 22))
    entry = jnp.where(entry < 6, entry, -100)
    code = 3 * (far_x - home_x + 1) + far_y + 1
    value = jnp.where(code == entry, table[:, 7:8], 0.0)
    value = value + jnp.where(code == entry + 6, table[:, 6:7], 0.0)
    middle = jnp.sum(value[0:8], axis=0, keepdims=True)
    rest = value[16:32]
    at = lax.broadcasted_iota(jnp.int32, (16, FAR), 0)
    before = jnp.sum(jnp.where(at < 6, rest, 0.0), axis=0, keepdims=True)
    after = jnp.sum(jnp.where(at >= 6, rest, 0.0), axis=0, keepdims=True)
    return middle, before, after


def bonds(far, home):
    vector = [far[j : j + 1, :] - home[:, j : j + 1] for j in range(3)]
    square = vector[0] * vector[0] + vector[1] * vector[1] + vector[2] * vector[2]
    return vector, jnp.maximum(1.0 - square * (1.0 / 9.0), 0.0)


def locate(own, below, above, geo, geo_cols, geo_far, strips):
    geo[...] = jnp.zeros((8, 1024), f32)
    geo[:, 256:768] = own[...]
    for part, lane in ((below, 64), (above, 768)):
        if part is not None:
            geo[0:4, lane : lane + 192] = part[84:88, 0:192]
            geo[4:8, lane : lane + 192] = part[84:88, 256:448]
    lane = lax.broadcasted_iota(jnp.int32, (8, 1024), 1)
    channel = lax.broadcasted_iota(jnp.int32, (8, 1024), 0)
    xi = lane & 31
    at_x = jnp.where(xi < 16, xi, jnp.where(xi < 22, xi - 22, xi - 6))
    at_y = (lane >> 5) - 8
    place = jnp.where(channel == 0, at_x, jnp.where(channel == 1, at_y, 0)).astype(f32)
    placed = geo[...] + place
    geo[...] = placed
    geo_cols[...] = placed.T
    for s in strips:
        start = GROUP * (2 * s + 1)
        geo_far[s] = geo[:, start : start + FAR]


def rows_of(s):
    near = pl.multiple_of(GROUP * (2 * s + 4), 64)
    start = pl.multiple_of(GROUP * (2 * s + 1), 32)
    return near, start


def dilatation(s, geo_cols, geo_far, high, low, shift):
    row = lax.broadcasted_iota(jnp.int32, (64, FAR), 0)
    lane = lax.broadcasted_iota(jnp.int32, (64, FAR), 1)
    home_row = row & 31
    near, start = rows_of(s)
    home = geo_cols[pl.ds(near, 64), :]
    middle, before, after = block_masks(s, home[0:32])
    vector, weight = bonds(geo_far[s], home)
    weight = weight * jnp.where(home_row < 16, middle, jnp.where(home_row < 22, before, after))
    far = pl.ds(pl.multiple_of(start - shift, 32), FAR)
    total = jnp.zeros((64, NCOL), f32)
    for j in range(3):
        matrix = weight * vector[j]
        matrix = jnp.where(lane == row + 96, -jnp.sum(matrix, axis=1, keepdims=True), matrix)
        total = total + product(matrix, high[j, far, :], low[j, far, :])
    return split(total * (home[:, 4:5] * (1.0 / 27.0)))


def own_bonds(s, geo_cols, geo_far):
    row = lax.broadcasted_iota(jnp.int32, (32, FAR), 0)
    lane = lax.broadcasted_iota(jnp.int32, (32, FAR), 1)
    at_self = lane == row + jnp.where(row < 16, 96, 112)
    near, _ = rows_of(s)
    first = geo_cols[pl.ds(near, 32), :]
    second = geo_cols[pl.ds(near + 32, 16), :]
    home = jnp.concatenate([first[0:16], second], axis=0)
    middle, _, _ = block_masks(s, first)
    vector, weight = bonds(geo_far[s], home)
    return home, vector, weight * middle, at_self


def bond_forces(s, tied, geo_far, high, low, shift):
    home, vector, weight, at_self = tied
    coupling = weight * ((home[:, 3:4] + geo_far[s, 3:4, :]) * (1.0 / 18.0))
    spring = home[:, 5:6]
    pairs = {}
    for i in range(3):
        side = coupling * vector[i]
        for j in range(i, 3):
            matrix = side * vector[j]
            total = jnp.sum(matrix, axis=1, keepdims=True)
            if i == j:
                total = total + spring
            pairs[i, j] = pairs[j, i] = jnp.where(at_self, total, -matrix)
    _, start = rows_of(s)
    far = pl.ds(pl.multiple_of(start - shift, 32), FAR)
    image = jnp.zeros((96, NCOL), f32)
    for j in range(3):
        stacked = jnp.concatenate([pairs[i, j] for i in range(3)], axis=0)
        image = image + product(stacked, high[j, far, :], low[j, far, :])
    return image


def dilatation_forces(s, tied, dil_high, dil_low):
    _, vector, weight, at_self = tied
    sides = []
    for i in range(3):
        matrix = weight * vector[i]
        total = jnp.sum(matrix, axis=1, keepdims=True)
        sides.append(-jnp.where(at_self, total, matrix))
    _, start = rows_of(s)
    far = pl.ds(start, FAR)
    return product(jnp.concatenate(sides, axis=0), dil_high[far, :], dil_low[far, :])


def inner(
    rows, left, right, own, high, low, dil_high, dil_low, forces,
    geo, geo_cols, geo_far, field,
):
    locate(own, None, None, geo, geo_cols, geo_far, range(4, 8))
    for c in range(3):
        for y in range(SIDE):
            j, t = divmod(y, 2)
            src = j * 18 + c * 6
            row = GROUP * y
            point = 256 * c + 16 * y
            field[c, row : row + 16, :] = rows[point : point + 16, :]
            field[c, row + 16 : row + 22, :] = left[src : src + 6, t * NCOL : (t + 1) * NCOL]
            field[c, row + 22 : row + 28, :] = right[src : src + 6, t * NCOL : (t + 1) * NCOL]
            field[c, row + 28 : row + 32, :] = jnp.zeros((4, NCOL), f32)
        for y in range(SIDE):
            row = GROUP * y
            parts = split(field[c, row : row + 32, :])
            high[c, row : row + 32, :] = parts[0]
            low[c, row : row + 32, :] = parts[1]

    def middle(s, carry):
        at = pl.ds(pl.multiple_of(64 * (s - 4), 64), 64)
        parts = dilatation(s, geo_cols, geo_far, high, low, 256)
        dil_high[at, :] = parts[0]
        dil_low[at, :] = parts[1]
        tied = own_bonds(s, geo_cols, geo_far)
        image = bond_forces(s, tied, geo_far, high, low, 256)
        at = pl.ds(pl.multiple_of(32 * (s - 4), 32), 32)
        for i in range(3):
            forces[i, at, :] = image[32 * i : 32 * i + 32]
        return carry

    lax.fori_loop(4, 8, middle, 0, unroll=2)


def stiffness(
    turned, mass, own, below, above, high_own, low_own, dil_high_own, dil_low_own, forces,
    result, grams,
    geo, geo_cols, geo_far, high, low, dil_high, dil_low,
):
    locate(own, below, above, geo, geo_cols, geo_far, range(STRIPS))
    for c in range(3):
        high[c, 256:768, :] = high_own[c]
        low[c, 256:768, :] = low_own[c]
        for j in range(HALO):
            for part, first in ((below, 2), (above, 24)):
                row = GROUP * (first + j)
                parts = split(part[RING * c : RING * c + GROUP, j * NCOL : (j + 1) * NCOL])
                high[c, row : row + 32, :] = parts[0]
                low[c, row : row + 32, :] = parts[1]
        for row in (0, 960):
            for ref in (high, low):
                ref[c, row : row + 64, :] = jnp.zeros((64, NCOL), bf16)
    dil_high[384:640, :] = dil_high_own[...]
    dil_low[384:640, :] = dil_low_own[...]

    def ends(i, carry):
        s = i + 4 * (i // 4)
        near, _ = rows_of(s)
        parts = dilatation(s, geo_cols, geo_far, high, low, 0)
        dil_high[pl.ds(near, 64), :] = parts[0]
        dil_low[pl.ds(near, 64), :] = parts[1]
        return carry

    lax.fori_loop(0, 8, ends, 0, unroll=4)

    def images(i, carry):
        tasks = []
        for s, whole in ((4 + i, False), (2 + i + 4 * (i // 2), True)):
            tied = own_bonds(s, geo_cols, geo_far)
            image = dilatation_forces(s, tied, dil_high, dil_low)
            if whole:
                image = image + bond_forces(s, tied, geo_far, high, low, 0)
            else:
                at = pl.ds(pl.multiple_of(32 * (s - 4), 32), 32)
                image = image + jnp.concatenate([forces[k, at, :] for k in range(3)], axis=0)
            tasks.append((s, image))
        for s, image in tasks:
            at = pl.multiple_of(32 * (s - 2), 32)
            for k in range(3):
                result[pl.ds(pl.multiple_of(at + 256 * k, 32), 32), :] = image[32 * k : 32 * k + 32]
        return carry

    lax.fori_loop(0, 4, images, 0, unroll=2)

    stiff = exact(turned[...], result[...])
    at_row = lax.broadcasted_iota(jnp.int32, (NCOL, NCOL), 0)
    at_col = lax.broadcasted_iota(jnp.int32, (NCOL, NCOL), 1)
    packed = jnp.where(at_row >= at_col, mass[...], stiff)
    diagonal = jnp.sum(jnp.where(at_row == at_col, stiff, 0.0), axis=0, keepdims=True)
    grams[0:192, :] = packed[:, 0:128]
    grams[192:288, 0:64] = packed[0:96, 128:192]
    grams[192:288, 64:128] = packed[96:192, 128:192]
    grams[288:320, :] = jnp.zeros((32, 128), f32)
    grams[288:289, :] = diagonal[:, 0:128]
    grams[289:290, 0:64] = diagonal[:, 128:192]


def lanes_of(tile, column):
    half = tile[column // 128 - 2 + len(tile)]
    at = column % 128
    return jnp.broadcast_to(half[:, at : at + 1], (8, 128))


def row_of(value, row):
    return jnp.broadcast_to(value[row : row + 1, :], (8, 128))


def reduce_block(ref, row0, col0, halves, out):
    at = lax.broadcasted_iota(jnp.int32, (8, 128), 0)
    tiles = []
    for q in range(8):
        row = row0 + 8 * q
        tiles.append([ref[row : row + 8, 128 * h : 128 * h + 128] for h in halves])
    pivots = [lanes_of(tiles[0], col0 + j) for j in range(8)]
    for t in range(8):
        first = col0 + 8 * t
        others = [q for q in range(8) if q != t]
        if out is not None:
            others = [q for q in others if q > t]
        columns = {q: [lanes_of(tiles[q], first + i) for i in range(8)] for q in others}
        ahead, following = [], []
        if t < 7:
            ahead = [lanes_of(tiles[t], first + 8 + j) for j in range(8)]
            following = [lanes_of(tiles[t + 1], first + 8 + j) for j in range(8)]
        panel = tiles[t]
        caught = list(panel)
        for i in range(8):
            pivot = row_of(pivots[i], i)
            inverse = 1.0 / pivot
            chosen = at == i
            factor = jnp.where(chosen, -1.0, pivots[i]) * inverse

            def step(value):
                return jnp.where(chosen, 0.0, value) - factor * row_of(value, i)

            if out is not None:
                root = lax.rsqrt(pivot)
                root = root * (1.5 - 0.5 * pivot * root * root)
                caught = [jnp.where(chosen, row_of(p, i) * root, c) for p, c in zip(panel, caught)]
            pivots = [step(p) if j > i else p for j, p in enumerate(pivots)]
            ahead = [step(p) for p in ahead]
            panel = [step(p) for p in panel]
        tiles[t] = panel
        if out is not None:
            out(t, caught)
        if t < 7:
            pivots = following
            for i in range(8):
                pivots = [
                    p - columns[t + 1][i] * row_of(a, i) for p, a in zip(pivots, ahead)
                ]
        for i in range(8):
            rows = [row_of(p, i) for p in panel]
            for q in others:
                tiles[q] = [v - columns[q][i] * r for v, r in zip(tiles[q], rows)]
    if out is None:
        for q in range(8):
            row = row0 + 8 * q
            for h, value in zip(halves, tiles[q]):
                ref[row : row + 8, 128 * h : 128 * h + 128] = value


def rotation(
    scale, grams, rows, images, modes, mode_images, reduced, square, work, small, factor, moved,
):
    square[...] = jnp.zeros((256, 256), f32)
    square[0:192, 0:128] = grams[0:192, :] * scale
    square[0:96, 128:192] = grams[192:288, 0:64] * scale
    square[96:192, 128:192] = grams[192:288, 64:128] * scale
    packed = square[0:192, 0:192]
    diagonal = jnp.concatenate([grams[288:289, :], grams[289:290, 0:64]], axis=1) * scale
    flipped = square[...].T[0:192, 0:192]
    at_row = lax.broadcasted_iota(jnp.int32, (NCOL, NCOL), 0)
    at_col = lax.broadcasted_iota(jnp.int32, (NCOL, NCOL), 1)
    mass = jnp.where(at_row >= at_col, packed, flipped)
    stiff = jnp.where(at_row < at_col, packed, jnp.where(at_row > at_col, flipped, diagonal))
    work[:, 0:192] = stiff
    work[:, 192:256] = mass[:, 0:64]
    for block in range(3):
        base = 64 * block
        halves = (1,) if block == 2 else (0, 1)
        lanes = slice(128 * halves[0], 256)
        reduce_block(work, base, base, halves, None)
        rest = [slice(64 * other, 64 * other + 64) for other in range(3) if other != block]
        change = exact(
            jnp.concatenate([work[part, base : base + 64] for part in rest], axis=0),
            work[base : base + 64, lanes],
        )
        work[rest[0], lanes] = work[rest[0], lanes] - change[0:64]
        work[rest[1], lanes] = work[rest[1], lanes] - change[64:128]
    solved = work[:, 192:256]
    weighted = exact(mass, solved)
    square[0:192, 0:64] = solved
    turned = square[...].T[0:64, 0:192]
    small[:, 0:64] = exact(turned, weighted)
    at_row = lax.broadcasted_iota(jnp.int32, (64, 64), 0)
    at_col = lax.broadcasted_iota(jnp.int32, (64, 64), 1)
    small[:, 64:128] = jnp.where(at_row == at_col, 1.0, 0.0)
    energy = exact(turned, exact(stiff, solved))
    for k, source in enumerate((rows, images)):
        value = source[...].reshape(24, 2, SIDE, NCOL)
        value = jnp.concatenate([value[:, h].reshape(384, NCOL) for h in range(2)], axis=0)
        value = product(value, *split(solved))
        parts = split(jnp.concatenate([value[0:384], value[384:768]], axis=1))
        moved[k, 0:384, :] = parts[0]
        moved[k, 384:768, :] = parts[1]
    upper = lax.broadcasted_iota(jnp.int32, (8, 128), 1) < 64

    def keep(t, caught):
        value = caught[0]
        factor[8 * t : 8 * t + 8, :] = jnp.where(upper, pltpu.roll(value, 64, 1), 0.0)
        factor[64 + 8 * t : 72 + 8 * t, :] = jnp.where(upper, 0.0, value)

    reduce_block(small, 0, 0, (0,), keep)
    high, low = split(factor[...])
    across = (((1,), (1,)), ((), ()))

    def dot(left, right):
        return lax.dot_general(left, right, across, preferred_element_type=f32)

    for k, out in enumerate((modes, mode_images)):
        both = dot(moved[k], high)
        total = both[0:384] + both[384:] + dot(moved[k, 0:384], low)
        for c in range(3):
            for y in range(SIDE // 2):
                row = 128 * c + 16 * y
                out[c, :, 128 * y : 128 * y + 128] = total[row : row + 16]
    inverse = factor[0:64, 0:64]
    reduced[...] = exact(exact(inverse, energy), inverse, True)


def exchange(up, down, axis):
    size = lax.axis_size(axis)
    forward = [(i, i + 1) for i in range(size - 1)]
    backward = [(i + 1, i) for i in range(size - 1)]
    return lax.ppermute(up, axis, forward), lax.ppermute(down, axis, backward)


def spread(value, axis):
    size = lax.axis_size(axis)
    return lax.all_to_all(jnp.broadcast_to(value[None], (size,) + value.shape), axis, 0, 0, tiled=True)


def local(basis, offsets, bond_modulus, bulk_modulus, springs, intact):
    slabs = lax.axis_size("slab")
    bands = lax.axis_size("band")
    total_rows = float(3 * SIDE * SIDE * slabs * bands)

    with jax.named_scope("halo"):
        up, down, geo = call(
            pack_x,
            [(152, 384)] * 2 + [(8, 256)],
            [pltpu.VMEM((128, 128), f32)] * 2,
            (basis, offsets, bond_modulus, bulk_modulus, springs, intact),
            1000,
            "pack_x",
            room=56,
        )
        left, right = exchange(up, down, "slab")
        rows, turned, mass = call(
            prepare,
            [(768, NCOL), ((3 * NCOL, 768), bf16), (NCOL, NCOL)],
            [pltpu.VMEM((768, 256), f32)],
            (hold(basis),),
            3 * 10**8,
            "prepare",
        )
        up, down, own = call(
            pack_y, [(88, 1152)] * 2 + [(8, 512)], [], (hold(basis), hold(geo), hold(left), hold(right)), 1000, "pack_y"
        )
        below, above = exchange(up, down, "band")

    with jax.named_scope("stiffness"):
        rows, turned, mass, left, right, own = [
            hold(a) for a in (rows, turned, mass, left, right, own)
        ]
        places = [
            pltpu.VMEM((8, 1024), f32),
            pltpu.VMEM((1024, 8), f32),
            pltpu.VMEM((STRIPS, 8, FAR), f32),
        ]
        middle = call(
            inner,
            [((3, 512, NCOL), bf16)] * 2 + [((256, NCOL), bf16)] * 2 + [((3, 128, NCOL), f32)],
            places + [pltpu.VMEM((3, 512, NCOL), f32)],
            (rows, left, right, own),
            10**9,
            "inner",
        )
        images, grams = call(
            stiffness,
            [(768, NCOL), (320, 128)],
            places
            + [pltpu.VMEM((3, 1024, NCOL), bf16)] * 2
            + [pltpu.VMEM((1024, NCOL), bf16)] * 2,
            (turned, mass, own, hold(below), hold(above), *[hold(a) for a in middle]),
            2 * 10**9,
            "stiffness",
        )

    with jax.named_scope("sums"):
        part = lax.all_to_all(grams.reshape(slabs, 1, 40960 // slabs), "slab", 0, 0, tiled=True)
        part = spread(jnp.sum(part, axis=0), "band")
        part = spread(jnp.sum(part, axis=0), "slab")
        grams = part.reshape(320, 128)

    with jax.named_scope("rotation"):
        def kernel(*refs):
            rotation(1.0 / total_rows, *refs)

        modes, mode_images, reduced = call(
            kernel,
            [(3, SIDE, SIDE * MODES)] * 2 + [(MODES, MODES)],
            [
                pltpu.VMEM((256, 256), f32),
                pltpu.VMEM((192, 256), f32),
                pltpu.VMEM((64, 128), f32),
                pltpu.VMEM((128, 128), f32),
                pltpu.VMEM((2, 768, 128), bf16),
            ],
            (hold(grams), hold(rows), hold(images)),
            10**9,
            "rotation",
            False,
        )
    return modes, mode_images, reduced


def solution(mesh):
    in_specs = (
        P(None, "slab", "band"),
        P(None, "slab", "band"),
        P("slab", "band"),
        P("slab", "band"),
        P("slab", "band"),
        P("slab", "band", None),
    )
    out_specs = (P(None, "slab", "band"), P(None, "slab", "band"), P())
    return jax.shard_map(local, mesh=mesh, in_specs=in_specs, out_specs=out_specs, check_vma=False)
```

```python
import jax
import jax.numpy as jnp
from jax import lax
from jax.experimental import pallas as pl
from jax.experimental.pallas import tpu as pltpu
from jax.sharding import PartitionSpec as P


MODES = 64
NCOL = 192
SIDE = 16
HALO = 6
GROUP = 32
RING = 28
STRIPS = 12
FAR = 256
f32 = jnp.float32
bf16 = jnp.bfloat16

VMEM = pl.BlockSpec(memory_space=pltpu.VMEM)


def hold(value):
    return pltpu.with_memory_space_constraint(value, pltpu.VMEM)


def call(kernel, outs, scratch, args, flops, name, near=True, room=24):
    outs = [(o, f32) if isinstance(o[0], int) else o for o in outs]
    size = sum(a.size for a in args)
    return pl.pallas_call(
        kernel,
        out_shape=[(pltpu.VMEM if near else jax.ShapeDtypeStruct)(*o) for o in outs],
        in_specs=[VMEM] * len(args),
        out_specs=[VMEM] * len(outs),
        scratch_shapes=scratch,
        compiler_params=pltpu.CompilerParams(vmem_limit_bytes=room * 1024 * 1024),
        cost_estimate=pl.CostEstimate(flops=flops, bytes_accessed=4 * size, transcendentals=0),
        name=name,
    )(*args)


def pack_x(basis, offsets, bond, bulk, springs, intact, up, down, geo, square, table):
    square[...] = jnp.zeros((128, 128), f32)
    for channel in range(3):
        square[16 * channel : 16 * channel + 16, 0:16] = offsets[channel]
    for channel, part in ((3, bond), (4, bulk), (5, springs)):
        square[16 * channel : 16 * channel + 16, 0:16] = part[...]
    table[...] = square[...].T
    for y in range(SIDE):
        for channel in range(6):
            at = 16 * channel
            geo[channel : channel + 1, 16 * y : 16 * y + 16] = table[y : y + 1, at : at + 16]
    lists = intact[...].astype(f32)
    gap = jnp.zeros((1, 4), f32)
    fill = jnp.zeros((1, 3), f32)
    for by in range(2):
        most = lists[0, by : by + 1, 0:6]
        rest = jnp.concatenate([lists[0, by : by + 1, 6:9], fill], axis=1)
        for row, part in ((6, rest), (7, most)):
            pattern = jnp.concatenate([part, gap, part], axis=1)
            pattern = jnp.concatenate([pattern, pattern], axis=1)
            pattern = jnp.concatenate([pattern, pattern], axis=1)
            pattern = jnp.concatenate([pattern, pattern], axis=1)
            geo[row : row + 1, 128 * by : 128 * by + 128] = pattern
    for out, first in ((up, SIDE - HALO), (down, 0)):
        for c in range(3):
            for j in range(8):
                row = j * 18 + c * 6
                out[row : row + 6, :] = basis[c, first : first + 6, j * 384 : (j + 1) * 384]
        out[144:152, 0:256] = geo[...]
        out[144:152, 256:384] = jnp.zeros((8, 128), f32)


def pack_y(basis, geo, left, right, up, down, own):
    own[...] = jnp.zeros((8, 512), f32)
    for y in range(SIDE):
        at = GROUP * y
        own[:, at : at + 16] = geo[:, 16 * y : 16 * y + 16]
        own[:, at + 16 : at + 22] = left[144:152, 16 * y + 10 : 16 * y + 16]
        own[:, at + 22 : at + 28] = right[144:152, 16 * y : 16 * y + 6]
    for out, first in ((up, SIDE - HALO), (down, 0)):
        for c in range(3):
            row = RING * c
            out[row : row + 16, :] = basis[c, :, first * NCOL : (first + HALO) * NCOL]
            for j in range(HALO // 2):
                src = (first // 2 + j) * 18 + c * 6
                lanes = slice(384 * j, 384 * j + 384)
                out[row + 16 : row + 22, lanes] = left[src : src + 6, :]
                out[row + 22 : row + 28, lanes] = right[src : src + 6, :]
        lanes = slice(first * GROUP, (first + HALO) * GROUP)
        out[84:88, :] = jnp.zeros((4, 1152), f32)
        out[84:88, 0:192] = own[0:4, lanes]
        out[84:88, 256:448] = own[4:8, lanes]


def split(value):
    high = value.astype(bf16)
    return high, (value - high.astype(f32)).astype(bf16)


def product(left, right_high, right_low):
    count = left.shape[0]
    parts = split(left)
    both = jnp.dot(jnp.concatenate(parts, axis=0), right_high, preferred_element_type=f32)
    rest = jnp.dot(parts[0], right_low, preferred_element_type=f32)
    return both[0:count] + both[count:] + rest


def split3(value):
    high, rest = split(value)
    middle, low = split(value - high.astype(f32))
    return high, middle, low


def exact(left, right, across=False):
    if left.dtype == f32:
        left = jnp.concatenate(split3(left), axis=0)
    count = left.shape[0] // 3
    dims = (((1,), (1 if across else 0,)), ((), ()))
    total = None
    for k, part in reversed(list(enumerate(split3(right)))):
        value = lax.dot_general(
            left[0 : (3 - k) * count], part, dims, preferred_element_type=f32
        )
        for m in reversed(range(3 - k)):
            piece = value[m * count : (m + 1) * count]
            total = piece if total is None else total + piece
    return total


def prepare(basis, rows, turned, mass, wide):
    wide[...] = jnp.zeros((768, 256), f32)
    for c in range(3):
        for y in range(SIDE):
            row = 256 * c + 16 * y
            value = basis[c, :, y * NCOL : (y + 1) * NCOL]
            rows[row : row + 16, :] = value
            wide[row : row + 16, 0:NCOL] = value
    parts = split3(wide[...].T[0:NCOL, :])
    for k in range(3):
        turned[k * NCOL : (k + 1) * NCOL, :] = parts[k]
    mass[...] = exact(turned[...], rows[...])


def block_masks(s, table):
    y0 = 2 * s - 4
    lane = lax.broadcasted_iota(jnp.int32, (32, FAR), 1)
    row = lax.broadcasted_iota(jnp.int32, (32, FAR), 0)
    xi = lane & 31
    far_x = jnp.where(xi < 16, 0, jnp.where(xi < 22, -1, 1))
    far_y = ((y0 - 3 + (lane >> 5)) >> 3) - (y0 >> 3)
    home_x = jnp.where(row < 16, 0, jnp.where(row < 22, -1, 1))
    entry = row - jnp.where(row < 16, 0, jnp.where(row < 22, 16, 22))
    entry = jnp.where(entry < 6, entry, -100)
    code = 3 * (far_x - home_x + 1) + far_y + 1
    value = jnp.where(code == entry, table[:, 7:8], 0.0)
    value = value + jnp.where(code == entry + 6, table[:, 6:7], 0.0)
    middle = jnp.sum(value[0:8], axis=0, keepdims=True)
    rest = value[16:32]
    at = lax.broadcasted_iota(jnp.int32, (16, FAR), 0)
    before = jnp.sum(jnp.where(at < 6, rest, 0.0), axis=0, keepdims=True)
    after = jnp.sum(jnp.where(at >= 6, rest, 0.0), axis=0, keepdims=True)
    return middle, before, after


def bonds(far, home):
    vector = [far[j : j + 1, :] - home[:, j : j + 1] for j in range(3)]
    square = vector[0] * vector[0] + vector[1] * vector[1] + vector[2] * vector[2]
    return vector, jnp.maximum(1.0 - square * (1.0 / 9.0), 0.0)


def locate(own, below, above, geo, geo_cols, geo_far, strips):
    geo[...] = jnp.zeros((8, 1024), f32)
    geo[:, 256:768] = own[...]
    for part, lane in ((below, 64), (above, 768)):
        if part is not None:
            geo[0:4, lane : lane + 192] = part[84:88, 0:192]
            geo[4:8, lane : lane + 192] = part[84:88, 256:448]
    lane = lax.broadcasted_iota(jnp.int32, (8, 1024), 1)
    channel = lax.broadcasted_iota(jnp.int32, (8, 1024), 0)
    xi = lane & 31
    at_x = jnp.where(xi < 16, xi, jnp.where(xi < 22, xi - 22, xi - 6))
    at_y = (lane >> 5) - 8
    place = jnp.where(channel == 0, at_x, jnp.where(channel == 1, at_y, 0)).astype(f32)
    placed = geo[...] + place
    geo[...] = placed
    geo_cols[...] = placed.T
    for s in strips:
        start = GROUP * (2 * s + 1)
        geo_far[s] = geo[:, start : start + FAR]


def rows_of(s):
    near = pl.multiple_of(GROUP * (2 * s + 4), 64)
    start = pl.multiple_of(GROUP * (2 * s + 1), 32)
    return near, start


def dilatation(s, geo_cols, geo_far, high, low, shift):
    row = lax.broadcasted_iota(jnp.int32, (64, FAR), 0)
    lane = lax.broadcasted_iota(jnp.int32, (64, FAR), 1)
    home_row = row & 31
    near, start = rows_of(s)
    home = geo_cols[pl.ds(near, 64), :]
    middle, before, after = block_masks(s, home[0:32])
    vector, weight = bonds(geo_far[s], home)
    weight = weight * jnp.where(home_row < 16, middle, jnp.where(home_row < 22, before, after))
    far = pl.ds(pl.multiple_of(start - shift, 32), FAR)
    total = jnp.zeros((64, NCOL), f32)
    for j in range(3):
        matrix = weight * vector[j]
        matrix = jnp.where(lane == row + 96, -jnp.sum(matrix, axis=1, keepdims=True), matrix)
        total = total + product(matrix, high[j, far, :], low[j, far, :])
    return split(total * (home[:, 4:5] * (1.0 / 27.0)))


def own_bonds(s, geo_cols, geo_far):
    row = lax.broadcasted_iota(jnp.int32, (32, FAR), 0)
    lane = lax.broadcasted_iota(jnp.int32, (32, FAR), 1)
    at_self = lane == row + jnp.where(row < 16, 96, 112)
    near, _ = rows_of(s)
    first = geo_cols[pl.ds(near, 32), :]
    second = geo_cols[pl.ds(near + 32, 16), :]
    home = jnp.concatenate([first[0:16], second], axis=0)
    middle, _, _ = block_masks(s, first)
    vector, weight = bonds(geo_far[s], home)
    return home, vector, weight * middle, at_self


def bond_forces(s, tied, geo_far, high, low, shift):
    home, vector, weight, at_self = tied
    coupling = weight * ((home[:, 3:4] + geo_far[s, 3:4, :]) * (1.0 / 18.0))
    spring = home[:, 5:6]
    pairs = {}
    for i in range(3):
        side = coupling * vector[i]
        for j in range(i, 3):
            matrix = side * vector[j]
            total = jnp.sum(matrix, axis=1, keepdims=True)
            if i == j:
                total = total + spring
            pairs[i, j] = pairs[j, i] = jnp.where(at_self, total, -matrix)
    _, start = rows_of(s)
    far = pl.ds(pl.multiple_of(start - shift, 32), FAR)
    image = jnp.zeros((96, NCOL), f32)
    for j in range(3):
        stacked = jnp.concatenate([pairs[i, j] for i in range(3)], axis=0)
        image = image + product(stacked, high[j, far, :], low[j, far, :])
    return image


def dilatation_forces(s, tied, dil_high, dil_low):
    _, vector, weight, at_self = tied
    sides = []
    for i in range(3):
        matrix = weight * vector[i]
        total = jnp.sum(matrix, axis=1, keepdims=True)
        sides.append(-jnp.where(at_self, total, matrix))
    _, start = rows_of(s)
    far = pl.ds(start, FAR)
    return product(jnp.concatenate(sides, axis=0), dil_high[far, :], dil_low[far, :])


def inner(
    rows, left, right, own, high, low, dil_high, dil_low, forces,
    geo, geo_cols, geo_far, field,
):
    locate(own, None, None, geo, geo_cols, geo_far, range(4, 8))
    for c in range(3):
        for y in range(SIDE):
            j, t = divmod(y, 2)
            src = j * 18 + c * 6
            row = GROUP * y
            point = 256 * c + 16 * y
            field[c, row : row + 16, :] = rows[point : point + 16, :]
            field[c, row + 16 : row + 22, :] = left[src : src + 6, t * NCOL : (t + 1) * NCOL]
            field[c, row + 22 : row + 28, :] = right[src : src + 6, t * NCOL : (t + 1) * NCOL]
            field[c, row + 28 : row + 32, :] = jnp.zeros((4, NCOL), f32)
        for y in range(SIDE):
            row = GROUP * y
            parts = split(field[c, row : row + 32, :])
            high[c, row : row + 32, :] = parts[0]
            low[c, row : row + 32, :] = parts[1]

    def middle(s, carry):
        at = pl.ds(pl.multiple_of(64 * (s - 4), 64), 64)
        parts = dilatation(s, geo_cols, geo_far, high, low, 256)
        dil_high[at, :] = parts[0]
        dil_low[at, :] = parts[1]
        tied = own_bonds(s, geo_cols, geo_far)
        image = bond_forces(s, tied, geo_far, high, low, 256)
        at = pl.ds(pl.multiple_of(32 * (s - 4), 32), 32)
        for i in range(3):
            forces[i, at, :] = image[32 * i : 32 * i + 32]
        return carry

    lax.fori_loop(4, 8, middle, 0, unroll=2)


def stiffness(
    turned, mass, own, below, above, high_own, low_own, dil_high_own, dil_low_own, forces,
    result, grams,
    geo, geo_cols, geo_far, high, low, dil_high, dil_low,
):
    locate(own, below, above, geo, geo_cols, geo_far, range(STRIPS))
    for c in range(3):
        high[c, 256:768, :] = high_own[c]
        low[c, 256:768, :] = low_own[c]
        for j in range(HALO):
            for part, first in ((below, 2), (above, 24)):
                row = GROUP * (first + j)
                parts = split(part[RING * c : RING * c + GROUP, j * NCOL : (j + 1) * NCOL])
                high[c, row : row + 32, :] = parts[0]
                low[c, row : row + 32, :] = parts[1]
        for row in (0, 960):
            for ref in (high, low):
                ref[c, row : row + 64, :] = jnp.zeros((64, NCOL), bf16)
    dil_high[384:640, :] = dil_high_own[...]
    dil_low[384:640, :] = dil_low_own[...]

    def ends(i, carry):
        s = i + 4 * (i // 4)
        near, _ = rows_of(s)
        parts = dilatation(s, geo_cols, geo_far, high, low, 0)
        dil_high[pl.ds(near, 64), :] = parts[0]
        dil_low[pl.ds(near, 64), :] = parts[1]
        return carry

    lax.fori_loop(0, 8, ends, 0, unroll=8)

    def images(i, carry):
        tasks = []
        for s, whole in ((4 + i, False), (2 + i + 4 * (i // 2), True)):
            tied = own_bonds(s, geo_cols, geo_far)
            image = dilatation_forces(s, tied, dil_high, dil_low)
            if whole:
                image = image + bond_forces(s, tied, geo_far, high, low, 0)
            else:
                at = pl.ds(pl.multiple_of(32 * (s - 4), 32), 32)
                image = image + jnp.concatenate([forces[k, at, :] for k in range(3)], axis=0)
            tasks.append((s, image))
        for s, image in tasks:
            at = pl.multiple_of(32 * (s - 2), 32)
            for k in range(3):
                result[pl.ds(pl.multiple_of(at + 256 * k, 32), 32), :] = image[32 * k : 32 * k + 32]
        return carry

    lax.fori_loop(0, 4, images, 0, unroll=4)

    stiff = exact(turned[...], result[...])
    at_row = lax.broadcasted_iota(jnp.int32, (NCOL, NCOL), 0)
    at_col = lax.broadcasted_iota(jnp.int32, (NCOL, NCOL), 1)
    packed = jnp.where(at_row >= at_col, mass[...], stiff)
    diagonal = jnp.sum(jnp.where(at_row == at_col, stiff, 0.0), axis=0, keepdims=True)
    grams[0:192, :] = packed[:, 0:128]
    grams[192:288, 0:64] = packed[0:96, 128:192]
    grams[192:288, 64:128] = packed[96:192, 128:192]
    grams[288:320, :] = jnp.zeros((32, 128), f32)
    grams[288:289, :] = diagonal[:, 0:128]
    grams[289:290, 0:64] = diagonal[:, 128:192]


def lanes_of(tile, column):
    half = tile[column // 128 - 2 + len(tile)]
    at = column % 128
    return jnp.broadcast_to(half[:, at : at + 1], (8, 128))


def row_of(value, row):
    return jnp.broadcast_to(value[row : row + 1, :], (8, 128))


def reduce_block(ref, row0, col0, halves, out):
    at = lax.broadcasted_iota(jnp.int32, (8, 128), 0)
    tiles = []
    for q in range(8):
        row = row0 + 8 * q
        tiles.append([ref[row : row + 8, 128 * h : 128 * h + 128] for h in halves])
    pivots = [lanes_of(tiles[0], col0 + j) for j in range(8)]
    for t in range(8):
        first = col0 + 8 * t
        others = [q for q in range(8) if q != t]
        if out is not None:
            others = [q for q in others if q > t]
        columns = {q: [lanes_of(tiles[q], first + i) for i in range(8)] for q in others}
        ahead, following = [], []
        if t < 7:
            ahead = [lanes_of(tiles[t], first + 8 + j) for j in range(8)]
            following = [lanes_of(tiles[t + 1], first + 8 + j) for j in range(8)]
        panel = tiles[t]
        caught = list(panel)
        for i in range(8):
            pivot = row_of(pivots[i], i)
            inverse = 1.0 / pivot
            chosen = at == i
            factor = jnp.where(chosen, -1.0, pivots[i]) * inverse

            def step(value):
                return jnp.where(chosen, 0.0, value) - factor * row_of(value, i)

            if out is not None:
                root = lax.rsqrt(pivot)
                root = root * (1.5 - 0.5 * pivot * root * root)
                caught = [jnp.where(chosen, row_of(p, i) * root, c) for p, c in zip(panel, caught)]
            pivots = [step(p) if j > i else p for j, p in enumerate(pivots)]
            ahead = [step(p) for p in ahead]
            panel = [step(p) for p in panel]
        tiles[t] = panel
        if out is not None:
            out(t, caught)
        if t < 7:
            pivots = following
            for i in range(8):
                pivots = [
                    p - columns[t + 1][i] * row_of(a, i) for p, a in zip(pivots, ahead)
                ]
        for i in range(8):
            rows = [row_of(p, i) for p in panel]
            for q in others:
                tiles[q] = [v - columns[q][i] * r for v, r in zip(tiles[q], rows)]
    if out is None:
        for q in range(8):
            row = row0 + 8 * q
            for h, value in zip(halves, tiles[q]):
                ref[row : row + 8, 128 * h : 128 * h + 128] = value


def rotation(
    scale, grams, rows, images, modes, mode_images, reduced, square, work, small, factor, moved,
):
    square[...] = jnp.zeros((256, 256), f32)
    square[0:192, 0:128] = grams[0:192, :] * scale
    square[0:96, 128:192] = grams[192:288, 0:64] * scale
    square[96:192, 128:192] = grams[192:288, 64:128] * scale
    packed = square[0:192, 0:192]
    diagonal = jnp.concatenate([grams[288:289, :], grams[289:290, 0:64]], axis=1) * scale
    flipped = square[...].T[0:192, 0:192]
    at_row = lax.broadcasted_iota(jnp.int32, (NCOL, NCOL), 0)
    at_col = lax.broadcasted_iota(jnp.int32, (NCOL, NCOL), 1)
    mass = jnp.where(at_row >= at_col, packed, flipped)
    stiff = jnp.where(at_row < at_col, packed, jnp.where(at_row > at_col, flipped, diagonal))
    work[:, 0:192] = stiff
    work[:, 192:256] = mass[:, 0:64]
    for block in range(3):
        base = 64 * block
        halves = (1,) if block == 2 else (0, 1)
        lanes = slice(128 * halves[0], 256)
        reduce_block(work, base, base, halves, None)
        rest = [slice(64 * other, 64 * other + 64) for other in range(3) if other != block]
        change = exact(
            jnp.concatenate([work[part, base : base + 64] for part in rest], axis=0),
            work[base : base + 64, lanes],
        )
        work[rest[0], lanes] = work[rest[0], lanes] - change[0:64]
        work[rest[1], lanes] = work[rest[1], lanes] - change[64:128]
    solved = work[:, 192:256]
    weighted = exact(mass, solved)
    square[0:192, 0:64] = solved
    turned = square[...].T[0:64, 0:192]
    small[:, 0:64] = exact(turned, weighted)
    at_row = lax.broadcasted_iota(jnp.int32, (64, 64), 0)
    at_col = lax.broadcasted_iota(jnp.int32, (64, 64), 1)
    small[:, 64:128] = jnp.where(at_row == at_col, 1.0, 0.0)
    energy = exact(turned, exact(stiff, solved))
    for k, source in enumerate((rows, images)):
        value = source[...].reshape(24, 2, SIDE, NCOL)
        value = jnp.concatenate([value[:, h].reshape(384, NCOL) for h in range(2)], axis=0)
        value = product(value, *split(solved))
        parts = split(jnp.concatenate([value[0:384], value[384:768]], axis=1))
        moved[k, 0:384, :] = parts[0]
        moved[k, 384:768, :] = parts[1]
    upper = lax.broadcasted_iota(jnp.int32, (8, 128), 1) < 64

    def keep(t, caught):
        value = caught[0]
        factor[8 * t : 8 * t + 8, :] = jnp.where(upper, pltpu.roll(value, 64, 1), 0.0)
        factor[64 + 8 * t : 72 + 8 * t, :] = jnp.where(upper, 0.0, value)

    reduce_block(small, 0, 0, (0,), keep)
    high, low = split(factor[...])
    across = (((1,), (1,)), ((), ()))

    def dot(left, right):
        return lax.dot_general(left, right, across, preferred_element_type=f32)

    for k, out in enumerate((modes, mode_images)):
        both = dot(moved[k], high)
        total = both[0:384] + both[384:] + dot(moved[k, 0:384], low)
        for c in range(3):
            for y in range(SIDE // 2):
                row = 128 * c + 16 * y
                out[c, :, 128 * y : 128 * y + 128] = total[row : row + 16]
    inverse = factor[0:64, 0:64]
    reduced[...] = exact(exact(inverse, energy), inverse, True)


def exchange(up, down, axis):
    size = lax.axis_size(axis)
    forward = [(i, i + 1) for i in range(size - 1)]
    backward = [(i + 1, i) for i in range(size - 1)]
    return lax.ppermute(up, axis, forward), lax.ppermute(down, axis, backward)


def spread(value, axis):
    size = lax.axis_size(axis)
    return lax.all_to_all(jnp.broadcast_to(value[None], (size,) + value.shape), axis, 0, 0, tiled=True)


def local(basis, offsets, bond_modulus, bulk_modulus, springs, intact):
    slabs = lax.axis_size("slab")
    bands = lax.axis_size("band")
    total_rows = float(3 * SIDE * SIDE * slabs * bands)

    with jax.named_scope("halo"):
        up, down, geo = call(
            pack_x,
            [(152, 384)] * 2 + [(8, 256)],
            [pltpu.VMEM((128, 128), f32)] * 2,
            (basis, offsets, bond_modulus, bulk_modulus, springs, intact),
            1000,
            "pack_x",
            room=56,
        )
        left, right = exchange(up, down, "slab")
        rows, turned, mass = call(
            prepare,
            [(768, NCOL), ((3 * NCOL, 768), bf16), (NCOL, NCOL)],
            [pltpu.VMEM((768, 256), f32)],
            (hold(basis),),
            3 * 10**8,
            "prepare",
        )
        up, down, own = call(
            pack_y, [(88, 1152)] * 2 + [(8, 512)], [], (hold(basis), hold(geo), hold(left), hold(right)), 1000, "pack_y"
        )
        below, above = exchange(up, down, "band")

    with jax.named_scope("stiffness"):
        rows, turned, mass, left, right, own = [
            hold(a) for a in (rows, turned, mass, left, right, own)
        ]
        places = [
            pltpu.VMEM((8, 1024), f32),
            pltpu.VMEM((1024, 8), f32),
            pltpu.VMEM((STRIPS, 8, FAR), f32),
        ]
        middle = call(
            inner,
            [((3, 512, NCOL), bf16)] * 2 + [((256, NCOL), bf16)] * 2 + [((3, 128, NCOL), f32)],
            places + [pltpu.VMEM((3, 512, NCOL), f32)],
            (rows, left, right, own),
            10**9,
            "inner",
        )
        images, grams = call(
            stiffness,
            [(768, NCOL), (320, 128)],
            places
            + [pltpu.VMEM((3, 1024, NCOL), bf16)] * 2
            + [pltpu.VMEM((1024, NCOL), bf16)] * 2,
            (turned, mass, own, hold(below), hold(above), *[hold(a) for a in middle]),
            2 * 10**9,
            "stiffness",
        )

    with jax.named_scope("sums"):
        part = lax.all_to_all(grams.reshape(slabs, 1, 40960 // slabs), "slab", 0, 0, tiled=True)
        part = spread(jnp.sum(part, axis=0), "band")
        part = spread(jnp.sum(part, axis=0), "slab")
        grams = part.reshape(320, 128)

    with jax.named_scope("rotation"):
        def kernel(*refs):
            rotation(1.0 / total_rows, *refs)

        modes, mode_images, reduced = call(
            kernel,
            [(3, SIDE, SIDE * MODES)] * 2 + [(MODES, MODES)],
            [
                pltpu.VMEM((256, 256), f32),
                pltpu.VMEM((192, 256), f32),
                pltpu.VMEM((64, 128), f32),
                pltpu.VMEM((128, 128), f32),
                pltpu.VMEM((2, 768, 128), bf16),
            ],
            (hold(grams), hold(rows), hold(images)),
            10**9,
            "rotation",
            False,
        )
    return modes, mode_images, reduced


def solution(mesh):
    in_specs = (
        P(None, "slab", "band"),
        P(None, "slab", "band"),
        P("slab", "band"),
        P("slab", "band"),
        P("slab", "band"),
        P("slab", "band", None),
    )
    out_specs = (P(None, "slab", "band"), P(None, "slab", "band"), P())
    return jax.shard_map(local, mesh=mesh, in_specs=in_specs, out_specs=out_specs, check_vma=False)
```
